256 devices in a mesh: leaf: 256 (over z, x, y, core).
Axes of the slice: x: 4, y: 4, z: 8, core: 2. Of those that a mesh axis runs over, the one named last changes fastest.
Arguments:
- coords: float32 [3, 131072], P(None, 'leaf'), may hold values from 0 to 2
- latent: float32 [131072], P('leaf'), may hold values from -3 to 3
- labels: int32 [131072], P('leaf'), may hold values from 0 to 1
- site_order: int32 [256, 512], P('leaf'), may hold values from 0 to 511, each once within a row
- level_bases: bfloat16 [4, 256, 131072], P(None, None, 'leaf'), may hold values from -0.75 to 0.75
Outputs:
- solution: float32 [131072], P('leaf')
The draws below stay inside these ranges and needn't reach their ends.
Inputs may be any that keep to these rules, and one draw needn't show every extreme that they name: Each row of site_order is a permutation of 0 to 511.
All inputs are finite; a program needn't handle non-finite values.
Results may differ from the reference program's by a relative error of at most 0.0003.
Values sent between devices are 32-bit elements; how exact they have to be, the bound alone decides.
A program may use at most 64 MiB of HBM per device.

```python
import math
import jax
import jax.numpy as jnp
from jax import lax

M = 512
R = 256
LEVELS = 4
LEAVES = 256
SITES = 131072


def with_ends(drawn, stream_key, low, top_value):
    dims = drawn.shape
    spot = [jax.random.randint(jax.random.fold_in(stream_key, axis), (), 0, dims[axis]) for axis in range(len(dims))]
    drawn = drawn.at[tuple(spot)].set(low)
    longest = dims.index(max(dims))
    spot[longest] = (spot[longest] + 1) % dims[longest]
    return drawn.at[tuple(spot)].set(top_value)


def block_scale(own_key, extent, cuts, smallest, high):
    def one(axis_at, shards_of):
        steps = jax.random.uniform(jax.random.fold_in(jax.random.fold_in(own_key, 6), axis_at), (shards_of,), jnp.float32, smallest / len(cuts), high / len(cuts))
        return jnp.repeat(jnp.exp(steps), extent[axis_at] // shards_of).reshape((-1,) + (1,) * (len(extent) - axis_at - 1))

    gain = one(*cuts[0])
    for cut in cuts[1:]:
        gain = gain * one(*cut)
    return gain


def centred(rng, shape, deviation, most, pieces=(), kind=jnp.bfloat16):
    array = jax.random.normal(rng, shape, jnp.float32) * deviation
    if len(pieces) > 0:
        array = block_scale(rng, shape, pieces, -0.22, 0.18) * array
    return jnp.clip(array, min=-most, max=most).astype(kind)


def setup_inputs(seed: int = 0) -> dict:
    splits = jax.random.split(jax.random.key(seed), 6)
    coords = jnp.clip(2.0 * jax.random.uniform(splits[0], (3, SITES), jnp.float32) ** block_scale(splits[0], (3, SITES), ((1, 256),), -0.2, 0.2), 0.0, 2.0)
    latent = centred(splits[1], (SITES,), 1.0, 3.0, ((0, 256),), jnp.float32)
    labels = with_ends(jax.random.randint(splits[2], (SITES,), 0, 2), jax.random.fold_in(splits[2], 1), 0, 1).astype(jnp.int32)
    site_order = jax.vmap(lambda own: jax.random.permutation(own, M))(jax.random.split(splits[3], LEAVES)).reshape((LEAVES, M)).astype(jnp.int32)
    level_bases = centred(splits[4], (LEVELS, R, SITES), (R // 4) ** -0.5, 0.75, ((2, 256),))
    return {"coords": coords, "latent": latent, "labels": labels, "site_order": site_order, "level_bases": level_bases}


length_scale = 0.25
signal_variance = 16.0
root_five = math.sqrt(5.0)
highest = lax.Precision.HIGHEST

def leaf_solve(coords, latent, labels, site_order, level_bases):
    tree_latent = jnp.take(latent, site_order)
    tree_target = jnp.take(labels, site_order).astype(jnp.float32)
    probability = jax.nn.sigmoid(tree_latent)
    weight = probability * (1.0 - probability)
    root_weight = jnp.sqrt(weight)
    right_side = root_weight * (weight * tree_latent + tree_target - probability)
    differences = coords[:, :, None] - coords[:, None, :]
    distance = jnp.sqrt(lax.optimization_barrier(jnp.sum(differences * differences, axis=0)))
    scaled = root_five * distance / length_scale
    kernel = signal_variance * (1.0 + scaled + scaled * scaled / 3.0) * jnp.exp(-scaled)
    site_count = tree_latent.shape[0]
    leaf_matrix = jnp.eye(site_count, dtype=jnp.float32) + root_weight[:, None] * kernel * root_weight[None, :]
    factor = jnp.linalg.cholesky(leaf_matrix)
    scaled_bases = level_bases.astype(jnp.float32) * root_weight[None, None, :]
    stacked = jnp.concatenate([scaled_bases.reshape(-1, site_count).T, right_side[:, None]], axis=1)
    solved = jax.scipy.linalg.cho_solve((factor, True), stacked)
    applied = solved[:, :-1].T.reshape(scaled_bases.shape)
    return (scaled_bases, applied, solved[:, -1])

def node_terms(level_basis, applied, vector):
    gram_terms = jnp.einsum('rm,jsm->jrs', level_basis, applied, precision=highest)
    projection = jnp.dot(level_basis, vector, precision=highest)
    return (gram_terms, projection)

def core_solve(gram_terms, projection):
    rank_size = gram_terms.shape[1]
    remaining = gram_terms.shape[0] - 1
    core_matrix = jnp.eye(rank_size, dtype=jnp.float32) + gram_terms[0]
    core_factor = jnp.linalg.cholesky(core_matrix)
    right_hand = jnp.concatenate([jnp.transpose(gram_terms[1:], (1, 0, 2)).reshape(rank_size, remaining * rank_size), projection[:, None]], axis=1)
    solution = jax.scipy.linalg.cho_solve((core_factor, True), right_hand)
    coefficients = jnp.transpose(solution[:, :remaining * rank_size].reshape(rank_size, remaining, rank_size), (1, 0, 2))
    return (coefficients, solution[:, -1])

def apply_update(applied, vector, coefficients, coeff_vector):
    current_cols = applied[0]
    remaining_cols = applied[1:] - jnp.einsum('jrs,rm->jsm', coefficients, current_cols, precision=highest)
    vector = vector - jnp.dot(coeff_vector, current_cols, precision=highest)
    return (remaining_cols, vector)

def reference(coords, latent, labels, site_order, level_bases):
    leaf_count = site_order.shape[0]
    leaf_rows = site_order.shape[1]
    leaf_coords = jnp.transpose(coords.reshape(3, leaf_count, leaf_rows), (1, 0, 2))
    leaf_latent = latent.reshape(leaf_count, leaf_rows)
    leaf_labels = labels.reshape(leaf_count, leaf_rows)
    leaf_bases = jnp.transpose(level_bases.reshape(LEVELS, R, leaf_count, leaf_rows), (2, 0, 1, 3))

    def one_leaf(packed):
        return leaf_solve(packed[0], packed[1], packed[2], packed[3], packed[4])
    scaled_bases, applied, vector = lax.map(one_leaf, (leaf_coords, leaf_latent, leaf_labels, site_order, leaf_bases))
    for level_idx in range(LEVELS):
        group_size = leaf_count // 2 ** (LEVELS - 1 - level_idx)
        gram_terms, projection = jax.vmap(node_terms)(scaled_bases[:, level_idx], applied, vector)
        node_count = leaf_count // group_size
        gram_terms = lax.optimization_barrier(jnp.sum(gram_terms.reshape((node_count, group_size) + gram_terms.shape[1:]), axis=1))
        projection = lax.optimization_barrier(jnp.sum(projection.reshape(node_count, group_size, R), axis=1))
        coefficients, coeff_vector = jax.vmap(core_solve)(gram_terms, projection)
        coefficients = jnp.repeat(coefficients, group_size, axis=0)
        coeff_vector = jnp.repeat(coeff_vector, group_size, axis=0)
        applied, vector = jax.vmap(apply_update)(applied, vector, coefficients, coeff_vector)
    return vector.reshape(-1)
```

```python
import functools
import math

import jax
import jax.numpy as jnp
from jax import lax
from jax.experimental import pallas as pl
from jax.experimental.pallas import tpu as pltpu
from jax.sharding import PartitionSpec as P

F32 = jnp.float32
BF16 = jnp.bfloat16
HIGHEST = lax.Precision.HIGHEST
LENGTH_SCALE = 0.25
VARIANCE = 16.0
ROOT_FIVE = math.sqrt(5.0)
M = 512
R = 256
LEVELS = 4
LANES = 128
PLANE = 32
NN = (((1,), (0,)), ((), ()))
NT = (((1,), (1,)), ((), ()))


def dot(a, b, dims=NN):
    return lax.dot_general(a, b, dims, preferred_element_type=F32)


def dot_f32(a, b, dims=NN):
    return lax.dot_general(a, b, dims, precision=HIGHEST, preferred_element_type=F32)


def split(x):
    hi = x.astype(BF16)
    return hi, (x - hi.astype(F32)).astype(BF16)


def split3(x):
    hi = x.astype(BF16)
    rest = x - hi.astype(F32)
    mid = rest.astype(BF16)
    return hi, mid, (rest - mid.astype(F32)).astype(BF16)


def dot3(a, b, dims=NN):
    return dot(a[0], b[0], dims) + (dot(a[0], b[1], dims) + dot(a[1], b[0], dims))


def eye(n):
    return jnp.where(
        lax.broadcasted_iota(jnp.int32, (n, n), 0) == lax.broadcasted_iota(jnp.int32, (n, n), 1), 1.0, 0.0
    ).astype(F32)


def newton_inverse(s, z_ref):
    n = s.shape[0]
    bound = jnp.max(jnp.sum(jnp.abs(s), axis=0, keepdims=True))
    alpha = 2.0 / (1.0 + bound)
    gap = (bound - 1.0) / (bound + 1.0)
    scale = 2.0 / (2.0 - gap * gap)
    z_ref[...] = (alpha * scale) * (2.0 * eye(n) - alpha * s)
    gap = gap * gap / (2.0 - gap * gap)
    parts = split(s)

    def body(gap):
        z = z_ref[...]
        zs = split(z)
        residual = eye(n) - dot3(parts, zs)
        scale = 2.0 / (2.0 - gap * gap)
        z_ref[...] = scale * (z + dot3(zs, split(residual)))
        return gap * gap / (2.0 - gap * gap)

    lax.while_loop(lambda gap: gap > 2e-3, body, gap)
    z = z_ref[...]
    residual = eye(n) - dot_f32(s, z)
    return z + dot3(split(z), split(residual))


def leaf_kernel(coord_ref, latent_ref, label_ref, order_ref, basis_ref, front_ref, inverse_ref, rows_ref,
                a_ref, z_ref, mh_ref, ml_ref):
    picked = lax.broadcasted_iota(jnp.int32, (M, M), 0) == order_ref[...]
    one_hot = jnp.where(picked, 1.0, 0.0).astype(BF16)
    hi, mid, lo = split3(latent_ref[...])
    row = lax.broadcasted_iota(jnp.int32, (16, M), 0)
    packed = jnp.where(row == 0, hi.astype(F32), 0.0)
    packed = jnp.where(row == 1, mid.astype(F32), packed)
    packed = jnp.where(row == 2, lo.astype(F32), packed)
    packed = jnp.where(row == 3, label_ref[...].astype(F32), packed)
    got = dot(packed.astype(BF16), one_hot)
    tree_latent = (got[0:1] + got[1:2]) + got[2:3]
    tree_target = got[3:4]
    probability = 1.0 / (1.0 + jnp.exp(-tree_latent))
    weight = probability * (1.0 - probability)
    root_weight = jnp.sqrt(weight)
    right_side = root_weight * (weight * tree_latent + tree_target - probability)

    def column(value, i):
        return jnp.broadcast_to(value[:, i * LANES:(i + 1) * LANES], (LANES, LANES)).T

    axes = [coord_ref[k:k + 1, :] for k in range(3)]
    columns = []
    for i in range(4):
        cols = [column(axis, i) for axis in axes]
        weight_col = column(root_weight, i)
        columns.append(weight_col)
        for j in range(i, 4):
            span = slice(j * LANES, (j + 1) * LANES)
            total = None
            for axis, col in zip(axes, cols):
                difference = col - axis[:, span]
                total = difference * difference if total is None else total + difference * difference
            scaled = (ROOT_FIVE / LENGTH_SCALE) * jnp.sqrt(total)
            kernel = VARIANCE * (1.0 + scaled + scaled * scaled / 3.0) * jnp.exp(-scaled)
            block = weight_col * kernel * root_weight[:, span]
            if i == j:
                block = block + eye(LANES)
            a_ref[i * LANES:(i + 1) * LANES, span] = block
            if i != j:
                a_ref[span, i * LANES:(i + 1) * LANES] = block.T

    top, bottom = slice(0, R), slice(R, M)
    x = newton_inverse(a_ref[top, top], z_ref)
    u = dot_f32(x, a_ref[top, bottom])
    v = dot_f32(a_ref[bottom, top], x)
    schur = newton_inverse(a_ref[bottom, bottom] - dot_f32(v, a_ref[top, bottom]), z_ref)
    us = dot_f32(u, schur)
    inverse_ref[bottom, bottom] = schur
    inverse_ref[top, bottom] = -us
    inverse_ref[bottom, top] = -dot_f32(schur, v)
    inverse_ref[top, top] = x + dot_f32(us, v)

    for i in range(4):
        for j in range(4):
            rows, span = slice(i * LANES, (i + 1) * LANES), slice(j * LANES, (j + 1) * LANES)
            hi, lo = split(columns[i] * inverse_ref[rows, span] * root_weight[:, span])
            mh_ref[rows, span] = hi
            ml_ref[rows, span] = lo
    solved = dot_f32(jnp.broadcast_to(right_side, (8, M)), inverse_ref[...])[0:1]
    weighted = split3(root_weight * solved)
    lane = lax.broadcasted_iota(jnp.int32, (LANES, M), 0)
    tile = jnp.zeros((R, LANES), F32)
    offset = 0
    for level in range(LEVELS):
        basis = basis_ref[level]
        part = split(dot(basis, mh_ref[...]) + dot(basis, ml_ref[...]))
        for other in range(level, LEVELS):
            front_ref[:, offset:offset + R] = dot(part[0], basis_ref[other], NT) + dot(part[1], basis_ref[other], NT)
            offset += R
        if level == 0:
            offset += LANES
        for piece in weighted:
            placed = jnp.where(lane == level, piece.astype(F32), 0.0).astype(BF16)
            tile = tile + dot(basis, placed, NT)
    front_ref[:, LEVELS * R:LEVELS * R + LANES] = tile
    row = lax.broadcasted_iota(jnp.int32, (8, M), 0)
    rows_ref[...] = jnp.where(row == 0, root_weight, right_side)


def vmem(n):
    return [pl.BlockSpec(memory_space=pltpu.VMEM)] * n


FRONT = LEVELS * R + LANES + 6 * R
PARAMS = pltpu.CompilerParams(vmem_limit_bytes=60 * 1024 * 1024)


def leaf_call(coords, latent, labels, order, bases):
    return pl.pallas_call(
        leaf_kernel,
        out_shape=(
            jax.ShapeDtypeStruct((R, FRONT), F32),
            jax.ShapeDtypeStruct((M, M), F32),
            jax.ShapeDtypeStruct((8, M), F32),
        ),
        in_specs=vmem(5),
        out_specs=tuple(vmem(3)),
        scratch_shapes=[
            pltpu.VMEM((M, M), F32), pltpu.VMEM((R, R), F32), pltpu.VMEM((M, M), BF16), pltpu.VMEM((M, M), BF16)
        ],
        compiler_params=PARAMS,
        name="leaf",
    )(coords, latent, labels, order, bases)


def eliminate(left, gathered_ref, z_ref):
    inverse = newton_inverse(gathered_ref[:, 0:R] + eye(R), z_ref)
    return dot3(split(inverse), split(gathered_ref[:, R:left * R + LANES]))


def level_kernel(left, gathered_ref, own_ref, next_ref, h_ref, z_ref):
    h = eliminate(left, gathered_ref, z_ref)
    h_ref[...] = h
    width = (left - 1) * R
    h_parts = split(h)
    mine = lax.rem(lax.axis_index("leaf"), PLANE) * 8
    wanted = lax.broadcasted_iota(jnp.int32, (8, R), 1) == lax.broadcasted_iota(jnp.int32, (8, R), 0) + mine
    one_hot = jnp.where(wanted, 1.0, 0.0).astype(BF16)
    lane = lax.broadcasted_iota(jnp.int32, (8, LANES), 1)
    tile = own_ref[:, left * R:left * R + LANES]
    source, target = left * R + LANES, 0
    for k in range(1, left):
        block = split3(gathered_ref[:, k * R:(k + 1) * R])
        rows = dot(one_hot, block[0], NT) + dot(one_hot, block[1], NT) + dot(one_hot, block[2], NT)
        drop = dot3(split(rows), h_parts)
        span = (left - k) * R
        next_ref[:, target:target + span] = own_ref[:, source:source + span] - drop[:, (k - 1) * R:width]
        source, target = source + span, target + span
        if k == 1:
            target += LANES
        at = LEVELS - left
        tile = tile - jnp.where(lane == at + k, drop[:, width + at:width + at + 1], 0.0)
    next_ref[:, width:width + LANES] = tile


def own_width(left):
    return LANES + R * (left * (left + 1) // 2)


def level_call(left, gathered, own):
    return pl.pallas_call(
        functools.partial(level_kernel, left),
        out_shape=(
            jax.ShapeDtypeStruct((8, own_width(left - 1)), F32),
            jax.ShapeDtypeStruct((R, (left - 1) * R + LANES), F32),
        ),
        in_specs=vmem(2),
        out_specs=tuple(vmem(2)),
        scratch_shapes=[pltpu.VMEM((R, R), F32)],
        compiler_params=PARAMS,
        name=f"level{LEVELS - left + 1}",
    )(gathered, own)


def last_kernel(gathered_ref, h1_ref, h2_ref, h3_ref, inverse_ref, rows_ref, basis_ref, out_ref, z_ref):
    h4 = eliminate(1, gathered_ref, z_ref)
    total = jnp.zeros((16, M), F32)
    later = []
    for level in reversed(range(LEVELS)):
        rest = LEVELS - 1 - level
        h_ref = (h1_ref, h2_ref, h3_ref, None)[level]
        tile = h4 if h_ref is None else h_ref[:, rest * R:rest * R + LANES]
        z = jnp.broadcast_to(tile.T[level:level + 1, :], (8, R))
        for k, done in enumerate(later):
            z = z - dot_f32(done, h_ref[:, k * R:(k + 1) * R], NT)
        later.insert(0, z)
        hi, mid, lo = split3(z[0:1])
        row = lax.broadcasted_iota(jnp.int32, (16, R), 0)
        packed = jnp.where(row == 0, hi.astype(F32), jnp.where(row == 1, mid.astype(F32), jnp.where(row == 2, lo.astype(F32), 0.0)))
        total = total + dot(packed.astype(BF16), basis_ref[level])
    spread = (total[0:1] + total[1:2]) + total[2:3]
    right = rows_ref[1:2] - rows_ref[0:1] * spread
    out_ref[...] = dot_f32(jnp.broadcast_to(right, (8, M)), inverse_ref[...])


def last_call(gathered, h1, h2, h3, inverse, rows, bases):
    return pl.pallas_call(
        last_kernel,
        out_shape=jax.ShapeDtypeStruct((8, M), F32),
        in_specs=vmem(7),
        out_specs=vmem(1)[0],
        scratch_shapes=[pltpu.VMEM((R, R), F32)],
        compiler_params=PARAMS,
        name="last",
    )(gathered, h1, h2, h3, inverse, rows, bases)


def planes(count):
    return [[p * PLANE + d for d in range(PLANE)] for p in range(count)]


def local(coords, latent, labels, site_order, level_bases):
    count = lax.axis_size("leaf")
    groups = planes(count // PLANE)
    front, inverse, rows = leaf_call(
        coords, latent.reshape(1, M), labels.reshape(1, M), site_order, level_bases
    )
    own = lax.psum_scatter(front, "leaf", axis_index_groups=groups, scatter_dimension=0, tiled=True)
    h = []
    for level in range(LEVELS):
        left = LEVELS - level
        if level > 0:
            bit = PLANE << (level - 1)
            own = own + lax.ppermute(own, "leaf", [(d, d ^ bit) for d in range(count)])
        gathered = lax.all_gather(
            own[:, :left * R + LANES], "leaf", axis_index_groups=groups, axis=0, tiled=True
        )
        if left > 1:
            own, part = level_call(left, gathered, own)
            h.append(part)
    return last_call(gathered, *h, inverse, rows, level_bases)[0]


def solution(mesh):
    placed = (P(None, "leaf"), P("leaf"), P("leaf"), P("leaf", None), P(None, None, "leaf"))
    return jax.shard_map(local, mesh=mesh, in_specs=placed, out_specs=P("leaf"), check_vma=False)
```

```python
import functools
import math

import jax
import jax.numpy as jnp
from jax import lax
from jax.experimental import pallas as pl
from jax.experimental.pallas import tpu as pltpu
from jax.sharding import PartitionSpec as P

F32 = jnp.float32
BF16 = jnp.bfloat16
HIGHEST = lax.Precision.HIGHEST
LENGTH_SCALE = 0.25
VARIANCE = 16.0
ROOT_FIVE = math.sqrt(5.0)
M = 512
R = 256
LEVELS = 4
LANES = 128
PLANE = 32
NN = (((1,), (0,)), ((), ()))
NT = (((1,), (1,)), ((), ()))


def dot(a, b, dims=NN):
    return lax.dot_general(a, b, dims, preferred_element_type=F32)


def dot_f32(a, b, dims=NN):
    return lax.dot_general(a, b, dims, precision=HIGHEST, preferred_element_type=F32)


def split(x):
    hi = x.astype(BF16)
    return hi, (x - hi.astype(F32)).astype(BF16)


def split3(x):
    hi = x.astype(BF16)
    rest = x - hi.astype(F32)
    mid = rest.astype(BF16)
    return hi, mid, (rest - mid.astype(F32)).astype(BF16)


def dot3(a, b, dims=NN):
    return dot(a[0], b[0], dims) + (dot(a[0], b[1], dims) + dot(a[1], b[0], dims))


def eye(n):
    return jnp.where(
        lax.broadcasted_iota(jnp.int32, (n, n), 0) == lax.broadcasted_iota(jnp.int32, (n, n), 1), 1.0, 0.0
    ).astype(F32)


def newton_inverse(s, z_ref):
    n = s.shape[0]
    bound = jnp.max(jnp.sum(jnp.abs(s), axis=0, keepdims=True))
    alpha = 2.0 / (1.0 + bound)
    gap = (bound - 1.0) / (bound + 1.0)
    scale = 2.0 / (2.0 - gap * gap)
    z_ref[...] = (alpha * scale) * (2.0 * eye(n) - alpha * s)
    gap = gap * gap / (2.0 - gap * gap)
    parts = split(s)

    def body(gap):
        z = z_ref[...]
        zs = split(z)
        residual = eye(n) - dot3(parts, zs)
        scale = 2.0 / (2.0 - gap * gap)
        z_ref[...] = scale * (z + dot3(zs, split(residual)))
        return gap * gap / (2.0 - gap * gap)

    lax.while_loop(lambda gap: gap > 2e-3, body, gap)
    z = z_ref[...]
    residual = eye(n) - dot_f32(s, z)
    return z + dot3(split(z), split(residual))


def leaf_kernel(coord_ref, latent_ref, label_ref, order_ref, basis_ref, front_ref, inverse_ref, rows_ref,
                a_ref, z_ref, mh_ref, ml_ref):
    picked = lax.broadcasted_iota(jnp.int32, (M, M), 0) == order_ref[...]
    one_hot = jnp.where(picked, 1.0, 0.0).astype(BF16)
    hi, mid, lo = split3(latent_ref[...])
    row = lax.broadcasted_iota(jnp.int32, (16, M), 0)
    packed = jnp.where(row == 0, hi.astype(F32), 0.0)
    packed = jnp.where(row == 1, mid.astype(F32), packed)
    packed = jnp.where(row == 2, lo.astype(F32), packed)
    packed = jnp.where(row == 3, label_ref[...].astype(F32), packed)
    got = dot(packed.astype(BF16), one_hot)
    tree_latent = (got[0:1] + got[1:2]) + got[2:3]
    tree_target = got[3:4]
    probability = 1.0 / (1.0 + jnp.exp(-tree_latent))
    weight = probability * (1.0 - probability)
    root_weight = jnp.sqrt(weight)
    right_side = root_weight * (weight * tree_latent + tree_target - probability)

    def column(value, i):
        return jnp.broadcast_to(value[:, i * LANES:(i + 1) * LANES], (LANES, LANES)).T

    axes = [coord_ref[k:k + 1, :] for k in range(3)]
    columns = []
    for i in range(4):
        cols = [column(axis, i) for axis in axes]
        weight_col = column(root_weight, i)
        columns.append(weight_col)
        for j in range(i, 4):
            span = slice(j * LANES, (j + 1) * LANES)
            total = None
            for axis, col in zip(axes, cols):
                difference = col - axis[:, span]
                total = difference * difference if total is None else total + difference * difference
            scaled = (ROOT_FIVE / LENGTH_SCALE) * jnp.sqrt(total)
            kernel = VARIANCE * (1.0 + scaled + scaled * scaled / 3.0) * jnp.exp(-scaled)
            block = weight_col * kernel * root_weight[:, span]
            if i == j:
                block = block + eye(LANES)
            a_ref[i * LANES:(i + 1) * LANES, span] = block
            if i != j:
                a_ref[span, i * LANES:(i + 1) * LANES] = block.T

    top, bottom = slice(0, R), slice(R, M)
    x = newton_inverse(a_ref[top, top], z_ref)
    u = dot_f32(x, a_ref[top, bottom])
    v = dot_f32(a_ref[bottom, top], x)
    schur = newton_inverse(a_ref[bottom, bottom] - dot_f32(v, a_ref[top, bottom]), z_ref)
    us = dot_f32(u, schur)
    inverse_ref[bottom, bottom] = schur
    inverse_ref[top, bottom] = -us
    inverse_ref[bottom, top] = -dot_f32(schur, v)
    inverse_ref[top, top] = x + dot_f32(us, v)

    for i in range(4):
        for j in range(4):
            rows, span = slice(i * LANES, (i + 1) * LANES), slice(j * LANES, (j + 1) * LANES)
            hi, lo = split(columns[i] * inverse_ref[rows, span] * root_weight[:, span])
            mh_ref[rows, span] = hi
            ml_ref[rows, span] = lo
    solved = dot_f32(jnp.broadcast_to(right_side, (8, M)), inverse_ref[...])[0:1]
    weighted = split3(root_weight * solved)
    lane = lax.broadcasted_iota(jnp.int32, (LANES, M), 0)
    tile = jnp.zeros((R, LANES), F32)
    offset = 0
    for level in range(LEVELS):
        basis = basis_ref[level]
        part = split(dot(basis, mh_ref[...]) + dot(basis, ml_ref[...]))
        for other in range(level, LEVELS):
            front_ref[:, offset:offset + R] = dot(part[0], basis_ref[other], NT) + dot(part[1], basis_ref[other], NT)
            offset += R
        if level == 0:
            offset += LANES
        for piece in weighted:
            placed = jnp.where(lane == level, piece.astype(F32), 0.0).astype(BF16)
            tile = tile + dot(basis, placed, NT)
    front_ref[:, LEVELS * R:LEVELS * R + LANES] = tile
    row = lax.broadcasted_iota(jnp.int32, (8, M), 0)
    rows_ref[...] = jnp.where(row == 0, root_weight, right_side)


def vmem(n):
    return [pl.BlockSpec(memory_space=pltpu.VMEM)] * n


FRONT = LEVELS * R + LANES + 6 * R
PARAMS = pltpu.CompilerParams(vmem_limit_bytes=60 * 1024 * 1024)


def leaf_call(coords, latent, labels, order, bases):
    return pl.pallas_call(
        leaf_kernel,
        out_shape=(
            jax.ShapeDtypeStruct((R, FRONT), F32),
            jax.ShapeDtypeStruct((M, M), F32),
            jax.ShapeDtypeStruct((8, M), F32),
        ),
        in_specs=vmem(5),
        out_specs=tuple(vmem(3)),
        scratch_shapes=[
            pltpu.VMEM((M, M), F32), pltpu.VMEM((R, R), F32), pltpu.VMEM((M, M), BF16), pltpu.VMEM((M, M), BF16)
        ],
        compiler_params=PARAMS,
        name="leaf",
    )(coords, latent, labels, order, bases)


def eliminate(left, gathered_ref, z_ref):
    inverse = newton_inverse(gathered_ref[:, 0:R] + eye(R), z_ref)
    return dot3(split(inverse), split(gathered_ref[:, R:left * R + LANES]))


def level_kernel(left, gathered_ref, own_ref, next_ref, h_ref, z_ref):
    h = eliminate(left, gathered_ref, z_ref)
    h_ref[...] = h
    width = (left - 1) * R
    h_parts = split(h)
    mine = own_tile() * 8
    wanted = lax.broadcasted_iota(jnp.int32, (8, R), 1) == lax.broadcasted_iota(jnp.int32, (8, R), 0) + mine
    one_hot = jnp.where(wanted, 1.0, 0.0).astype(BF16)
    lane = lax.broadcasted_iota(jnp.int32, (8, LANES), 1)
    tile = own_ref[:, left * R:left * R + LANES]
    source, target = left * R + LANES, 0
    for k in range(1, left):
        block = split3(gathered_ref[:, k * R:(k + 1) * R])
        rows = dot(one_hot, block[0], NT) + dot(one_hot, block[1], NT) + dot(one_hot, block[2], NT)
        drop = dot3(split(rows), h_parts)
        span = (left - k) * R
        next_ref[:, target:target + span] = own_ref[:, source:source + span] - drop[:, (k - 1) * R:width]
        source, target = source + span, target + span
        if k == 1:
            target += LANES
        at = LEVELS - left
        tile = tile - jnp.where(lane == at + k, drop[:, width + at:width + at + 1], 0.0)
    next_ref[:, width:width + LANES] = tile


def own_width(left):
    return LANES + R * (left * (left + 1) // 2)


def level_call(left, gathered, own):
    return pl.pallas_call(
        functools.partial(level_kernel, left),
        out_shape=(
            jax.ShapeDtypeStruct((8, own_width(left - 1)), F32),
            jax.ShapeDtypeStruct((R, (left - 1) * R + LANES), F32),
        ),
        in_specs=vmem(2),
        out_specs=tuple(vmem(2)),
        scratch_shapes=[pltpu.VMEM((R, R), F32)],
        compiler_params=PARAMS,
        name=f"level{LEVELS - left + 1}",
    )(gathered, own)


def last_kernel(gathered_ref, h1_ref, h2_ref, h3_ref, inverse_ref, rows_ref, basis_ref, out_ref, z_ref):
    h4 = eliminate(1, gathered_ref, z_ref)
    total = jnp.zeros((16, M), F32)
    later = []
    for level in reversed(range(LEVELS)):
        rest = LEVELS - 1 - level
        h_ref = (h1_ref, h2_ref, h3_ref, None)[level]
        tile = h4 if h_ref is None else h_ref[:, rest * R:rest * R + LANES]
        z = jnp.broadcast_to(tile.T[level:level + 1, :], (8, R))
        for k, done in enumerate(later):
            z = z - dot_f32(done, h_ref[:, k * R:(k + 1) * R], NT)
        later.insert(0, z)
        hi, mid, lo = split3(z[0:1])
        row = lax.broadcasted_iota(jnp.int32, (16, R), 0)
        packed = jnp.where(row == 0, hi.astype(F32), jnp.where(row == 1, mid.astype(F32), jnp.where(row == 2, lo.astype(F32), 0.0)))
        total = total + dot(packed.astype(BF16), basis_ref[level])
    spread = (total[0:1] + total[1:2]) + total[2:3]
    right = rows_ref[1:2] - rows_ref[0:1] * spread
    out_ref[...] = dot_f32(jnp.broadcast_to(right, (8, M)), inverse_ref[...])


def last_call(gathered, h1, h2, h3, inverse, rows, bases):
    return pl.pallas_call(
        last_kernel,
        out_shape=jax.ShapeDtypeStruct((8, M), F32),
        in_specs=vmem(7),
        out_specs=vmem(1)[0],
        scratch_shapes=[pltpu.VMEM((R, R), F32)],
        compiler_params=PARAMS,
        name="last",
    )(gathered, h1, h2, h3, inverse, rows, bases)


def place():
    at = lax.axis_index("leaf")
    return at // PLANE, at // 8 % 4, at // 2 % 4, at % 2


def device(plane, x, y, core):
    return ((plane * 4 + x) * 4 + y) * 2 + core


def own_tile():
    plane, x, y, core = place()
    return core * 16 + x * 4 + y


def along(axis, k):
    plane, x, y, core = place()
    if axis == 0:
        to = (x + k) % 4
        return device(plane, to, y, core), to
    to = (y + k) % 4
    return device(plane, x, to, core), to


def partner():
    plane, x, y, core = place()
    return device(plane, x, y, 1 - core)


def greet(others):
    barrier = pltpu.get_barrier_semaphore()
    for other in others:
        pl.semaphore_signal(barrier, inc=1, device_id=(other,), device_id_type=pl.DeviceIdType.MESH)
    pl.semaphore_wait(barrier, len(others))


def plane_mates():
    return [partner()] + [along(axis, k)[0] for axis in (0, 1) for k in (1, 2, 3)]


def send(source, target, sems, index, to):
    copy = pltpu.make_async_remote_copy(
        src_ref=source,
        dst_ref=target,
        send_sem=sems[0].at[index],
        recv_sem=sems[1].at[index],
        device_id=(to,),
        device_id_type=pl.DeviceIdType.MESH,
    )
    copy.start()
    return copy


def gather(own_ref, gathered_ref, sems, width):
    plane, x, y, core = place()
    half = width // 2 // LANES * LANES
    halves = ((0, slice(0, half)), (1, slice(half, width)))
    fence = []
    index = 0
    first, second = [], []
    for axis, cols in halves:
        copies = []
        for k in (1, 2, 3):
            to = along(axis, k)[0]
            copies.append(send(own_ref.at[:, cols], gathered_ref.at[core, x, y, :, cols], sems, index, to))
            index += 1
        first.append(copies)
        gathered_ref[core, x, y, :, cols] = own_ref[:, cols]
    fence.append(send(own_ref.at[:, 0:width], gathered_ref.at[core, x, y], sems, index, partner()))
    index += 1
    for (axis, cols), copies in zip(halves, first):
        for copy in copies:
            copy.wait_recv()
        moved = []
        for k in (1, 2, 3):
            to = along(1 - axis, k)[0]
            if axis == 0:
                block = gathered_ref.at[core, :, y, :, cols]
            else:
                block = gathered_ref.at[core, x, :, :, cols]
            moved.append(send(block, block, sems, index, to))
            index += 1
        for k in (1, 2, 3):
            at = (along(axis, k)[1], y) if axis == 0 else (x, along(axis, k)[1])
            block = gathered_ref.at[core, at[0], at[1], :, cols]
            fence.append(send(block, block, sems, index, partner()))
            index += 1
        second.append(moved)
    for k in (1, 2, 3):
        for (axis, cols), moved in zip(halves, second):
            moved[k - 1].wait_recv()
            if axis == 0:
                block = gathered_ref.at[core, :, along(1, 4 - k)[1], :, cols]
            else:
                block = gathered_ref.at[core, along(0, 4 - k)[1], :, :, cols]
            fence.append(send(block, block, sems, index, partner()))
            index += 1
    for copies in first + second:
        for copy in copies:
            copy.wait_send()
    for copy in fence:
        copy.wait()


GATHER_COPIES = 25
SPLIT = 11 * LANES


def sum_kernel(front_ref, own_ref, gathered_ref, got_ref, a_ref, b_ref, got_a_ref, got_b_ref, a2_ref, b2_ref,
               got_a2_ref, got_b2_ref, send_sem, recv_sem, gather_send, gather_recv):
    plane, x, y, core = place()
    greet(plane_mates())
    sems = (send_sem, recv_sem)
    cols = (slice(0, SPLIT), slice(SPLIT, FRONT))
    other = partner()
    swaps = [send(front_ref.at[1 - core, :, :, :, c], got_ref.at[:, :, :, c], sems, i, other) for i, c in enumerate(cols)]
    swaps[0].wait_recv()
    a_ref[...] = front_ref[core, :, :, :, cols[0]] + got_ref[:, :, :, cols[0]]
    first_a = []
    for k in (1, 2, 3):
        to, at = along(0, k)
        first_a.append(send(a_ref.at[at], got_a_ref.at[k - 1], sems, 1 + k, to))
    swaps[1].wait_recv()
    for i in range(4):
        b_ref[:, i] = front_ref[core, i, :, :, cols[1]] + got_ref[i, :, :, cols[1]]
    first_b = []
    for k in (1, 2, 3):
        to, at = along(1, k)
        first_b.append(send(b_ref.at[at], got_b_ref.at[k - 1], sems, 4 + k, to))
    for copy in first_a:
        copy.wait_recv()
    a2_ref[...] = (a_ref[x] + got_a_ref[0]) + (got_a_ref[1] + got_a_ref[2])
    second_a = []
    for k in (1, 2, 3):
        to, at = along(1, k)
        second_a.append(send(a2_ref.at[at], got_a2_ref.at[k - 1], sems, 7 + k, to))
    for copy in first_b:
        copy.wait_recv()
    b2_ref[...] = (b_ref[y] + got_b_ref[0]) + (got_b_ref[1] + got_b_ref[2])
    second_b = []
    for k in (1, 2, 3):
        to, at = along(0, k)
        second_b.append(send(b2_ref.at[at], got_b2_ref.at[k - 1], sems, 10 + k, to))
    for copy in second_a:
        copy.wait_recv()
    own_ref[:, cols[0]] = (a2_ref[y] + got_a2_ref[0]) + (got_a2_ref[1] + got_a2_ref[2])
    for copy in second_b:
        copy.wait_recv()
    own_ref[:, cols[1]] = (b2_ref[x] + got_b2_ref[0]) + (got_b2_ref[1] + got_b2_ref[2])
    gather(own_ref, gathered_ref, (gather_send, gather_recv), gathered_ref.shape[-1])
    for copy in swaps + first_a + first_b + second_a + second_b:
        copy.wait_send()


def sum_call(front):
    width = LEVELS * R + LANES
    rest = FRONT - SPLIT
    return pl.pallas_call(
        sum_kernel,
        out_shape=(
            jax.ShapeDtypeStruct((8, FRONT), F32),
            jax.ShapeDtypeStruct((2, 4, 4, 8, width), F32),
        ),
        in_specs=vmem(1),
        out_specs=tuple(vmem(2)),
        scratch_shapes=[
            pltpu.VMEM((4, 4, 8, FRONT), F32),
            pltpu.VMEM((4, 4, 8, SPLIT), F32),
            pltpu.VMEM((4, 4, 8, rest), F32),
            pltpu.VMEM((3, 4, 8, SPLIT), F32),
            pltpu.VMEM((3, 4, 8, rest), F32),
            pltpu.VMEM((4, 8, SPLIT), F32),
            pltpu.VMEM((4, 8, rest), F32),
            pltpu.VMEM((3, 8, SPLIT), F32),
            pltpu.VMEM((3, 8, rest), F32),
            pltpu.SemaphoreType.DMA((14,)),
            pltpu.SemaphoreType.DMA((14,)),
            pltpu.SemaphoreType.DMA((GATHER_COPIES,)),
            pltpu.SemaphoreType.DMA((GATHER_COPIES,)),
        ],
        compiler_params=pltpu.CompilerParams(
            vmem_limit_bytes=60 * 1024 * 1024, collective_id=0, has_side_effects=True
        ),
        name="sum_gather",
    )(front.reshape(2, 4, 4, 8, FRONT))


def pair_kernel(step, part_ref, own_ref, gathered_ref, got_ref, send_sem, recv_sem, gather_send, gather_recv):
    plane, x, y, core = place()
    beyond = plane + step - 2 * step * (plane // step % 2)
    mate = device(beyond, x, y, core)
    greet(plane_mates() + [mate])
    swap = send(part_ref, got_ref, (send_sem, recv_sem), 0, mate)
    swap.wait()
    own_ref[...] = part_ref[...] + got_ref[...]
    gather(own_ref, gathered_ref, (gather_send, gather_recv), gathered_ref.shape[-1])


def pair_call(level, part):
    left = LEVELS - level
    width = left * R + LANES
    return pl.pallas_call(
        functools.partial(pair_kernel, 2 ** (level - 1)),
        out_shape=(
            jax.ShapeDtypeStruct(part.shape, F32),
            jax.ShapeDtypeStruct((2, 4, 4, 8, width), F32),
        ),
        in_specs=vmem(1),
        out_specs=tuple(vmem(2)),
        scratch_shapes=[
            pltpu.VMEM(part.shape, F32),
            pltpu.SemaphoreType.DMA((1,)),
            pltpu.SemaphoreType.DMA((1,)),
            pltpu.SemaphoreType.DMA((GATHER_COPIES,)),
            pltpu.SemaphoreType.DMA((GATHER_COPIES,)),
        ],
        compiler_params=pltpu.CompilerParams(
            vmem_limit_bytes=60 * 1024 * 1024, collective_id=level, has_side_effects=True
        ),
        name=f"pair_gather{level}",
    )(part)


def local(coords, latent, labels, site_order, level_bases):
    front, inverse, rows = leaf_call(
        coords, latent.reshape(1, M), labels.reshape(1, M), site_order, level_bases
    )
    own, gathered = sum_call(front)
    h = []
    for level in range(LEVELS):
        left = LEVELS - level
        if level > 0:
            own, gathered = pair_call(level, own)
        gathered = gathered.reshape(R, left * R + LANES)
        if left > 1:
            own, part = level_call(left, gathered, own)
            h.append(part)
    return last_call(gathered, *h, inverse, rows, level_bases)[0]


def solution(mesh):
    placed = (P(None, "leaf"), P("leaf"), P("leaf"), P("leaf", None), P(None, None, "leaf"))
    return jax.shard_map(local, mesh=mesh, in_specs=placed, out_specs=P("leaf"), check_vma=False)
```

```python
import functools
import math

import jax
import jax.numpy as jnp
from jax import lax
from jax.experimental import pallas as pl
from jax.experimental.pallas import tpu as pltpu
from jax.sharding import PartitionSpec as P

F32 = jnp.float32
BF16 = jnp.bfloat16
HIGHEST = lax.Precision.HIGHEST
LENGTH_SCALE = 0.25
VARIANCE = 16.0
ROOT_FIVE = math.sqrt(5.0)
M = 512
R = 256
LEVELS = 4
LANES = 128
PLANE = 32
NN = (((1,), (0,)), ((), ()))
NT = (((1,), (1,)), ((), ()))


def dot(a, b, dims=NN):
    return lax.dot_general(a, b, dims, preferred_element_type=F32)


def dot_f32(a, b, dims=NN):
    return lax.dot_general(a, b, dims, precision=HIGHEST, preferred_element_type=F32)


def split(x):
    hi = x.astype(BF16)
    return hi, (x - hi.astype(F32)).astype(BF16)


def split3(x):
    hi = x.astype(BF16)
    rest = x - hi.astype(F32)
    mid = rest.astype(BF16)
    return hi, mid, (rest - mid.astype(F32)).astype(BF16)


def dot3(a, b, dims=NN):
    return dot(a[0], b[0], dims) + (dot(a[0], b[1], dims) + dot(a[1], b[0], dims))


def packed_rows(v):
    row = lax.broadcasted_iota(jnp.int32, (16, v.shape[1]), 0)
    out = jnp.zeros((16, v.shape[1]), F32)
    for i, part in enumerate(split3(v)):
        out = jnp.where(row == i, part.astype(F32), out)
    return out.astype(BF16)


def row_dot(v, parts, dims=NN):
    rows = packed_rows(v)
    total = dot(rows, parts[0], dims)
    for part in parts[1:]:
        total = total + dot(rows, part, dims)
    return (total[0:1] + total[1:2]) + total[2:3]


def eye(n):
    return jnp.where(
        lax.broadcasted_iota(jnp.int32, (n, n), 0) == lax.broadcasted_iota(jnp.int32, (n, n), 1), 1.0, 0.0
    ).astype(F32)


def newton_inverse(s, z_ref):
    n = s.shape[0]
    bound = jnp.max(jnp.sum(jnp.abs(s), axis=0, keepdims=True))
    alpha = 2.0 / (1.0 + bound)
    gap = (bound - 1.0) / (bound + 1.0)
    scale = 2.0 / (2.0 - gap * gap)
    z_ref[...] = (alpha * scale) * (2.0 * eye(n) - alpha * s)
    gap = gap * gap / (2.0 - gap * gap)
    parts = split(s)

    def body(gap):
        z = z_ref[...]
        zs = split(z)
        residual = eye(n) - dot3(parts, zs)
        scale = 2.0 / (2.0 - gap * gap)
        z_ref[...] = scale * (z + dot3(zs, split(residual)))
        return gap * gap / (2.0 - gap * gap)

    lax.while_loop(lambda gap: gap > 2e-3, body, gap)
    z = z_ref[...]
    residual = eye(n) - dot_f32(s, z)
    return z + dot3(split(z), split(residual))


def leaf_kernel(coord_ref, latent_ref, label_ref, order_ref, basis_ref, mh_ref, ml_ref, tile_ref,
                inverse_ref, rows_ref, a_ref, z_ref):
    picked = lax.broadcasted_iota(jnp.int32, (M, M), 0) == order_ref[...]
    one_hot = jnp.where(picked, 1.0, 0.0).astype(BF16)
    hi, mid, lo = split3(latent_ref[...])
    row = lax.broadcasted_iota(jnp.int32, (16, M), 0)
    packed = jnp.where(row == 0, hi.astype(F32), 0.0)
    packed = jnp.where(row == 1, mid.astype(F32), packed)
    packed = jnp.where(row == 2, lo.astype(F32), packed)
    packed = jnp.where(row == 3, label_ref[...].astype(F32), packed)
    got = dot(packed.astype(BF16), one_hot)
    tree_latent = (got[0:1] + got[1:2]) + got[2:3]
    tree_target = got[3:4]
    probability = 1.0 / (1.0 + jnp.exp(-tree_latent))
    weight = probability * (1.0 - probability)
    root_weight = jnp.sqrt(weight)
    right_side = root_weight * (weight * tree_latent + tree_target - probability)

    def column(value, i):
        return jnp.broadcast_to(value[:, i * LANES:(i + 1) * LANES], (LANES, LANES)).T

    axes = [coord_ref[k:k + 1, :] for k in range(3)]
    columns = []
    for i in range(4):
        cols = [column(axis, i) for axis in axes]
        weight_col = column(root_weight, i)
        columns.append(weight_col)
        for j in range(i, 4):
            span = slice(j * LANES, (j + 1) * LANES)
            total = None
            for axis, col in zip(axes, cols):
                difference = col - axis[:, span]
                total = difference * difference if total is None else total + difference * difference
            scaled = (ROOT_FIVE / LENGTH_SCALE) * jnp.sqrt(total)
            kernel = VARIANCE * (1.0 + scaled + scaled * scaled / 3.0) * jnp.exp(-scaled)
            block = weight_col * kernel * root_weight[:, span]
            if i == j:
                block = block + eye(LANES)
            a_ref[i * LANES:(i + 1) * LANES, span] = block
            if i != j:
                a_ref[span, i * LANES:(i + 1) * LANES] = block.T

    top, bottom = slice(0, R), slice(R, M)
    x = newton_inverse(a_ref[top, top], z_ref)
    u = dot_f32(x, a_ref[top, bottom])
    v = dot_f32(a_ref[bottom, top], x)
    schur = newton_inverse(a_ref[bottom, bottom] - dot_f32(v, a_ref[top, bottom]), z_ref)
    us = dot_f32(u, schur)
    inverse_ref[bottom, bottom] = schur
    inverse_ref[top, bottom] = -us
    inverse_ref[bottom, top] = -dot_f32(schur, v)
    inverse_ref[top, top] = x + dot_f32(us, v)

    for i in range(4):
        for j in range(4):
            rows, span = slice(i * LANES, (i + 1) * LANES), slice(j * LANES, (j + 1) * LANES)
            hi, lo = split(columns[i] * inverse_ref[rows, span] * root_weight[:, span])
            mh_ref[rows, span] = hi
            ml_ref[rows, span] = lo
    solved = row_dot(right_side, split3(inverse_ref[...]))
    weighted = split3(root_weight * solved)
    lane = lax.broadcasted_iota(jnp.int32, (LANES, M), 0)
    tile = jnp.zeros((R, LANES), F32)
    for level in range(LEVELS):
        for piece in weighted:
            placed = jnp.where(lane == level, piece.astype(F32), 0.0).astype(BF16)
            tile = tile + dot(basis_ref[level], placed, NT)
    tile_ref[...] = tile
    row = lax.broadcasted_iota(jnp.int32, (8, M), 0)
    rows_ref[...] = jnp.where(row == 0, root_weight, right_side)


def vmem(n):
    return [pl.BlockSpec(memory_space=pltpu.VMEM)] * n


FRONT = LEVELS * R + LANES + 6 * R
PARAMS = pltpu.CompilerParams(vmem_limit_bytes=60 * 1024 * 1024)


def leaf_call(coords, latent, labels, order, bases):
    return pl.pallas_call(
        leaf_kernel,
        out_shape=(
            jax.ShapeDtypeStruct((M, M), BF16),
            jax.ShapeDtypeStruct((M, M), BF16),
            jax.ShapeDtypeStruct((R, LANES), F32),
            jax.ShapeDtypeStruct((M, M), F32),
            jax.ShapeDtypeStruct((8, M), F32),
        ),
        in_specs=vmem(5),
        out_specs=tuple(vmem(5)),
        scratch_shapes=[pltpu.VMEM((M, M), F32), pltpu.VMEM((R, R), F32)],
        compiler_params=PARAMS,
        name="leaf",
    )(coords, latent, labels, order, bases)


def inverse_kernel(gathered_ref, inverse_ref, z_ref):
    inverse_ref[...] = newton_inverse(gathered_ref[...] + eye(R), z_ref)


def inverse_call(gathered):
    return pl.pallas_call(
        inverse_kernel,
        grid=(1,),
        out_shape=jax.ShapeDtypeStruct((R, R), F32),
        in_specs=[pl.BlockSpec((R, R), lambda i: (0, 0))],
        out_specs=pl.BlockSpec((R, R), lambda i: (0, 0)),
        scratch_shapes=[pltpu.VMEM((R, R), F32)],
        compiler_params=PARAMS,
        name="inverse",
    )(gathered)


def eliminate(left, inverse_ref, gathered_ref, own_ref, next_ref, h_ref):
    h = dot3(split(inverse_ref[...]), split(gathered_ref[:, R:left * R + LANES]))
    h_ref[...] = h
    width = (left - 1) * R
    h_parts = split(h)
    mine = own_tile() * 8
    wanted = lax.broadcasted_iota(jnp.int32, (8, R), 1) == lax.broadcasted_iota(jnp.int32, (8, R), 0) + mine
    one_hot = jnp.where(wanted, 1.0, 0.0).astype(BF16)
    lane = lax.broadcasted_iota(jnp.int32, (8, LANES), 1)
    tile = own_ref[:, left * R:left * R + LANES]
    source, target = left * R + LANES, 0
    for k in range(1, left):
        block = split(gathered_ref[:, k * R:(k + 1) * R])
        rows = dot(one_hot, block[0], NT) + dot(one_hot, block[1], NT)
        drop = dot3(split(rows), h_parts)
        span = (left - k) * R
        next_ref[:, target:target + span] = own_ref[:, source:source + span] - drop[:, (k - 1) * R:width]
        source, target = source + span, target + span
        if k == 1:
            target += LANES
        at = LEVELS - left
        tile = tile - jnp.where(lane == at + k, drop[:, width + at:width + at + 1], 0.0)
    next_ref[:, width:width + LANES] = tile


def own_width(left):
    return LANES + R * (left * (left + 1) // 2)


def last_kernel(gathered_ref, h1_any, h2_any, h3_any, inverse_any, basis_any, rows_ref, out_ref,
                z_ref, h1_ref, h2_ref, h3_ref, inverse_ref, basis_ref, sems):
    copies = [
        pltpu.make_async_copy(source, target, sems.at[i])
        for i, (source, target) in enumerate(
            ((h3_any, h3_ref), (h2_any, h2_ref), (h1_any, h1_ref), (inverse_any, inverse_ref), (basis_any, basis_ref))
        )
    ]
    for copy in copies:
        copy.start()
    inverse = newton_inverse(gathered_ref[:, 0:R] + eye(R), z_ref)
    h4 = dot3(split(inverse), split(gathered_ref[:, R:R + LANES]))
    for copy in copies:
        copy.wait()
    h_refs = (h1_ref, h2_ref, h3_ref)
    rows = [h_refs[i][:, (3 - i) * R:(3 - i) * R + LANES].T[i:i + 1, :] for i in range(3)] + [h4.T[3:4, :]]
    total = jnp.zeros((16, M), F32)
    for level in reversed(range(LEVELS)):
        z = packed_rows(rows[level])
        total = total + dot(z, basis_ref[level])
        for i in range(level):
            at = (level - i - 1) * R
            parts = split(h_refs[i][:, at:at + R])
            drop = dot(z, parts[0], NT) + dot(z, parts[1], NT)
            rows[i] = rows[i] - ((drop[0:1] + drop[1:2]) + drop[2:3])
    spread = (total[0:1] + total[1:2]) + total[2:3]
    out_ref[...] = row_dot(rows_ref[1:2] - rows_ref[0:1] * spread, split3(inverse_ref[...]))


def last_call(gathered, h1, h2, h3, inverse, rows, bases):
    kept = (h1, h2, h3, inverse, bases)
    return pl.pallas_call(
        last_kernel,
        out_shape=jax.ShapeDtypeStruct((1, M), F32),
        in_specs=vmem(1) + [pl.BlockSpec(memory_space=pl.ANY)] * 5 + vmem(1),
        out_specs=vmem(1)[0],
        scratch_shapes=[pltpu.VMEM((R, R), F32)]
        + [pltpu.VMEM(array.shape, array.dtype) for array in kept]
        + [pltpu.SemaphoreType.DMA((5,))],
        compiler_params=PARAMS,
        name="last",
    )(gathered, *kept, rows)


def place():
    at = lax.axis_index("leaf")
    return at // PLANE, at // 8 % 4, at // 2 % 4, at % 2


def device(plane, x, y, core):
    return ((plane * 4 + x) * 4 + y) * 2 + core


def own_tile():
    plane, x, y, core = place()
    return core * 16 + x * 4 + y


def along(axis, k):
    plane, x, y, core = place()
    if axis == 0:
        to = (x + k) % 4
        return device(plane, to, y, core), to
    to = (y + k) % 4
    return device(plane, x, to, core), to


def partner():
    plane, x, y, core = place()
    return device(plane, x, y, 1 - core)


def greet(others):
    barrier = pltpu.get_barrier_semaphore()
    for other in others:
        pl.semaphore_signal(barrier, inc=1, device_id=(other,), device_id_type=pl.DeviceIdType.MESH)


def meet(others):
    pl.semaphore_wait(pltpu.get_barrier_semaphore(), len(others))


def plane_mates():
    return [partner()] + [along(axis, k)[0] for axis in (0, 1) for k in (1, 2, 3)]


def send(source, target, sems, index, to):
    copy = pltpu.make_async_remote_copy(
        src_ref=source,
        dst_ref=target,
        send_sem=sems[0].at[index],
        recv_sem=sems[1].at[index],
        device_id=(to,),
        device_id_type=pl.DeviceIdType.MESH,
    )
    copy.start()
    return copy


class Gather:
    def __init__(self, own_ref, gathered_ref, sems):
        width = gathered_ref.shape[-1]
        half = width // 2 // LANES * LANES
        self.own, self.out, self.sems = own_ref, gathered_ref, sems
        self.halves = ((0, slice(0, half)), (1, slice(half, width)))
        self.width, self.index, self.fence = width, 0, []
        self.first, self.second = [], []

    def send(self, source, target, to):
        self.index += 1
        return send(source, target, self.sems, self.index - 1, to)

    def share(self, block):
        self.fence.append(self.send(block, block, partner()))

    def start(self):
        plane, x, y, core = place()
        for axis, cols in self.halves:
            self.first.append([
                self.send(self.own.at[:, cols], self.out.at[core, x, y, :, cols], along(axis, k)[0])
                for k in (2, 1, 3)
            ])
        whole = slice(0, self.width)
        self.fence.append(self.send(self.own.at[:, whole], self.out.at[core, x, y], partner()))
        self.out[core, x, y] = self.own[:, whole]

    def turn(self):
        plane, x, y, core = place()
        for (axis, cols), copies in zip(self.halves, self.first):
            for copy in copies:
                copy.wait_recv()
            if axis == 0:
                block = self.out.at[core, :, y, :, cols]
            else:
                block = self.out.at[core, x, :, :, cols]
            self.second.append([self.send(block, block, along(1 - axis, k)[0]) for k in (2, 1, 3)])
        for axis, cols in self.halves:
            for k in (1, 2, 3):
                at = (along(axis, k)[1], y) if axis == 0 else (x, along(axis, k)[1])
                self.share(self.out.at[core, at[0], at[1], :, cols])

    def finish(self):
        plane, x, y, core = place()
        for i, k in ((1, 1), (2, 3), (0, 2)):
            for (axis, cols), moved in zip(self.halves, self.second):
                moved[i].wait_recv()
                if axis == 0:
                    self.share(self.out.at[core, :, along(1, 4 - k)[1], :, cols])
                else:
                    self.share(self.out.at[core, along(0, 4 - k)[1], :, :, cols])

    def close(self):
        for copies in self.first + self.second:
            for copy in copies:
                copy.wait_send()
        for copy in self.fence:
            copy.wait()


class Scatter:
    def __init__(self, mine, got, a, b, got_a, got_b, a2, b2, got_a2, got_b2, sems):
        self.mine, self.got, self.a, self.b, self.got_a, self.got_b = mine, got, a, b, got_a, got_b
        self.a2, self.b2, self.got_a2, self.got_b2, self.sems = a2, b2, got_a2, got_b2, sems
        split_at = a.shape[-1]
        self.cols = (slice(0, split_at), slice(split_at, mine.shape[-1]))
        self.all = []

    def spread(self, source, target, axis, index):
        copies = []
        for k in (2, 1, 3):
            to, at = along(axis, k)
            copies.append(send(source.at[at], target.at[k - 1], self.sems, index + k - 1, to))
        self.all += copies
        return copies

    def swap(self, theirs):
        self.swaps = [
            send(theirs.at[:, :, :, c], self.got.at[:, :, :, c], self.sems, i, partner()) for i, c in enumerate(self.cols)
        ]
        self.all += self.swaps

    def first(self):
        self.swaps[0].wait_recv()
        self.a[...] = self.mine[:, :, :, self.cols[0]] + self.got[:, :, :, self.cols[0]]
        self.first_a = self.spread(self.a, self.got_a, 0, 2)
        self.swaps[1].wait_recv()
        for i in range(4):
            self.b[:, i] = self.mine[i, :, :, self.cols[1]] + self.got[i, :, :, self.cols[1]]
        self.first_b = self.spread(self.b, self.got_b, 1, 5)

    def second(self):
        plane, x, y, core = place()
        for copy in self.first_a:
            copy.wait_recv()
        self.a2[...] = (self.a[x] + self.got_a[0]) + (self.got_a[1] + self.got_a[2])
        self.second_a = self.spread(self.a2, self.got_a2, 1, 8)
        for copy in self.first_b:
            copy.wait_recv()
        self.b2[...] = (self.b[y] + self.got_b[0]) + (self.got_b[1] + self.got_b[2])
        self.second_b = self.spread(self.b2, self.got_b2, 0, 11)

    def finish(self, own_ref, offset):
        plane, x, y, core = place()
        cut, end = offset + self.cols[0].stop, offset + self.cols[1].stop
        for copy in self.second_a:
            copy.wait_recv()
        own_ref[:, offset:cut] = (self.a2[y] + self.got_a2[0]) + (self.got_a2[1] + self.got_a2[2])
        for copy in self.second_b:
            copy.wait_recv()
        own_ref[:, cut:end] = (self.b2[x] + self.got_b2[0]) + (self.got_b2[1] + self.got_b2[2])

    def close(self):
        for copy in self.all:
            copy.wait_send()


GATHER_COPIES = 25
HEAD = LEVELS * R + LANES
TAIL = FRONT - HEAD
HEAD_CUT = 5 * LANES
TAIL_CUT = 6 * LANES
TILES = (4, 4, 8)


def scatter_scratch(width, cut):
    rest = width - cut
    shapes = [
        TILES + (width,), TILES + (width,), TILES + (width,), TILES + (cut,), TILES + (rest,), (3, 4, 8, cut),
        (3, 4, 8, rest), (4, 8, cut), (4, 8, rest), (3, 8, cut), (3, 8, rest),
    ]
    return [pltpu.VMEM(shape, F32) for shape in shapes] + [pltpu.SemaphoreType.DMA((14,))] * 2


def sum_kernel(mh_ref, ml_ref, tile_ref, basis_ref, own_ref, gathered_ref, *scratch):
    plane, x, y, core = place()
    mates = plane_mates()
    greet(mates)

    def grams(half, level, target, offset):
        basis = basis_ref[level, pl.ds(pl.multiple_of(half * LANES, LANES), LANES), :]
        part = split(dot(basis, mh_ref[...]) + dot(basis, ml_ref[...]))
        for other in range(level, LEVELS):
            block = dot(part[0], basis_ref[other], NT) + dot(part[1], basis_ref[other], NT)
            target[:, :, :, offset:offset + R] = block.reshape(TILES + (R,))
            offset += R
        if level == 0:
            tile = tile_ref[pl.ds(pl.multiple_of(half * LANES, LANES), LANES), :]
            target[:, :, :, offset:offset + LANES] = tile.reshape(TILES + (LANES,))

    def tail(half, target):
        grams(half, 1, target, 0)
        grams(half, 2, target, 3 * R)
        grams(half, 3, target, 5 * R)

    theirs0, mine0, theirs1, mine1 = scratch[0], scratch[1], scratch[13], scratch[14]
    head_sum = Scatter(*scratch[1:11], scratch[11:13])
    tail_sum = Scatter(*scratch[14:24], scratch[24:26])
    gather = Gather(own_ref, gathered_ref, scratch[26:28])
    grams(1 - core, 0, theirs0, 0)
    meet(mates)
    head_sum.swap(theirs0)
    grams(core, 0, mine0, 0)
    head_sum.first()
    tail(1 - core, theirs1)
    tail_sum.swap(theirs1)
    tail(core, mine1)
    head_sum.second()
    tail_sum.first()
    head_sum.finish(own_ref, 0)
    gather.start()
    gather.turn()
    tail_sum.second()
    gather.finish()
    tail_sum.finish(own_ref, HEAD)
    gather.close()
    head_sum.close()
    tail_sum.close()


def sum_call(mh, ml, tile, bases):
    return pl.pallas_call(
        sum_kernel,
        out_shape=(
            jax.ShapeDtypeStruct((8, FRONT), F32),
            jax.ShapeDtypeStruct((2,) + TILES + (HEAD,), F32),
        ),
        in_specs=vmem(4),
        out_specs=tuple(vmem(2)),
        scratch_shapes=scatter_scratch(HEAD, HEAD_CUT)
        + scatter_scratch(TAIL, TAIL_CUT)
        + [pltpu.SemaphoreType.DMA((GATHER_COPIES,))] * 2,
        compiler_params=pltpu.CompilerParams(
            vmem_limit_bytes=60 * 1024 * 1024, collective_id=0, has_side_effects=True
        ),
        name="sum_gather",
    )(mh, ml, tile, bases)


def pair_kernel(level, inverse_ref, before_ref, had_ref, own_ref, gathered_ref, h_ref, part_ref, got_ref,
                send_sem, recv_sem, gather_send, gather_recv):
    plane, x, y, core = place()
    step = 2 ** (level - 1)
    if level == LEVELS - 1:
        beyond = 2 * step - 1 - plane
    else:
        beyond = plane + step - 2 * step * (plane // step % 2)
    mates = plane_mates() + [device(beyond, x, y, core)]
    greet(mates)
    eliminate(LEVELS - level + 1, inverse_ref, before_ref, had_ref, part_ref, h_ref)
    meet(mates)
    swap = send(part_ref, got_ref, (send_sem, recv_sem), 0, mates[-1])
    swap.wait_recv()
    own_ref[...] = part_ref[...] + got_ref[...]
    gather = Gather(own_ref, gathered_ref, (gather_send, gather_recv))
    gather.start()
    gather.turn()
    gather.finish()
    gather.close()
    swap.wait_send()


def pair_call(level, inverse, gathered, own):
    left = LEVELS - level
    width = left * R + LANES
    slab = (8, own_width(left))
    return pl.pallas_call(
        functools.partial(pair_kernel, level),
        out_shape=(
            jax.ShapeDtypeStruct(slab, F32),
            jax.ShapeDtypeStruct((2,) + TILES + (width,), F32),
            jax.ShapeDtypeStruct((R, width), F32),
        ),
        in_specs=vmem(3),
        out_specs=tuple(vmem(3)),
        scratch_shapes=[
            pltpu.VMEM(slab, F32),
            pltpu.VMEM(slab, F32),
            pltpu.SemaphoreType.DMA((1,)),
            pltpu.SemaphoreType.DMA((1,)),
            pltpu.SemaphoreType.DMA((GATHER_COPIES,)),
            pltpu.SemaphoreType.DMA((GATHER_COPIES,)),
        ],
        compiler_params=pltpu.CompilerParams(
            vmem_limit_bytes=60 * 1024 * 1024, collective_id=level, has_side_effects=True
        ),
        name=f"pair_gather{level}",
    )(inverse, gathered, own)


def local(coords, latent, labels, site_order, level_bases):
    mh, ml, tile, inverse, rows = leaf_call(
        coords, latent.reshape(1, M), labels.reshape(1, M), site_order, level_bases
    )
    own, gathered = sum_call(mh, ml, tile, level_bases)
    gathered = gathered.reshape(R, HEAD)
    h = []
    for level in range(1, LEVELS):
        own, after, part = pair_call(level, inverse_call(gathered), gathered, own)
        h.append(part)
        gathered = after.reshape(R, (LEVELS - level) * R + LANES)
    return last_call(gathered, *h, inverse, rows, level_bases).reshape(M)


def solution(mesh):
    placed = (P(None, "leaf"), P("leaf"), P("leaf"), P("leaf", None), P(None, None, "leaf"))
    return jax.shard_map(local, mesh=mesh, in_specs=placed, out_specs=P("leaf"), check_vma=False)
```

```python
import functools
import math

import jax
import jax.numpy as jnp
from jax import lax
from jax.experimental import pallas as pl
from jax.experimental.pallas import tpu as pltpu
from jax.sharding import PartitionSpec as P

F32 = jnp.float32
BF16 = jnp.bfloat16
HIGHEST = lax.Precision.HIGHEST
LENGTH_SCALE = 0.25
VARIANCE = 16.0
ROOT_FIVE = math.sqrt(5.0)
M = 512
R = 256
LEVELS = 4
LANES = 128
PLANE = 32
NN = (((1,), (0,)), ((), ()))
NT = (((1,), (1,)), ((), ()))


def dot(a, b, dims=NN):
    return lax.dot_general(a, b, dims, preferred_element_type=F32)


def dot_f32(a, b, dims=NN):
    return lax.dot_general(a, b, dims, precision=HIGHEST, preferred_element_type=F32)


def split(x):
    hi = x.astype(BF16)
    return hi, (x - hi.astype(F32)).astype(BF16)


def split3(x):
    hi = x.astype(BF16)
    rest = x - hi.astype(F32)
    mid = rest.astype(BF16)
    return hi, mid, (rest - mid.astype(F32)).astype(BF16)


def dot3(a, b, dims=NN):
    return dot(a[0], b[0], dims) + (dot(a[0], b[1], dims) + dot(a[1], b[0], dims))


def packed_rows(v):
    row = lax.broadcasted_iota(jnp.int32, (16, v.shape[1]), 0)
    out = jnp.zeros((16, v.shape[1]), F32)
    for i, part in enumerate(split3(v)):
        out = jnp.where(row == i, part.astype(F32), out)
    return out.astype(BF16)


def row_dot(v, parts, dims=NN):
    rows = packed_rows(v)
    total = dot(rows, parts[0], dims)
    for part in parts[1:]:
        total = total + dot(rows, part, dims)
    return (total[0:1] + total[1:2]) + total[2:3]


def eye(n):
    return jnp.where(
        lax.broadcasted_iota(jnp.int32, (n, n), 0) == lax.broadcasted_iota(jnp.int32, (n, n), 1), 1.0, 0.0
    ).astype(F32)


def newton_inverses(matrices, z_refs):
    n = matrices[0].shape[0]
    sums = [jnp.sum(jnp.abs(s), axis=0, keepdims=True) for s in matrices]
    bound = jnp.max(functools.reduce(jnp.maximum, sums))
    alpha = 2.0 / (1.0 + bound)
    gap = (bound - 1.0) / (bound + 1.0)
    scale = 2.0 / (2.0 - gap * gap)
    for s, z_ref in zip(matrices, z_refs):
        z_ref[...] = (alpha * scale) * (2.0 * eye(n) - alpha * s)
    gap = gap * gap / (2.0 - gap * gap)
    parts = [split(s) for s in matrices]

    def body(gap):
        scale = 2.0 / (2.0 - gap * gap)
        for part, z_ref in zip(parts, z_refs):
            z = z_ref[...]
            zs = split(z)
            residual = eye(n) - dot3(part, zs)
            z_ref[...] = scale * (z + dot3(zs, split(residual)))
        return gap * gap / (2.0 - gap * gap)

    lax.while_loop(lambda gap: gap > 2e-3, body, gap)
    found = []
    for s, z_ref in zip(matrices, z_refs):
        z = z_ref[...]
        residual = eye(n) - dot_f32(s, z)
        found.append(z + dot3(split(z), split(residual)))
    return found


def newton_inverse(s, z_ref):
    return newton_inverses([s], [z_ref])[0]


def leaf_kernel(coord_ref, latent_ref, label_ref, order_ref, basis_ref, mh_ref, ml_ref, tile_ref,
                inverse_ref, rows_ref, a_ref, z_ref):
    picked = lax.broadcasted_iota(jnp.int32, (M, M), 0) == order_ref[...]
    one_hot = jnp.where(picked, 1.0, 0.0).astype(BF16)
    hi, mid, lo = split3(latent_ref[...])
    row = lax.broadcasted_iota(jnp.int32, (16, M), 0)
    packed = jnp.where(row == 0, hi.astype(F32), 0.0)
    packed = jnp.where(row == 1, mid.astype(F32), packed)
    packed = jnp.where(row == 2, lo.astype(F32), packed)
    packed = jnp.where(row == 3, label_ref[...].astype(F32), packed)
    got = dot(packed.astype(BF16), one_hot)
    tree_latent = (got[0:1] + got[1:2]) + got[2:3]
    tree_target = got[3:4]
    probability = 1.0 / (1.0 + jnp.exp(-tree_latent))
    weight = probability * (1.0 - probability)
    root_weight = jnp.sqrt(weight)
    right_side = root_weight * (weight * tree_latent + tree_target - probability)

    def column(value, i):
        return jnp.broadcast_to(value[:, i * LANES:(i + 1) * LANES], (LANES, LANES)).T

    axes = [coord_ref[k:k + 1, :] for k in range(3)]
    columns = []
    for i in range(4):
        cols = [column(axis, i) for axis in axes]
        weight_col = column(root_weight, i)
        columns.append(weight_col)
        for j in range(i, 4):
            span = slice(j * LANES, (j + 1) * LANES)
            total = None
            for axis, col in zip(axes, cols):
                difference = col - axis[:, span]
                total = difference * difference if total is None else total + difference * difference
            scaled = (ROOT_FIVE / LENGTH_SCALE) * jnp.sqrt(total)
            kernel = VARIANCE * (1.0 + scaled + scaled * scaled / 3.0) * jnp.exp(-scaled)
            block = weight_col * kernel * root_weight[:, span]
            if i == j:
                block = block + eye(LANES)
            a_ref[i * LANES:(i + 1) * LANES, span] = block
            if i != j:
                a_ref[span, i * LANES:(i + 1) * LANES] = block.T

    top, bottom = slice(0, R), slice(R, M)
    x = newton_inverse(a_ref[top, top], z_ref)
    u = dot_f32(x, a_ref[top, bottom])
    v = dot_f32(a_ref[bottom, top], x)
    schur = newton_inverse(a_ref[bottom, bottom] - dot_f32(v, a_ref[top, bottom]), z_ref)
    us = dot_f32(u, schur)
    inverse_ref[bottom, bottom] = schur
    inverse_ref[top, bottom] = -us
    inverse_ref[bottom, top] = -dot_f32(schur, v)
    inverse_ref[top, top] = x + dot_f32(us, v)

    for i in range(4):
        for j in range(4):
            rows, span = slice(i * LANES, (i + 1) * LANES), slice(j * LANES, (j + 1) * LANES)
            hi, lo = split(columns[i] * inverse_ref[rows, span] * root_weight[:, span])
            mh_ref[rows, span] = hi
            ml_ref[rows, span] = lo
    solved = row_dot(right_side, split3(inverse_ref[...]))
    weighted = [jnp.broadcast_to(part.astype(F32), (LANES, M)).astype(BF16) for part in split3(root_weight * solved)]
    bases = basis_ref[...].reshape(LEVELS * R, M)
    projections = dot(bases, weighted[0], NT) + (dot(bases, weighted[1], NT) + dot(bases, weighted[2], NT))
    lane = lax.broadcasted_iota(jnp.int32, (R, LANES), 1)
    tile = jnp.zeros((R, LANES), F32)
    for level in range(LEVELS):
        tile = jnp.where(lane == level, projections[level * R:(level + 1) * R], tile)
    tile_ref[...] = tile
    row = lax.broadcasted_iota(jnp.int32, (8, M), 0)
    rows_ref[...] = jnp.where(row == 0, root_weight, right_side)


def vmem(n):
    return [pl.BlockSpec(memory_space=pltpu.VMEM)] * n


FRONT = LEVELS * R + LANES + 6 * R
PARAMS = pltpu.CompilerParams(vmem_limit_bytes=60 * 1024 * 1024)


def leaf_call(coords, latent, labels, order, bases):
    return pl.pallas_call(
        leaf_kernel,
        out_shape=(
            jax.ShapeDtypeStruct((M, M), BF16),
            jax.ShapeDtypeStruct((M, M), BF16),
            jax.ShapeDtypeStruct((R, LANES), F32),
            jax.ShapeDtypeStruct((M, M), F32),
            jax.ShapeDtypeStruct((8, M), F32),
        ),
        in_specs=vmem(5),
        out_specs=tuple(vmem(5)),
        scratch_shapes=[pltpu.VMEM((M, M), F32), pltpu.VMEM((R, R), F32)],
        compiler_params=PARAMS,
        name="leaf",
    )(coords, latent, labels, order, bases)


def inverse_kernel(gathered_ref, inverse_ref, z_ref):
    inverse_ref[...] = newton_inverse(gathered_ref[...] + eye(R), z_ref)


def inverse_call(gathered):
    return pl.pallas_call(
        inverse_kernel,
        grid=(1,),
        out_shape=jax.ShapeDtypeStruct((R, R), F32),
        in_specs=[pl.BlockSpec((R, R), lambda i: (0, 0))],
        out_specs=pl.BlockSpec((R, R), lambda i: (0, 0)),
        scratch_shapes=[pltpu.VMEM((R, R), F32)],
        compiler_params=PARAMS,
        name="inverse",
    )(gathered)


def eliminate(left, inverse_ref, gathered_ref, own_ref, next_ref, h_ref):
    h = dot3(split(inverse_ref[...]), split(gathered_ref[:, R:left * R + LANES]))
    h_ref[...] = h
    width = (left - 1) * R
    h_parts = split(h)
    mine = own_tile() * 8
    wanted = lax.broadcasted_iota(jnp.int32, (8, R), 1) == lax.broadcasted_iota(jnp.int32, (8, R), 0) + mine
    one_hot = jnp.where(wanted, 1.0, 0.0).astype(BF16)
    lane = lax.broadcasted_iota(jnp.int32, (8, LANES), 1)
    tile = own_ref[:, left * R:left * R + LANES]
    source, target = left * R + LANES, 0
    for k in range(1, left):
        block = split(gathered_ref[:, k * R:(k + 1) * R])
        rows = dot(one_hot, block[0], NT) + dot(one_hot, block[1], NT)
        drop = dot3(split(rows), h_parts)
        span = (left - k) * R
        next_ref[:, target:target + span] = own_ref[:, source:source + span] - drop[:, (k - 1) * R:width]
        source, target = source + span, target + span
        if k == 1:
            target += LANES
        at = LEVELS - left
        tile = tile - jnp.where(lane == at + k, drop[:, width + at:width + at + 1], 0.0)
    next_ref[:, width:width + LANES] = tile


def own_width(left):
    return LANES + R * (left * (left + 1) // 2)


NODE = own_width(2)


def last_kernel(gathered_ref, h1_any, h2_any, inverse_any, basis_any, rows_ref, out_ref,
                za_ref, zb_ref, h1_ref, h2_ref, inverse_ref, basis_ref, sems):
    copies = [
        pltpu.make_async_copy(source, target, sems.at[i])
        for i, (source, target) in enumerate(
            ((h2_any, h2_ref), (h1_any, h1_ref), (inverse_any, inverse_ref), (basis_any, basis_ref))
        )
    ]
    for copy in copies:
        copy.start()
    inverses = newton_inverses(
        [gathered_ref[:, q * NODE:q * NODE + R] + eye(R) for q in range(2)], [za_ref, zb_ref]
    )
    core, right, h3 = eye(R), jnp.zeros((1, R), F32), None
    for q in range(2):
        at = q * NODE
        coupling = gathered_ref[:, at + R:at + 2 * R]
        h = dot3(split(inverses[q]), split(gathered_ref[:, at + R:at + 2 * R + LANES]))
        drop = dot3(split(coupling.T), split(h))
        core = core + (gathered_ref[:, at + 2 * R + LANES:at + NODE] - drop[:, 0:R])
        right = right + (gathered_ref[:, at + 2 * R:at + 2 * R + LANES].T[3:4, :] - drop[:, R:].T[2:3, :])
        h3 = h if h3 is None else h3
    z = row_dot(right, split(newton_inverse(core, za_ref)))
    for copy in copies:
        copy.wait()
    h_all = (h1_ref[...], h2_ref[...], h3)
    rows = [h[:, (3 - i) * R:(3 - i) * R + LANES].T[i:i + 1, :] for i, h in enumerate(h_all)] + [z]
    total = jnp.zeros((16, M), F32)
    for level in reversed(range(LEVELS)):
        z = packed_rows(rows[level])
        total = total + dot(z, basis_ref[level])
        for i in range(level):
            at = (level - i - 1) * R
            parts = split(h_all[i][:, at:at + R])
            drop = dot(z, parts[0], NT) + dot(z, parts[1], NT)
            rows[i] = rows[i] - ((drop[0:1] + drop[1:2]) + drop[2:3])
    spread = (total[0:1] + total[1:2]) + total[2:3]
    out_ref[...] = row_dot(rows_ref[1:2] - rows_ref[0:1] * spread, split3(inverse_ref[...]))


def last_call(gathered, h1, h2, inverse, rows, bases):
    kept = (h1, h2, inverse, bases)
    return pl.pallas_call(
        last_kernel,
        out_shape=jax.ShapeDtypeStruct((1, M), F32),
        in_specs=vmem(1) + [pl.BlockSpec(memory_space=pl.ANY)] * 4 + vmem(1),
        out_specs=vmem(1)[0],
        scratch_shapes=[pltpu.VMEM((R, R), F32)] * 2
        + [pltpu.VMEM(array.shape, array.dtype) for array in kept]
        + [pltpu.SemaphoreType.DMA((4,))],
        compiler_params=PARAMS,
        name="last",
    )(gathered, *kept, rows)


def place():
    at = lax.axis_index("leaf")
    return at // PLANE, at // 8 % 4, at // 2 % 4, at % 2


def device(plane, x, y, core):
    return ((plane * 4 + x) * 4 + y) * 2 + core


def own_tile():
    plane, x, y, core = place()
    return core * 16 + x * 4 + y


def along(axis, k):
    plane, x, y, core = place()
    if axis == 0:
        to = (x + k) % 4
        return device(plane, to, y, core), to
    to = (y + k) % 4
    return device(plane, x, to, core), to


def partner():
    plane, x, y, core = place()
    return device(plane, x, y, 1 - core)


def greet(others):
    barrier = pltpu.get_barrier_semaphore()
    for other in others:
        pl.semaphore_signal(barrier, inc=1, device_id=(other,), device_id_type=pl.DeviceIdType.MESH)


def meet(others):
    pl.semaphore_wait(pltpu.get_barrier_semaphore(), len(others))


def plane_mates():
    return [partner()] + [along(axis, k)[0] for axis in (0, 1) for k in (1, 2, 3)]


def send(source, target, sems, index, to):
    copy = pltpu.make_async_remote_copy(
        src_ref=source,
        dst_ref=target,
        send_sem=sems[0].at[index],
        recv_sem=sems[1].at[index],
        device_id=(to,),
        device_id_type=pl.DeviceIdType.MESH,
    )
    copy.start()
    return copy


class Gather:
    def __init__(self, own_ref, gathered_ref, sems):
        width = gathered_ref.shape[-1]
        half = width // 2 // LANES * LANES
        self.own, self.out, self.sems = own_ref, gathered_ref, sems
        self.halves = ((0, slice(0, half)), (1, slice(half, width)))
        self.width, self.index, self.fence = width, 0, []
        self.first, self.second = [], []

    def send(self, source, target, to):
        self.index += 1
        return send(source, target, self.sems, self.index - 1, to)

    def share(self, block):
        self.fence.append(self.send(block, block, partner()))

    def start(self):
        plane, x, y, core = place()
        for axis, cols in self.halves:
            self.first.append([
                self.send(self.own.at[:, cols], self.out.at[core, x, y, :, cols], along(axis, k)[0])
                for k in (2, 1, 3)
            ])
        whole = slice(0, self.width)
        self.fence.append(self.send(self.own.at[:, whole], self.out.at[core, x, y], partner()))
        self.out[core, x, y] = self.own[:, whole]

    def turn(self):
        plane, x, y, core = place()
        for (axis, cols), copies in zip(self.halves, self.first):
            for copy in copies:
                copy.wait_recv()
            if axis == 0:
                block = self.out.at[core, :, y, :, cols]
            else:
                block = self.out.at[core, x, :, :, cols]
            self.second.append([self.send(block, block, along(1 - axis, k)[0]) for k in (2, 1, 3)])
        for axis, cols in self.halves:
            for k in (1, 2, 3):
                at = (along(axis, k)[1], y) if axis == 0 else (x, along(axis, k)[1])
                self.share(self.out.at[core, at[0], at[1], :, cols])

    def finish(self):
        plane, x, y, core = place()
        for i, k in ((1, 1), (2, 3), (0, 2)):
            for (axis, cols), moved in zip(self.halves, self.second):
                moved[i].wait_recv()
                if axis == 0:
                    self.share(self.out.at[core, :, along(1, 4 - k)[1], :, cols])
                else:
                    self.share(self.out.at[core, along(0, 4 - k)[1], :, :, cols])

    def close(self):
        for copies in self.first + self.second:
            for copy in copies:
                copy.wait_send()
        for copy in self.fence:
            copy.wait()


class Scatter:
    def __init__(self, mine, got, a, b, got_a, got_b, a2, b2, got_a2, got_b2, sems):
        self.mine, self.got, self.a, self.b, self.got_a, self.got_b = mine, got, a, b, got_a, got_b
        self.a2, self.b2, self.got_a2, self.got_b2, self.sems = a2, b2, got_a2, got_b2, sems
        split_at = a.shape[-1]
        self.cols = (slice(0, split_at), slice(split_at, mine.shape[-1]))
        self.all = []

    def spread(self, source, target, axis, index):
        copies = []
        for k in (2, 1, 3):
            to, at = along(axis, k)
            copies.append(send(source.at[at], target.at[k - 1], self.sems, index + k - 1, to))
        self.all += copies
        return copies

    def swap(self, theirs):
        self.swaps = [
            send(theirs.at[:, :, :, c], self.got.at[:, :, :, c], self.sems, i, partner()) for i, c in enumerate(self.cols)
        ]
        self.all += self.swaps

    def first(self):
        self.swaps[0].wait_recv()
        self.a[...] = self.mine[:, :, :, self.cols[0]] + self.got[:, :, :, self.cols[0]]
        self.first_a = self.spread(self.a, self.got_a, 0, 2)
        self.swaps[1].wait_recv()
        for i in range(4):
            self.b[:, i] = self.mine[i, :, :, self.cols[1]] + self.got[i, :, :, self.cols[1]]
        self.first_b = self.spread(self.b, self.got_b, 1, 5)

    def second(self):
        plane, x, y, core = place()
        for copy in self.first_a:
            copy.wait_recv()
        self.a2[...] = (self.a[x] + self.got_a[0]) + (self.got_a[1] + self.got_a[2])
        self.second_a = self.spread(self.a2, self.got_a2, 1, 8)
        for copy in self.first_b:
            copy.wait_recv()
        self.b2[...] = (self.b[y] + self.got_b[0]) + (self.got_b[1] + self.got_b[2])
        self.second_b = self.spread(self.b2, self.got_b2, 0, 11)

    def finish(self, own_ref, offset):
        plane, x, y, core = place()
        cut, end = offset + self.cols[0].stop, offset + self.cols[1].stop
        for copy in self.second_a:
            copy.wait_recv()
        own_ref[:, offset:cut] = (self.a2[y] + self.got_a2[0]) + (self.got_a2[1] + self.got_a2[2])
        for copy in self.second_b:
            copy.wait_recv()
        own_ref[:, cut:end] = (self.b2[x] + self.got_b2[0]) + (self.got_b2[1] + self.got_b2[2])

    def close(self):
        for copy in self.all:
            copy.wait_send()


GATHER_COPIES = 25
HEAD = LEVELS * R + LANES
TAIL = FRONT - HEAD
HEAD_CUT = 5 * LANES
TAIL_CUT = 6 * LANES
TILES = (4, 4, 8)


def scatter_scratch(width, cut):
    rest = width - cut
    shapes = [
        TILES + (width,), TILES + (width,), TILES + (width,), TILES + (cut,), TILES + (rest,), (3, 4, 8, cut),
        (3, 4, 8, rest), (4, 8, cut), (4, 8, rest), (3, 8, cut), (3, 8, rest),
    ]
    return [pltpu.VMEM(shape, F32) for shape in shapes] + [pltpu.SemaphoreType.DMA((14,))] * 2


def sum_kernel(mh_ref, ml_ref, tile_ref, basis_ref, own_ref, gathered_ref, *scratch):
    plane, x, y, core = place()
    mates = plane_mates()
    greet(mates)

    def grams(half, level, target, offset):
        basis = basis_ref[level, pl.ds(pl.multiple_of(half * LANES, LANES), LANES), :]
        part = split(dot(basis, mh_ref[...]) + dot(basis, ml_ref[...]))
        for other in range(level, LEVELS):
            block = dot(part[0], basis_ref[other], NT) + dot(part[1], basis_ref[other], NT)
            target[:, :, :, offset:offset + R] = block.reshape(TILES + (R,))
            offset += R
        if level == 0:
            tile = tile_ref[pl.ds(pl.multiple_of(half * LANES, LANES), LANES), :]
            target[:, :, :, offset:offset + LANES] = tile.reshape(TILES + (LANES,))

    def tail(half, target):
        grams(half, 1, target, 0)
        grams(half, 2, target, 3 * R)
        grams(half, 3, target, 5 * R)

    theirs0, mine0, theirs1, mine1 = scratch[0], scratch[1], scratch[13], scratch[14]
    head_sum = Scatter(*scratch[1:11], scratch[11:13])
    tail_sum = Scatter(*scratch[14:24], scratch[24:26])
    gather = Gather(own_ref, gathered_ref, scratch[26:28])
    grams(1 - core, 0, theirs0, 0)
    meet(mates)
    head_sum.swap(theirs0)
    grams(core, 0, mine0, 0)
    head_sum.first()
    tail(1 - core, theirs1)
    tail_sum.swap(theirs1)
    tail(core, mine1)
    head_sum.second()
    tail_sum.first()
    head_sum.finish(own_ref, 0)
    gather.start()
    gather.turn()
    tail_sum.second()
    gather.finish()
    tail_sum.finish(own_ref, HEAD)
    gather.close()
    head_sum.close()
    tail_sum.close()


def sum_call(mh, ml, tile, bases):
    return pl.pallas_call(
        sum_kernel,
        out_shape=(
            jax.ShapeDtypeStruct((8, FRONT), F32),
            jax.ShapeDtypeStruct((2,) + TILES + (HEAD,), F32),
        ),
        in_specs=vmem(4),
        out_specs=tuple(vmem(2)),
        scratch_shapes=scatter_scratch(HEAD, HEAD_CUT)
        + scatter_scratch(TAIL, TAIL_CUT)
        + [pltpu.SemaphoreType.DMA((GATHER_COPIES,))] * 2,
        compiler_params=pltpu.CompilerParams(
            vmem_limit_bytes=60 * 1024 * 1024, collective_id=0, has_side_effects=True
        ),
        name="sum_gather",
    )(mh, ml, tile, bases)


def pair_kernel(inverse_ref, before_ref, had_ref, own_ref, gathered_ref, h_ref, part_ref, got_ref,
                send_sem, recv_sem, gather_send, gather_recv):
    plane, x, y, core = place()
    mates = plane_mates() + [device(plane + 1 - 2 * (plane % 2), x, y, core)]
    greet(mates)
    eliminate(LEVELS, inverse_ref, before_ref, had_ref, part_ref, h_ref)
    meet(mates)
    swap = send(part_ref, got_ref, (send_sem, recv_sem), 0, mates[-1])
    swap.wait_recv()
    own_ref[...] = part_ref[...] + got_ref[...]
    gather = Gather(own_ref, gathered_ref, (gather_send, gather_recv))
    gather.start()
    gather.turn()
    gather.finish()
    gather.close()
    swap.wait_send()


def pair_call(inverse, gathered, own):
    left = LEVELS - 1
    width = left * R + LANES
    slab = (8, own_width(left))
    return pl.pallas_call(
        pair_kernel,
        out_shape=(
            jax.ShapeDtypeStruct(slab, F32),
            jax.ShapeDtypeStruct((2,) + TILES + (width,), F32),
            jax.ShapeDtypeStruct((R, width), F32),
        ),
        in_specs=vmem(3),
        out_specs=tuple(vmem(3)),
        scratch_shapes=[
            pltpu.VMEM(slab, F32),
            pltpu.VMEM(slab, F32),
            pltpu.SemaphoreType.DMA((1,)),
            pltpu.SemaphoreType.DMA((1,)),
            pltpu.SemaphoreType.DMA((GATHER_COPIES,)),
            pltpu.SemaphoreType.DMA((GATHER_COPIES,)),
        ],
        compiler_params=pltpu.CompilerParams(
            vmem_limit_bytes=60 * 1024 * 1024, collective_id=1, has_side_effects=True
        ),
        name="pair_gather",
    )(inverse, gathered, own)


def node_kernel(inverse_ref, before_ref, had_ref, gathered_ref, h_ref, part_ref, got_ref, both_ref,
                send_sem, recv_sem, gather_send, gather_recv):
    plane, x, y, core = place()
    odd = plane // 2 % 2
    planes = (plane + 2 - 4 * odd, (plane + 6 + 4 * odd) % 8, (plane + 5 - 2 * (plane % 2)) % 8)
    others = [device(other, x, y, core) for other in planes]
    mates = plane_mates() + others
    greet(mates)
    eliminate(LEVELS - 1, inverse_ref, before_ref, had_ref, part_ref, h_ref)
    meet(mates)
    swaps = [send(part_ref, got_ref.at[i], (send_sem, recv_sem), i, others[i]) for i in (2, 0, 1)]
    for swap in swaps:
        swap.wait_recv()
    both_ref[:, 0:NODE] = part_ref[...] + got_ref[0]
    both_ref[:, NODE:] = got_ref[1] + got_ref[2]
    gather = Gather(both_ref, gathered_ref, (gather_send, gather_recv))
    gather.start()
    gather.turn()
    gather.finish()
    gather.close()
    for swap in swaps:
        swap.wait_send()


def node_call(inverse, gathered, own):
    return pl.pallas_call(
        node_kernel,
        out_shape=(
            jax.ShapeDtypeStruct((2,) + TILES + (2 * NODE,), F32),
            jax.ShapeDtypeStruct((R, 2 * R + LANES), F32),
        ),
        in_specs=vmem(3),
        out_specs=tuple(vmem(2)),
        scratch_shapes=[
            pltpu.VMEM((8, NODE), F32),
            pltpu.VMEM((3, 8, NODE), F32),
            pltpu.VMEM((8, 2 * NODE), F32),
            pltpu.SemaphoreType.DMA((3,)),
            pltpu.SemaphoreType.DMA((3,)),
            pltpu.SemaphoreType.DMA((GATHER_COPIES,)),
            pltpu.SemaphoreType.DMA((GATHER_COPIES,)),
        ],
        compiler_params=pltpu.CompilerParams(
            vmem_limit_bytes=60 * 1024 * 1024, collective_id=2, has_side_effects=True
        ),
        name="node_gather",
    )(inverse, gathered, own)


def local(coords, latent, labels, site_order, level_bases):
    mh, ml, tile, inverse, rows = leaf_call(
        coords, latent.reshape(1, M), labels.reshape(1, M), site_order, level_bases
    )
    own, gathered = sum_call(mh, ml, tile, level_bases)
    gathered = gathered.reshape(R, HEAD)
    own, after, h1 = pair_call(inverse_call(gathered), gathered, own)
    gathered = after.reshape(R, 3 * R + LANES)
    both, h2 = node_call(inverse_call(gathered), gathered, own)
    return last_call(both.reshape(R, 2 * NODE), h1, h2, inverse, rows, level_bases).reshape(M)


def solution(mesh):
    placed = (P(None, "leaf"), P("leaf"), P("leaf"), P("leaf", None), P(None, None, "leaf"))
    return jax.shard_map(local, mesh=mesh, in_specs=placed, out_specs=P("leaf"), check_vma=False)
```

```python
import functools
import math

import jax
import jax.numpy as jnp
from jax import lax
from jax.experimental import pallas as pl
from jax.experimental.pallas import tpu as pltpu
from jax.sharding import PartitionSpec as P

F32 = jnp.float32
BF16 = jnp.bfloat16
HIGHEST = lax.Precision.HIGHEST
LENGTH_SCALE = 0.25
VARIANCE = 16.0
ROOT_FIVE = math.sqrt(5.0)
M = 512
R = 256
LEVELS = 4
LANES = 128
PLANE = 32
NN = (((1,), (0,)), ((), ()))
NT = (((1,), (1,)), ((), ()))


def dot(a, b, dims=NN):
    return lax.dot_general(a, b, dims, preferred_element_type=F32)


def dot_f32(a, b, dims=NN):
    return lax.dot_general(a, b, dims, precision=HIGHEST, preferred_element_type=F32)


def split(x):
    hi = x.astype(BF16)
    return hi, (x - hi.astype(F32)).astype(BF16)


def split3(x):
    hi = x.astype(BF16)
    rest = x - hi.astype(F32)
    mid = rest.astype(BF16)
    return hi, mid, (rest - mid.astype(F32)).astype(BF16)


def dot3(a, b, dims=NN):
    return dot(a[0], b[0], dims) + (dot(a[0], b[1], dims) + dot(a[1], b[0], dims))


def packed_rows(v):
    row = lax.broadcasted_iota(jnp.int32, (16, v.shape[1]), 0)
    out = jnp.zeros((16, v.shape[1]), F32)
    for i, part in enumerate(split3(v)):
        out = jnp.where(row == i, part.astype(F32), out)
    return out.astype(BF16)


def row_dot(v, parts, dims=NN):
    rows = packed_rows(v)
    total = dot(rows, parts[0], dims)
    for part in parts[1:]:
        total = total + dot(rows, part, dims)
    return (total[0:1] + total[1:2]) + total[2:3]


def eye(n):
    return jnp.where(
        lax.broadcasted_iota(jnp.int32, (n, n), 0) == lax.broadcasted_iota(jnp.int32, (n, n), 1), 1.0, 0.0
    ).astype(F32)


def newton_polish(s, z):
    residual = eye(s.shape[0]) - dot_f32(s, z)
    return z + dot3(split(z), split(residual))


def newton_rough(matrices, refs):
    n = matrices[0].shape[0]
    sums = [jnp.sum(jnp.abs(s), axis=0, keepdims=True) for s in matrices]
    bound = jnp.max(functools.reduce(jnp.maximum, sums))
    alpha = 2.0 / (1.0 + bound)
    gap = (bound - 1.0) / (bound + 1.0)
    scale = 2.0 / (2.0 - gap * gap)
    for s, ref in zip(matrices, refs):
        first = eye(n) - alpha * s
        parts = split(first)
        ref[0:n] = (alpha * scale) * (eye(n) + first)
        ref[n:] = (1.0 - scale) * eye(n) + scale * dot3(parts, parts)

    def body(gap):
        scale = 2.0 / (2.0 - gap * gap)
        for ref in refs:
            hi, lo = split(ref[...])
            product = dot3((hi, lo), (hi[n:], lo[n:]))
            ref[0:n] = scale * (ref[0:n] + product[0:n])
            ref[n:] = (1.0 - scale) * eye(n) + scale * product[n:]
        return gap * gap / (2.0 - gap * gap)

    lax.while_loop(lambda gap: gap > 2e-3, body, gap * gap / (2.0 - gap * gap))

    def polish(step, carry):
        for s, ref in zip(matrices, refs):
            ref[0:n] = newton_polish(s, ref[0:n])
        return carry

    extra = jnp.where(bound < 256.0, 0, jnp.where(bound < 8192.0, 1, 2))
    lax.fori_loop(0, extra, polish, 0)


def newton_inverses(matrices, refs):
    newton_rough(matrices, refs)
    return [newton_polish(s, ref[0:s.shape[0]]) for s, ref in zip(matrices, refs)]


def newton_inverse(s, ref):
    return newton_inverses([s], [ref])[0]


def leaf_kernel(coord_ref, latent_ref, label_ref, order_ref, basis_ref, mh_ref, ml_ref, tile_ref,
                inverse_ref, rows_ref, a_ref, z_ref):
    picked = lax.broadcasted_iota(jnp.int32, (M, M), 0) == order_ref[...]
    one_hot = jnp.where(picked, 1.0, 0.0).astype(BF16)
    hi, mid, lo = split3(latent_ref[...])
    row = lax.broadcasted_iota(jnp.int32, (16, M), 0)
    packed = jnp.where(row == 0, hi.astype(F32), 0.0)
    packed = jnp.where(row == 1, mid.astype(F32), packed)
    packed = jnp.where(row == 2, lo.astype(F32), packed)
    packed = jnp.where(row == 3, label_ref[...].astype(F32), packed)
    got = dot(packed.astype(BF16), one_hot)
    tree_latent = (got[0:1] + got[1:2]) + got[2:3]
    tree_target = got[3:4]
    probability = 1.0 / (1.0 + jnp.exp(-tree_latent))
    weight = probability * (1.0 - probability)
    root_weight = jnp.sqrt(weight)
    right_side = root_weight * (weight * tree_latent + tree_target - probability)

    def column(value, i):
        return jnp.broadcast_to(value[:, i * LANES:(i + 1) * LANES], (LANES, LANES)).T

    axes = [coord_ref[k:k + 1, :] for k in range(3)]
    columns = []
    for i in range(4):
        cols = [column(axis, i) for axis in axes]
        weight_col = column(root_weight, i)
        columns.append(weight_col)
        for j in range(i, 4):
            span = slice(j * LANES, (j + 1) * LANES)
            total = None
            for axis, col in zip(axes, cols):
                difference = col - axis[:, span]
                total = difference * difference if total is None else total + difference * difference
            scaled = (ROOT_FIVE / LENGTH_SCALE) * jnp.sqrt(total)
            kernel = VARIANCE * (1.0 + scaled + scaled * scaled / 3.0) * jnp.exp(-scaled)
            block = weight_col * kernel * root_weight[:, span]
            if i == j:
                block = block + eye(LANES)
            a_ref[i * LANES:(i + 1) * LANES, span] = block
            if i != j:
                a_ref[span, i * LANES:(i + 1) * LANES] = block.T

    top, bottom = slice(0, R), slice(R, M)
    x = newton_inverse(a_ref[top, top], z_ref)
    u = dot_f32(x, a_ref[top, bottom])
    v = dot_f32(a_ref[bottom, top], x)
    schur = newton_inverse(a_ref[bottom, bottom] - dot_f32(v, a_ref[top, bottom]), z_ref)
    schur_parts, v_parts = split(schur), split(v)
    us = dot3(split(u), schur_parts)
    inverse_ref[bottom, bottom] = schur
    inverse_ref[top, bottom] = -us
    inverse_ref[bottom, top] = -dot3(schur_parts, v_parts)
    inverse_ref[top, top] = x + dot3(split(us), v_parts)

    for i in range(4):
        for j in range(4):
            rows, span = slice(i * LANES, (i + 1) * LANES), slice(j * LANES, (j + 1) * LANES)
            hi, lo = split(columns[i] * inverse_ref[rows, span] * root_weight[:, span])
            mh_ref[rows, span] = hi
            ml_ref[rows, span] = lo
    solved = row_dot(right_side, split3(inverse_ref[...]))
    weighted = [jnp.broadcast_to(part.astype(F32), (LANES, M)).astype(BF16) for part in split3(root_weight * solved)]
    bases = basis_ref[...].reshape(LEVELS * R, M)
    projections = dot(bases, weighted[0], NT) + (dot(bases, weighted[1], NT) + dot(bases, weighted[2], NT))
    lane = lax.broadcasted_iota(jnp.int32, (R, LANES), 1)
    tile = jnp.zeros((R, LANES), F32)
    for level in range(LEVELS):
        tile = jnp.where(lane == level, projections[level * R:(level + 1) * R], tile)
    tile_ref[...] = tile
    row = lax.broadcasted_iota(jnp.int32, (8, M), 0)
    rows_ref[...] = jnp.where(row == 0, root_weight, right_side)


def vmem(n):
    return [pl.BlockSpec(memory_space=pltpu.VMEM)] * n


FRONT = LEVELS * R + LANES + 6 * R
PARAMS = pltpu.CompilerParams(vmem_limit_bytes=60 * 1024 * 1024)


def leaf_call(coords, latent, labels, order, bases):
    return pl.pallas_call(
        leaf_kernel,
        out_shape=(
            jax.ShapeDtypeStruct((M, M), BF16),
            jax.ShapeDtypeStruct((M, M), BF16),
            jax.ShapeDtypeStruct((R, LANES), F32),
            jax.ShapeDtypeStruct((M, M), F32),
            jax.ShapeDtypeStruct((8, M), F32),
        ),
        in_specs=vmem(5),
        out_specs=tuple(vmem(5)),
        scratch_shapes=[pltpu.VMEM((M, M), F32), pltpu.VMEM((2 * R, R), F32)],
        compiler_params=PARAMS,
        name="leaf",
    )(coords, latent, labels, order, bases)


def inverse_kernel(gathered_ref, inverse_ref, z_ref):
    newton_rough([gathered_ref[...] + eye(R)], [z_ref])
    inverse_ref[...] = z_ref[0:R]


def inverse_call(gathered):
    return pl.pallas_call(
        inverse_kernel,
        grid=(1,),
        out_shape=jax.ShapeDtypeStruct((R, R), F32),
        in_specs=[pl.BlockSpec((R, R), lambda i: (0, 0))],
        out_specs=pl.BlockSpec((R, R), lambda i: (0, 0)),
        scratch_shapes=[pltpu.VMEM((2 * R, R), F32)],
        compiler_params=PARAMS,
        name="inverse",
    )(gathered)


def eliminate(left, inverse_ref, gathered_ref, own_ref, next_ref, h_ref):
    inverse = newton_polish(gathered_ref[:, 0:R] + eye(R), inverse_ref[...])
    h = dot3(split(inverse), split(gathered_ref[:, R:left * R + LANES]))
    h_ref[...] = h
    width = (left - 1) * R
    h_parts = split(h)
    mine = own_tile() * 8
    wanted = lax.broadcasted_iota(jnp.int32, (8, R), 1) == lax.broadcasted_iota(jnp.int32, (8, R), 0) + mine
    one_hot = jnp.where(wanted, 1.0, 0.0).astype(BF16)
    lane = lax.broadcasted_iota(jnp.int32, (8, LANES), 1)
    tile = own_ref[:, left * R:left * R + LANES]
    source, target = left * R + LANES, 0
    for k in range(1, left):
        block = split(gathered_ref[:, k * R:(k + 1) * R])
        rows = dot(one_hot, block[0], NT) + dot(one_hot, block[1], NT)
        drop = dot3(split(rows), h_parts)
        span = (left - k) * R
        next_ref[:, target:target + span] = own_ref[:, source:source + span] - drop[:, (k - 1) * R:width]
        source, target = source + span, target + span
        if k == 1:
            target += LANES
        at = LEVELS - left
        tile = tile - jnp.where(lane == at + k, drop[:, width + at:width + at + 1], 0.0)
    next_ref[:, width:width + LANES] = tile


def own_width(left):
    return LANES + R * (left * (left + 1) // 2)


NODE = own_width(2)
BOTH_B = 2 * R + LANES
BOTH = 5 * R + LANES


def last_kernel(gathered_ref, h1_any, h2_any, inverse_any, basis_any, rows_ref, out_ref,
                za_ref, zb_ref, h1_ref, h2_ref, inverse_ref, basis_ref, sems):
    copies = [
        pltpu.make_async_copy(source, target, sems.at[i])
        for i, (source, target) in enumerate(
            ((h2_any, h2_ref), (h1_any, h1_ref), (inverse_any, inverse_ref), (basis_any, basis_ref))
        )
    ]
    for copy in copies:
        copy.start()
    starts = (0, BOTH_B)
    inverses = newton_inverses([gathered_ref[:, at:at + R] + eye(R) for at in starts], [za_ref, zb_ref])
    tile = gathered_ref[:, 2 * R:BOTH_B]
    tile_parts = split(tile)
    core = eye(R) + gathered_ref[:, BOTH_B + 2 * R:]
    right = tile.T[3:4, :]
    kept = []
    for at, inverse, lane in zip(starts, inverses, (2, 1)):
        coupling = gathered_ref[:, at + R:at + 2 * R]
        inverse_parts, turned = split(inverse), split(coupling.T)
        h = dot3(inverse_parts, split(coupling))
        tile_h = dot3(inverse_parts, tile_parts)
        core = core - dot3(turned, split(h))
        right = right - dot3(turned, split(tile_h)).T[lane:lane + 1, :]
        kept.append((h, tile_h))
    z = row_dot(right, split(newton_inverse(core, za_ref)))
    for copy in copies:
        copy.wait()
    h_all = (h1_ref[...], h2_ref[...], kept[0][0])
    tiles = (h1_ref[:, 3 * R:], h2_ref[:, 2 * R:], kept[0][1])
    rows = [part.T[i:i + 1, :] for i, part in enumerate(tiles)] + [z]
    total = jnp.zeros((16, M), F32)
    for level in reversed(range(LEVELS)):
        z = packed_rows(rows[level])
        total = total + dot(z, basis_ref[level])
        for i in range(level):
            at = (level - i - 1) * R
            parts = split(h_all[i][:, at:at + R])
            drop = dot(z, parts[0], NT) + dot(z, parts[1], NT)
            rows[i] = rows[i] - ((drop[0:1] + drop[1:2]) + drop[2:3])
    spread = (total[0:1] + total[1:2]) + total[2:3]
    out_ref[...] = row_dot(rows_ref[1:2] - rows_ref[0:1] * spread, split3(inverse_ref[...]))


def last_call(gathered, h1, h2, inverse, rows, bases):
    kept = (h1, h2, inverse, bases)
    return pl.pallas_call(
        last_kernel,
        out_shape=jax.ShapeDtypeStruct((1, M), F32),
        in_specs=vmem(1) + [pl.BlockSpec(memory_space=pl.ANY)] * 4 + vmem(1),
        out_specs=vmem(1)[0],
        scratch_shapes=[pltpu.VMEM((2 * R, R), F32)] * 2
        + [pltpu.VMEM(array.shape, array.dtype) for array in kept]
        + [pltpu.SemaphoreType.DMA((4,))],
        compiler_params=PARAMS,
        name="last",
    )(gathered, *kept, rows)


def place():
    at = lax.axis_index("leaf")
    return at // PLANE, at // 8 % 4, at // 2 % 4, at % 2


def device(plane, x, y, core):
    return ((plane * 4 + x) * 4 + y) * 2 + core


def own_tile():
    plane, x, y, core = place()
    return core * 16 + x * 4 + y


def along(axis, k):
    plane, x, y, core = place()
    if axis == 0:
        to = (x + k) % 4
        return device(plane, to, y, core), to
    to = (y + k) % 4
    return device(plane, x, to, core), to


def partner():
    plane, x, y, core = place()
    return device(plane, x, y, 1 - core)


def greet(others):
    barrier = pltpu.get_barrier_semaphore()
    for other in others:
        pl.semaphore_signal(barrier, inc=1, device_id=(other,), device_id_type=pl.DeviceIdType.MESH)


def meet(others):
    pl.semaphore_wait(pltpu.get_barrier_semaphore(), len(others))


def plane_mates():
    return [partner()] + [along(axis, k)[0] for axis in (0, 1) for k in (1, 2, 3)]


def send(source, target, sems, index, to):
    copy = pltpu.make_async_remote_copy(
        src_ref=source,
        dst_ref=target,
        send_sem=sems[0].at[index],
        recv_sem=sems[1].at[index],
        device_id=(to,),
        device_id_type=pl.DeviceIdType.MESH,
    )
    copy.start()
    return copy


class Gather:
    def __init__(self, own_ref, gathered_ref, sems):
        width = gathered_ref.shape[-1]
        half = width // 2 // LANES * LANES
        self.own, self.out, self.sems = own_ref, gathered_ref, sems
        self.halves = ((0, slice(0, half)), (1, slice(half, width)))
        self.width, self.index, self.fence = width, 0, []
        self.first, self.second = [], ({}, {})

    def send(self, source, target, to):
        self.index += 1
        return send(source, target, self.sems, self.index - 1, to)

    def share(self, block):
        self.fence.append(self.send(block, block, partner()))

    def tile(self, axis, back):
        plane, x, y, core = place()
        at = along(axis, 4 - back)[1]
        return (core, at, y) if axis == 0 else (core, x, at)

    def start(self):
        plane, x, y, core = place()
        for half, (axis, cols) in enumerate(self.halves):
            block = self.own.at[:, cols]
            target = self.out.at[core, x, y, :, cols]
            self.first.append({k: self.send(block, target, along(axis, k)[0]) for k in (2, 1, 3)})
            self.second[half][0] = {k: self.send(block, target, along(1 - axis, k)[0]) for k in (2, 1, 3)}
        whole = slice(0, self.width)
        self.fence.append(self.send(self.own.at[:, whole], self.out.at[core, x, y], partner()))
        self.out[core, x, y] = self.own[:, whole]

    def turn(self):
        for back in (1, 3, 2):
            for half, (axis, cols) in enumerate(self.halves):
                self.first[half][back].wait_recv()
                core, at_x, at_y = self.tile(axis, back)
                block = self.out.at[core, at_x, at_y, :, cols]
                self.second[half][back] = {k: self.send(block, block, along(1 - axis, k)[0]) for k in (2, 1, 3)}
                self.share(block)

    def finish(self):
        plane, x, y, core = place()
        for k in (1, 3, 2):
            for half, (axis, cols) in enumerate(self.halves):
                for back in (0, 1, 3, 2):
                    self.second[half][back][k].wait_recv()
                if axis == 0:
                    self.share(self.out.at[core, :, along(1, 4 - k)[1], :, cols])
                else:
                    self.share(self.out.at[core, along(0, 4 - k)[1], :, :, cols])

    def close(self):
        for half in range(2):
            for copies in [self.first[half], *self.second[half].values()]:
                for copy in copies.values():
                    copy.wait_send()
        for copy in self.fence:
            copy.wait()


class Scatter:
    def __init__(self, mine, got, a, b, got_a, got_b, a2, b2, got_a2, got_b2, sems):
        self.mine, self.got, self.a, self.b, self.got_a, self.got_b = mine, got, a, b, got_a, got_b
        self.a2, self.b2, self.got_a2, self.got_b2, self.sems = a2, b2, got_a2, got_b2, sems
        split_at = a.shape[-1]
        self.cols = (slice(0, split_at), slice(split_at, mine.shape[-1]))
        self.all = []

    def spread(self, source, target, axis, index):
        copies = []
        for k in (2, 1, 3):
            to, at = along(axis, k)
            copies.append(send(source.at[at], target.at[k - 1], self.sems, index + k - 1, to))
        self.all += copies
        return copies

    def swap(self, theirs):
        self.swaps = [
            send(theirs.at[:, :, :, c], self.got.at[:, :, :, c], self.sems, i, partner()) for i, c in enumerate(self.cols)
        ]
        self.all += self.swaps

    def first(self):
        self.swaps[0].wait_recv()
        self.a[...] = self.mine[:, :, :, self.cols[0]] + self.got[:, :, :, self.cols[0]]
        self.first_a = self.spread(self.a, self.got_a, 0, 2)
        self.swaps[1].wait_recv()
        for i in range(4):
            self.b[:, i] = self.mine[i, :, :, self.cols[1]] + self.got[i, :, :, self.cols[1]]
        self.first_b = self.spread(self.b, self.got_b, 1, 5)

    def second(self):
        plane, x, y, core = place()
        for copy in self.first_a:
            copy.wait_recv()
        self.a2[...] = (self.a[x] + self.got_a[0]) + (self.got_a[1] + self.got_a[2])
        self.second_a = self.spread(self.a2, self.got_a2, 1, 8)
        for copy in self.first_b:
            copy.wait_recv()
        self.b2[...] = (self.b[y] + self.got_b[0]) + (self.got_b[1] + self.got_b[2])
        self.second_b = self.spread(self.b2, self.got_b2, 0, 11)

    def finish(self, own_ref, offset):
        plane, x, y, core = place()
        cut, end = offset + self.cols[0].stop, offset + self.cols[1].stop
        for copy in self.second_a:
            copy.wait_recv()
        own_ref[:, offset:cut] = (self.a2[y] + self.got_a2[0]) + (self.got_a2[1] + self.got_a2[2])
        for copy in self.second_b:
            copy.wait_recv()
        own_ref[:, cut:end] = (self.b2[x] + self.got_b2[0]) + (self.got_b2[1] + self.got_b2[2])

    def close(self):
        for copy in self.all:
            copy.wait_send()


GATHER_COPIES = 43
HEAD = LEVELS * R + LANES
TAIL = FRONT - HEAD
HEAD_CUT = 5 * LANES
TAIL_CUT = 6 * LANES
TILES = (4, 4, 8)


def scatter_scratch(width, cut):
    rest = width - cut
    shapes = [
        TILES + (width,), TILES + (width,), TILES + (width,), TILES + (cut,), TILES + (rest,), (3, 4, 8, cut),
        (3, 4, 8, rest), (4, 8, cut), (4, 8, rest), (3, 8, cut), (3, 8, rest),
    ]
    return [pltpu.VMEM(shape, F32) for shape in shapes] + [pltpu.SemaphoreType.DMA((14,))] * 2


def sum_kernel(mh_ref, ml_ref, tile_ref, basis_ref, own_ref, gathered_ref, *scratch):
    plane, x, y, core = place()
    mates = plane_mates()
    greet(mates)

    def grams(half, level, target, offset):
        basis = basis_ref[level, pl.ds(pl.multiple_of(half * LANES, LANES), LANES), :]
        part = split(dot(basis, mh_ref[...]) + dot(basis, ml_ref[...]))
        for other in range(level, LEVELS):
            block = dot(part[0], basis_ref[other], NT) + dot(part[1], basis_ref[other], NT)
            target[:, :, :, offset:offset + R] = block.reshape(TILES + (R,))
            offset += R
        if level == 0:
            tile = tile_ref[pl.ds(pl.multiple_of(half * LANES, LANES), LANES), :]
            target[:, :, :, offset:offset + LANES] = tile.reshape(TILES + (LANES,))

    def tail(half, target):
        grams(half, 1, target, 0)
        grams(half, 2, target, 3 * R)
        grams(half, 3, target, 5 * R)

    theirs0, mine0, theirs1, mine1 = scratch[0], scratch[1], scratch[13], scratch[14]
    head_sum = Scatter(*scratch[1:11], scratch[11:13])
    tail_sum = Scatter(*scratch[14:24], scratch[24:26])
    gather = Gather(own_ref, gathered_ref, scratch[26:28])
    grams(1 - core, 0, theirs0, 0)
    meet(mates)
    head_sum.swap(theirs0)
    grams(core, 0, mine0, 0)
    head_sum.first()
    tail(1 - core, theirs1)
    tail_sum.swap(theirs1)
    tail(core, mine1)
    head_sum.second()
    tail_sum.first()
    head_sum.finish(own_ref, 0)
    gather.start()
    gather.turn()
    tail_sum.second()
    gather.finish()
    tail_sum.finish(own_ref, HEAD)
    gather.close()
    head_sum.close()
    tail_sum.close()


def sum_call(mh, ml, tile, bases):
    return pl.pallas_call(
        sum_kernel,
        out_shape=(
            jax.ShapeDtypeStruct((8, FRONT), F32),
            jax.ShapeDtypeStruct((2,) + TILES + (HEAD,), F32),
        ),
        in_specs=vmem(4),
        out_specs=tuple(vmem(2)),
        scratch_shapes=scatter_scratch(HEAD, HEAD_CUT)
        + scatter_scratch(TAIL, TAIL_CUT)
        + [pltpu.SemaphoreType.DMA((GATHER_COPIES,))] * 2,
        compiler_params=pltpu.CompilerParams(
            vmem_limit_bytes=60 * 1024 * 1024, collective_id=0, has_side_effects=True
        ),
        name="sum_gather",
    )(mh, ml, tile, bases)


def pair_kernel(inverse_ref, before_ref, had_ref, own_ref, gathered_ref, h_ref, part_ref, got_ref,
                send_sem, recv_sem, gather_send, gather_recv):
    plane, x, y, core = place()
    mates = plane_mates() + [device(plane + 1 - 2 * (plane % 2), x, y, core)]
    greet(mates)
    eliminate(LEVELS, inverse_ref, before_ref, had_ref, part_ref, h_ref)
    meet(mates)
    swap = send(part_ref, got_ref, (send_sem, recv_sem), 0, mates[-1])
    swap.wait_recv()
    own_ref[...] = part_ref[...] + got_ref[...]
    gather = Gather(own_ref, gathered_ref, (gather_send, gather_recv))
    gather.start()
    gather.turn()
    gather.finish()
    gather.close()
    swap.wait_send()


def pair_call(inverse, gathered, own):
    left = LEVELS - 1
    width = left * R + LANES
    slab = (8, own_width(left))
    return pl.pallas_call(
        pair_kernel,
        out_shape=(
            jax.ShapeDtypeStruct(slab, F32),
            jax.ShapeDtypeStruct((2,) + TILES + (width,), F32),
            jax.ShapeDtypeStruct((R, width), F32),
        ),
        in_specs=vmem(3),
        out_specs=tuple(vmem(3)),
        scratch_shapes=[
            pltpu.VMEM(slab, F32),
            pltpu.VMEM(slab, F32),
            pltpu.SemaphoreType.DMA((1,)),
            pltpu.SemaphoreType.DMA((1,)),
            pltpu.SemaphoreType.DMA((GATHER_COPIES,)),
            pltpu.SemaphoreType.DMA((GATHER_COPIES,)),
        ],
        compiler_params=pltpu.CompilerParams(
            vmem_limit_bytes=60 * 1024 * 1024, collective_id=1, has_side_effects=True
        ),
        name="pair_gather",
    )(inverse, gathered, own)


def node_kernel(inverse_ref, before_ref, had_ref, gathered_ref, h_ref, part_ref, got_ref, both_ref,
                send_sem, recv_sem, gather_send, gather_recv):
    plane, x, y, core = place()
    odd = plane // 2 % 2
    planes = (plane + 2 - 4 * odd, (plane + 6 + 4 * odd) % 8, (plane + 5 - 2 * (plane % 2)) % 8)
    others = [device(other, x, y, core) for other in planes]
    mates = plane_mates() + others
    greet(mates)
    eliminate(LEVELS - 1, inverse_ref, before_ref, had_ref, part_ref, h_ref)
    meet(mates)
    swaps = [send(part_ref, got_ref.at[i], (send_sem, recv_sem), i, others[i]) for i in (2, 0, 1)]
    for swap in swaps:
        swap.wait_recv()
    mine = part_ref[...] + got_ref[0]
    other = got_ref[1] + got_ref[2]
    lane = lax.broadcasted_iota(jnp.int32, (8, LANES), 1)
    tile, other_tile = mine[:, 2 * R:BOTH_B], other[:, 2 * R:BOTH_B]
    tile = jnp.where(lane == 1, other_tile[:, 2:3], jnp.where(lane == 3, tile + other_tile, tile))
    both_ref[:, 0:2 * R] = mine[:, 0:2 * R]
    both_ref[:, 2 * R:BOTH_B] = tile
    both_ref[:, BOTH_B:BOTH_B + 2 * R] = other[:, 0:2 * R]
    both_ref[:, BOTH_B + 2 * R:] = mine[:, BOTH_B:] + other[:, BOTH_B:]
    gather = Gather(both_ref, gathered_ref, (gather_send, gather_recv))
    gather.start()
    gather.turn()
    gather.finish()
    gather.close()
    for swap in swaps:
        swap.wait_send()


def node_call(inverse, gathered, own):
    return pl.pallas_call(
        node_kernel,
        out_shape=(
            jax.ShapeDtypeStruct((2,) + TILES + (BOTH,), F32),
            jax.ShapeDtypeStruct((R, 2 * R + LANES), F32),
        ),
        in_specs=vmem(3),
        out_specs=tuple(vmem(2)),
        scratch_shapes=[
            pltpu.VMEM((8, NODE), F32),
            pltpu.VMEM((3, 8, NODE), F32),
            pltpu.VMEM((8, BOTH), F32),
            pltpu.SemaphoreType.DMA((3,)),
            pltpu.SemaphoreType.DMA((3,)),
            pltpu.SemaphoreType.DMA((GATHER_COPIES,)),
            pltpu.SemaphoreType.DMA((GATHER_COPIES,)),
        ],
        compiler_params=pltpu.CompilerParams(
            vmem_limit_bytes=60 * 1024 * 1024, collective_id=2, has_side_effects=True
        ),
        name="node_gather",
    )(inverse, gathered, own)


def local(coords, latent, labels, site_order, level_bases):
    mh, ml, tile, inverse, rows = leaf_call(
        coords, latent.reshape(1, M), labels.reshape(1, M), site_order, level_bases
    )
    own, gathered = sum_call(mh, ml, tile, level_bases)
    gathered = gathered.reshape(R, HEAD)
    own, after, h1 = pair_call(inverse_call(gathered), gathered, own)
    gathered = after.reshape(R, 3 * R + LANES)
    both, h2 = node_call(inverse_call(gathered), gathered, own)
    return last_call(both.reshape(R, BOTH), h1, h2, inverse, rows, level_bases).reshape(M)


def solution(mesh):
    placed = (P(None, "leaf"), P("leaf"), P("leaf"), P("leaf", None), P(None, None, "leaf"))
    return jax.shard_map(local, mesh=mesh, in_specs=placed, out_specs=P("leaf"), check_vma=False)
```

```python
import functools
import math

import jax
import jax.numpy as jnp
from jax import lax
from jax.experimental import pallas as pl
from jax.experimental.pallas import tpu as pltpu
from jax.sharding import PartitionSpec as P

F32 = jnp.float32
BF16 = jnp.bfloat16
HIGHEST = lax.Precision.HIGHEST
LENGTH_SCALE = 0.25
VARIANCE = 16.0
ROOT_FIVE = math.sqrt(5.0)
M = 512
R = 256
LEVELS = 4
LANES = 128
PLANE = 32
NN = (((1,), (0,)), ((), ()))
NT = (((1,), (1,)), ((), ()))


def dot(a, b, dims=NN):
    return lax.dot_general(a, b, dims, preferred_element_type=F32)


def dot_f32(a, b, dims=NN):
    return lax.dot_general(a, b, dims, precision=HIGHEST, preferred_element_type=F32)


def split(x):
    hi = x.astype(BF16)
    return hi, (x - hi.astype(F32)).astype(BF16)


def split3(x):
    hi = x.astype(BF16)
    rest = x - hi.astype(F32)
    mid = rest.astype(BF16)
    return hi, mid, (rest - mid.astype(F32)).astype(BF16)


def dot3(a, b, dims=NN):
    return dot(a[0], b[0], dims) + (dot(a[0], b[1], dims) + dot(a[1], b[0], dims))


def packed_rows(v):
    row = lax.broadcasted_iota(jnp.int32, (16, v.shape[1]), 0)
    out = jnp.zeros((16, v.shape[1]), F32)
    for i, part in enumerate(split3(v)):
        out = jnp.where(row == i, part.astype(F32), out)
    return out.astype(BF16)


def row_dot(v, parts, dims=NN):
    rows = packed_rows(v)
    total = dot(rows, parts[0], dims)
    for part in parts[1:]:
        total = total + dot(rows, part, dims)
    return (total[0:1] + total[1:2]) + total[2:3]


def eye(n):
    return jnp.where(
        lax.broadcasted_iota(jnp.int32, (n, n), 0) == lax.broadcasted_iota(jnp.int32, (n, n), 1), 1.0, 0.0
    ).astype(F32)


def newton_polish(s, z):
    residual = eye(s.shape[0]) - dot_f32(s, z)
    return z + dot3(split(z), split(residual))


def newton_rough(matrices, refs):
    n = matrices[0].shape[0]
    sums = [jnp.sum(jnp.abs(s), axis=0, keepdims=True) for s in matrices]
    bound = jnp.max(functools.reduce(jnp.maximum, sums))
    alpha = 2.0 / (1.0 + bound)
    gap = (bound - 1.0) / (bound + 1.0)
    scale = 2.0 / (2.0 - gap * gap)
    for s, ref in zip(matrices, refs):
        first = eye(n) - alpha * s
        parts = split(first)
        ref[0:n] = (alpha * scale) * (eye(n) + first)
        ref[n:] = (1.0 - scale) * eye(n) + scale * dot3(parts, parts)

    def body(gap):
        scale = 2.0 / (2.0 - gap * gap)
        for ref in refs:
            hi, lo = split(ref[...])
            product = dot3((hi, lo), (hi[n:], lo[n:]))
            ref[0:n] = scale * (ref[0:n] + product[0:n])
            ref[n:] = (1.0 - scale) * eye(n) + scale * product[n:]
        return gap * gap / (2.0 - gap * gap)

    lax.while_loop(lambda gap: gap > 2e-3, body, gap * gap / (2.0 - gap * gap))

    def polish(step, carry):
        for s, ref in zip(matrices, refs):
            ref[0:n] = newton_polish(s, ref[0:n])
        return carry

    extra = jnp.where(bound < 256.0, 0, jnp.where(bound < 8192.0, 1, 2))
    lax.fori_loop(0, extra, polish, 0)


def newton_inverses(matrices, refs):
    newton_rough(matrices, refs)
    return [newton_polish(s, ref[0:s.shape[0]]) for s, ref in zip(matrices, refs)]


def newton_inverse(s, ref):
    return newton_inverses([s], [ref])[0]


def leaf_kernel(sites_ref, mh_ref, ml_ref, inverse_ref, rows_ref, a_ref, z_ref):
    picked = lax.broadcasted_iota(jnp.int32, (M, M), 0) == sites_ref[5:6].astype(jnp.int32)
    one_hot = jnp.where(picked, 1.0, 0.0).astype(BF16)
    hi, mid, lo = split3(sites_ref[3:4])
    row = lax.broadcasted_iota(jnp.int32, (16, M), 0)
    packed = jnp.where(row == 0, hi.astype(F32), 0.0)
    packed = jnp.where(row == 1, mid.astype(F32), packed)
    packed = jnp.where(row == 2, lo.astype(F32), packed)
    packed = jnp.where(row == 3, sites_ref[4:5], packed)
    got = dot(packed.astype(BF16), one_hot)
    tree_latent = (got[0:1] + got[1:2]) + got[2:3]
    tree_target = got[3:4]
    probability = 1.0 / (1.0 + jnp.exp(-tree_latent))
    weight = probability * (1.0 - probability)
    root_weight = jnp.sqrt(weight)
    right_side = root_weight * (weight * tree_latent + tree_target - probability)

    def column(value, i):
        return jnp.broadcast_to(value[:, i * LANES:(i + 1) * LANES], (LANES, LANES)).T

    axes = [sites_ref[k:k + 1, :] for k in range(3)]
    columns = []
    for i in range(4):
        cols = [column(axis, i) for axis in axes]
        weight_col = column(root_weight, i)
        columns.append(weight_col)
        for j in range(i, 4):
            span = slice(j * LANES, (j + 1) * LANES)
            total = None
            for axis, col in zip(axes, cols):
                difference = col - axis[:, span]
                total = difference * difference if total is None else total + difference * difference
            scaled = (ROOT_FIVE / LENGTH_SCALE) * jnp.sqrt(total)
            kernel = VARIANCE * (1.0 + scaled + scaled * scaled / 3.0) * jnp.exp(-scaled)
            block = weight_col * kernel * root_weight[:, span]
            if i == j:
                block = block + eye(LANES)
            a_ref[i * LANES:(i + 1) * LANES, span] = block
            if i != j:
                a_ref[span, i * LANES:(i + 1) * LANES] = block.T

    top, bottom = slice(0, R), slice(R, M)
    x = newton_inverse(a_ref[top, top], z_ref)
    u = dot_f32(x, a_ref[top, bottom])
    v = dot_f32(a_ref[bottom, top], x)
    schur = newton_inverse(a_ref[bottom, bottom] - dot_f32(v, a_ref[top, bottom]), z_ref)
    schur_parts, v_parts = split(schur), split(v)
    us = dot3(split(u), schur_parts)
    inverse_ref[bottom, bottom] = schur
    inverse_ref[top, bottom] = -us
    inverse_ref[bottom, top] = -dot3(schur_parts, v_parts)
    inverse_ref[top, top] = x + dot3(split(us), v_parts)

    for i in range(4):
        for j in range(4):
            rows, span = slice(i * LANES, (i + 1) * LANES), slice(j * LANES, (j + 1) * LANES)
            hi, lo = split(columns[i] * inverse_ref[rows, span] * root_weight[:, span])
            mh_ref[rows, span] = hi
            ml_ref[rows, span] = lo
    solved = row_dot(right_side, split3(inverse_ref[...]))
    row = lax.broadcasted_iota(jnp.int32, (8, M), 0)
    rows_ref[...] = jnp.where(row == 0, root_weight, jnp.where(row == 1, right_side, root_weight * solved))


def vmem(n):
    return [pl.BlockSpec(memory_space=pltpu.VMEM)] * n


FRONT = LEVELS * R + LANES + 6 * R
PARAMS = pltpu.CompilerParams(vmem_limit_bytes=20 * 1024 * 1024)


def leaf_call(sites):
    return pl.pallas_call(
        leaf_kernel,
        out_shape=(
            jax.ShapeDtypeStruct((M, M), BF16),
            jax.ShapeDtypeStruct((M, M), BF16),
            jax.ShapeDtypeStruct((M, M), F32),
            jax.ShapeDtypeStruct((8, M), F32),
        ),
        in_specs=vmem(1),
        out_specs=tuple(vmem(4)),
        scratch_shapes=[pltpu.VMEM((M, M), F32), pltpu.VMEM((2 * R, R), F32)],
        compiler_params=PARAMS,
        name="leaf",
    )(sites)


def inverse_kernel(gathered_ref, inverse_ref, z_ref):
    newton_rough([gathered_ref[...] + eye(R)], [z_ref])
    inverse_ref[...] = z_ref[0:R]


def inverse_call(gathered):
    return pl.pallas_call(
        inverse_kernel,
        grid=(1,),
        out_shape=jax.ShapeDtypeStruct((R, R), F32),
        in_specs=[pl.BlockSpec((R, R), lambda i: (0, 0))],
        out_specs=pl.BlockSpec((R, R), lambda i: (0, 0)),
        scratch_shapes=[pltpu.VMEM((2 * R, R), F32)],
        compiler_params=PARAMS,
        name="inverse",
    )(gathered)


def eliminate(left, inverse_ref, gathered_ref, own_ref, next_ref, h_ref):
    inverse = newton_polish(gathered_ref[:, 0:R] + eye(R), inverse_ref[...])
    h = dot3(split(inverse), split(gathered_ref[:, R:left * R + LANES]))
    h_ref[...] = h
    width = (left - 1) * R
    h_parts = split(h)
    mine = own_tile() * 8
    wanted = lax.broadcasted_iota(jnp.int32, (8, R), 1) == lax.broadcasted_iota(jnp.int32, (8, R), 0) + mine
    one_hot = jnp.where(wanted, 1.0, 0.0).astype(BF16)
    lane = lax.broadcasted_iota(jnp.int32, (8, LANES), 1)
    tile = own_ref[:, left * R:left * R + LANES]
    source, target = left * R + LANES, 0
    for k in range(1, left):
        block = split(gathered_ref[:, k * R:(k + 1) * R])
        rows = dot(one_hot, block[0], NT) + dot(one_hot, block[1], NT)
        drop = dot3(split(rows), h_parts)
        span = (left - k) * R
        next_ref[:, target:target + span] = own_ref[:, source:source + span] - drop[:, (k - 1) * R:width]
        source, target = source + span, target + span
        if k == 1:
            target += LANES
        at = LEVELS - left
        tile = tile - jnp.where(lane == at + k, drop[:, width + at:width + at + 1], 0.0)
    next_ref[:, width:width + LANES] = tile


def own_width(left):
    return LANES + R * (left * (left + 1) // 2)


NODE = own_width(2)
BOTH_B = 2 * R + LANES
BOTH = 5 * R + LANES


def last_kernel(gathered_ref, h1_ref, h2_ref, inverse_ref, basis_ref, rows_ref, out_ref, za_ref, zb_ref):
    starts = (0, BOTH_B)
    inverses = newton_inverses([gathered_ref[:, at:at + R] + eye(R) for at in starts], [za_ref, zb_ref])
    tile = gathered_ref[:, 2 * R:BOTH_B]
    tile_parts = split(tile)
    core = eye(R) + gathered_ref[:, BOTH_B + 2 * R:]
    right = tile.T[3:4, :]
    kept = []
    for at, inverse, lane in zip(starts, inverses, (2, 1)):
        coupling = gathered_ref[:, at + R:at + 2 * R]
        inverse_parts, turned = split(inverse), split(coupling.T)
        h = dot3(inverse_parts, split(coupling))
        tile_h = dot3(inverse_parts, tile_parts)
        core = core - dot3(turned, split(h))
        right = right - dot3(turned, split(tile_h)).T[lane:lane + 1, :]
        kept.append((h, tile_h))
    z = row_dot(right, split(newton_inverse(core, za_ref)))
    h_all = (h1_ref[...], h2_ref[...], kept[0][0])
    tiles = (h1_ref[:, 3 * R:], h2_ref[:, 2 * R:], kept[0][1])
    rows = [part.T[i:i + 1, :] for i, part in enumerate(tiles)] + [z]
    total = jnp.zeros((16, M), F32)
    for level in reversed(range(LEVELS)):
        z = packed_rows(rows[level])
        total = total + dot(z, basis_ref[level])
        for i in range(level):
            at = (level - i - 1) * R
            parts = split(h_all[i][:, at:at + R])
            drop = dot(z, parts[0], NT) + dot(z, parts[1], NT)
            rows[i] = rows[i] - ((drop[0:1] + drop[1:2]) + drop[2:3])
    spread = (total[0:1] + total[1:2]) + total[2:3]
    out_ref[...] = row_dot(rows_ref[1:2] - rows_ref[0:1] * spread, split3(inverse_ref[...]))


def last_call(gathered, h1, h2, inverse, rows, bases):
    return pl.pallas_call(
        last_kernel,
        out_shape=jax.ShapeDtypeStruct((1, M), F32),
        in_specs=vmem(6),
        out_specs=vmem(1)[0],
        scratch_shapes=[pltpu.VMEM((2 * R, R), F32)] * 2,
        compiler_params=PARAMS,
        name="last",
    )(gathered, h1, h2, inverse, bases, rows)


def place():
    at = lax.axis_index("leaf")
    return at // PLANE, at // 8 % 4, at // 2 % 4, at % 2


def device(plane, x, y, core):
    return ((plane * 4 + x) * 4 + y) * 2 + core


def own_tile():
    plane, x, y, core = place()
    return core * 16 + x * 4 + y


def along(axis, k):
    plane, x, y, core = place()
    if axis == 0:
        to = (x + k) % 4
        return device(plane, to, y, core), to
    to = (y + k) % 4
    return device(plane, x, to, core), to


def partner():
    plane, x, y, core = place()
    return device(plane, x, y, 1 - core)


def greet(others):
    barrier = pltpu.get_barrier_semaphore()
    for other in others:
        pl.semaphore_signal(barrier, inc=1, device_id=(other,), device_id_type=pl.DeviceIdType.MESH)


def meet(others):
    pl.semaphore_wait(pltpu.get_barrier_semaphore(), len(others))


def plane_mates():
    return [partner()] + [along(axis, k)[0] for axis in (0, 1) for k in (1, 2, 3)]


def send(source, target, sems, index, to):
    copy = pltpu.make_async_remote_copy(
        src_ref=source,
        dst_ref=target,
        send_sem=sems[0].at[index],
        recv_sem=sems[1].at[index],
        device_id=(to,),
        device_id_type=pl.DeviceIdType.MESH,
    )
    copy.start()
    return copy


class Gather:
    def __init__(self, own_ref, gathered_ref, sems):
        width = gathered_ref.shape[-1]
        half = width // 2 // LANES * LANES
        self.own, self.out, self.sems = own_ref, gathered_ref, sems
        self.halves = ((0, slice(0, half)), (1, slice(half, width)))
        self.width, self.index, self.fence = width, 0, []
        self.first, self.second = [], ({}, {})

    def send(self, source, target, to):
        self.index += 1
        return send(source, target, self.sems, self.index - 1, to)

    def share(self, block):
        self.fence.append(self.send(block, block, partner()))

    def tile(self, axis, back):
        plane, x, y, core = place()
        at = along(axis, 4 - back)[1]
        return (core, at, y) if axis == 0 else (core, x, at)

    def start(self):
        plane, x, y, core = place()
        for half, (axis, cols) in enumerate(self.halves):
            block = self.own.at[:, cols]
            target = self.out.at[core, x, y, :, cols]
            self.first.append({k: self.send(block, target, along(axis, k)[0]) for k in (2, 1, 3)})
            self.second[half][0] = {k: self.send(block, target, along(1 - axis, k)[0]) for k in (2, 1, 3)}
        whole = slice(0, self.width)
        self.fence.append(self.send(self.own.at[:, whole], self.out.at[core, x, y], partner()))
        self.out[core, x, y] = self.own[:, whole]

    def turn(self):
        for back in (1, 3, 2):
            for half, (axis, cols) in enumerate(self.halves):
                self.first[half][back].wait_recv()
                core, at_x, at_y = self.tile(axis, back)
                block = self.out.at[core, at_x, at_y, :, cols]
                self.second[half][back] = {k: self.send(block, block, along(1 - axis, k)[0]) for k in (2, 1, 3)}
                self.share(block)

    def finish(self):
        plane, x, y, core = place()
        for k in (1, 3, 2):
            for half, (axis, cols) in enumerate(self.halves):
                for back in (0, 1, 3, 2):
                    self.second[half][back][k].wait_recv()
                if axis == 0:
                    self.share(self.out.at[core, :, along(1, 4 - k)[1], :, cols])
                else:
                    self.share(self.out.at[core, along(0, 4 - k)[1], :, :, cols])

    def close(self):
        for half in range(2):
            for copies in [self.first[half], *self.second[half].values()]:
                for copy in copies.values():
                    copy.wait_send()
        for copy in self.fence:
            copy.wait()


class Scatter:
    def __init__(self, mine, got, a, b, got_a, got_b, a2, b2, got_a2, got_b2, sems):
        self.mine, self.got, self.a, self.b, self.got_a, self.got_b = mine, got, a, b, got_a, got_b
        self.a2, self.b2, self.got_a2, self.got_b2, self.sems = a2, b2, got_a2, got_b2, sems
        split_at = a.shape[-1]
        self.cols = (slice(0, split_at), slice(split_at, mine.shape[-1]))
        self.all = []

    def spread(self, source, target, axis, index):
        copies = []
        for k in (2, 1, 3):
            to, at = along(axis, k)
            copies.append(send(source.at[at], target.at[k - 1], self.sems, index + k - 1, to))
        self.all += copies
        return copies

    def swap(self, theirs):
        self.swaps = [
            send(theirs.at[:, :, :, c], self.got.at[:, :, :, c], self.sems, i, partner()) for i, c in enumerate(self.cols)
        ]
        self.all += self.swaps

    def first(self):
        self.swaps[0].wait_recv()
        self.a[...] = self.mine[:, :, :, self.cols[0]] + self.got[:, :, :, self.cols[0]]
        self.first_a = self.spread(self.a, self.got_a, 0, 2)
        self.swaps[1].wait_recv()
        for i in range(4):
            self.b[:, i] = self.mine[i, :, :, self.cols[1]] + self.got[i, :, :, self.cols[1]]
        self.first_b = self.spread(self.b, self.got_b, 1, 5)

    def second(self):
        plane, x, y, core = place()
        for copy in self.first_a:
            copy.wait_recv()
        self.a2[...] = (self.a[x] + self.got_a[0]) + (self.got_a[1] + self.got_a[2])
        self.second_a = self.spread(self.a2, self.got_a2, 1, 8)
        for copy in self.first_b:
            copy.wait_recv()
        self.b2[...] = (self.b[y] + self.got_b[0]) + (self.got_b[1] + self.got_b[2])
        self.second_b = self.spread(self.b2, self.got_b2, 0, 11)

    def finish(self, own_ref, offset):
        plane, x, y, core = place()
        cut, end = offset + self.cols[0].stop, offset + self.cols[1].stop
        for copy in self.second_a:
            copy.wait_recv()
        own_ref[:, offset:cut] = (self.a2[y] + self.got_a2[0]) + (self.got_a2[1] + self.got_a2[2])
        for copy in self.second_b:
            copy.wait_recv()
        own_ref[:, cut:end] = (self.b2[x] + self.got_b2[0]) + (self.got_b2[1] + self.got_b2[2])

    def close(self):
        for copy in self.all:
            copy.wait_send()


GATHER_COPIES = 43
HEAD = LEVELS * R + LANES
TAIL = FRONT - HEAD
HEAD_CUT = 5 * LANES
TAIL_CUT = 6 * LANES
TILES = (4, 4, 8)


def scatter_scratch(width, cut):
    rest = width - cut
    shapes = [
        TILES + (width,), TILES + (width,), TILES + (width,), TILES + (cut,), TILES + (rest,), (3, 4, 8, cut),
        (3, 4, 8, rest), (4, 8, cut), (4, 8, rest), (3, 8, cut), (3, 8, rest),
    ]
    return [pltpu.VMEM(shape, F32) for shape in shapes] + [pltpu.SemaphoreType.DMA((14,))] * 2


def sum_kernel(mh_ref, ml_ref, rows_ref, basis_ref, own_ref, gathered_ref, tile_ref, *scratch):
    plane, x, y, core = place()
    mates = plane_mates()
    greet(mates)

    def grams(half, level, target, offset):
        basis = basis_ref[level, pl.ds(pl.multiple_of(half * LANES, LANES), LANES), :]
        part = split(dot(basis, mh_ref[...]) + dot(basis, ml_ref[...]))
        for other in range(level, LEVELS):
            block = dot(part[0], basis_ref[other], NT) + dot(part[1], basis_ref[other], NT)
            target[:, :, :, offset:offset + R] = block.reshape(TILES + (R,))
            offset += R
        if level == 0:
            tile = tile_ref[pl.ds(pl.multiple_of(half * LANES, LANES), LANES), :]
            target[:, :, :, offset:offset + LANES] = tile.reshape(TILES + (LANES,))

    def tail(half, target):
        grams(half, 1, target, 0)
        grams(half, 2, target, 3 * R)
        grams(half, 3, target, 5 * R)

    theirs0, mine0, theirs1, mine1 = scratch[0], scratch[1], scratch[13], scratch[14]
    head_sum = Scatter(*scratch[1:11], scratch[11:13])
    tail_sum = Scatter(*scratch[14:24], scratch[24:26])
    gather = Gather(own_ref, gathered_ref, scratch[26:28])
    weighted = [jnp.broadcast_to(part.astype(F32), (LANES, M)).astype(BF16) for part in split3(rows_ref[2:3])]
    bases = basis_ref[...].reshape(LEVELS * R, M)
    projections = dot(bases, weighted[0], NT) + (dot(bases, weighted[1], NT) + dot(bases, weighted[2], NT))
    lane = lax.broadcasted_iota(jnp.int32, (R, LANES), 1)
    tile = jnp.zeros((R, LANES), F32)
    for level in range(LEVELS):
        tile = jnp.where(lane == level, projections[level * R:(level + 1) * R], tile)
    tile_ref[...] = tile
    grams(1 - core, 0, theirs0, 0)
    meet(mates)
    head_sum.swap(theirs0)
    grams(core, 0, mine0, 0)
    head_sum.first()
    tail(1 - core, theirs1)
    tail_sum.swap(theirs1)
    tail(core, mine1)
    head_sum.second()
    tail_sum.first()
    head_sum.finish(own_ref, 0)
    gather.start()
    gather.turn()
    tail_sum.second()
    gather.finish()
    tail_sum.finish(own_ref, HEAD)
    gather.close()
    head_sum.close()
    tail_sum.close()


def sum_call(mh, ml, rows, bases):
    return pl.pallas_call(
        sum_kernel,
        out_shape=(
            jax.ShapeDtypeStruct((8, FRONT), F32),
            jax.ShapeDtypeStruct((2,) + TILES + (HEAD,), F32),
        ),
        in_specs=vmem(4),
        out_specs=tuple(vmem(2)),
        scratch_shapes=[pltpu.VMEM((R, LANES), F32)]
        + scatter_scratch(HEAD, HEAD_CUT)
        + scatter_scratch(TAIL, TAIL_CUT)
        + [pltpu.SemaphoreType.DMA((GATHER_COPIES,))] * 2,
        compiler_params=pltpu.CompilerParams(
            vmem_limit_bytes=20 * 1024 * 1024, collective_id=0, has_side_effects=True
        ),
        name="sum_gather",
    )(mh, ml, rows, bases)


def pair_kernel(inverse_ref, before_ref, had_ref, own_ref, gathered_ref, h_ref, part_ref, got_ref,
                send_sem, recv_sem, gather_send, gather_recv):
    plane, x, y, core = place()
    mates = plane_mates() + [device(plane + 1 - 2 * (plane % 2), x, y, core)]
    greet(mates)
    eliminate(LEVELS, inverse_ref, before_ref, had_ref, part_ref, h_ref)
    meet(mates)
    swap = send(part_ref, got_ref, (send_sem, recv_sem), 0, mates[-1])
    swap.wait_recv()
    own_ref[...] = part_ref[...] + got_ref[...]
    gather = Gather(own_ref, gathered_ref, (gather_send, gather_recv))
    gather.start()
    gather.turn()
    gather.finish()
    gather.close()
    swap.wait_send()


def pair_call(inverse, gathered, own):
    left = LEVELS - 1
    width = left * R + LANES
    slab = (8, own_width(left))
    return pl.pallas_call(
        pair_kernel,
        out_shape=(
            jax.ShapeDtypeStruct(slab, F32),
            jax.ShapeDtypeStruct((2,) + TILES + (width,), F32),
            jax.ShapeDtypeStruct((R, width), F32),
        ),
        in_specs=vmem(3),
        out_specs=tuple(vmem(3)),
        scratch_shapes=[
            pltpu.VMEM(slab, F32),
            pltpu.VMEM(slab, F32),
            pltpu.SemaphoreType.DMA((1,)),
            pltpu.SemaphoreType.DMA((1,)),
            pltpu.SemaphoreType.DMA((GATHER_COPIES,)),
            pltpu.SemaphoreType.DMA((GATHER_COPIES,)),
        ],
        compiler_params=pltpu.CompilerParams(
            vmem_limit_bytes=20 * 1024 * 1024, collective_id=1, has_side_effects=True
        ),
        name="pair_gather",
    )(inverse, gathered, own)


def node_kernel(inverse_ref, before_ref, had_ref, gathered_ref, h_ref, part_ref, got_ref, both_ref,
                send_sem, recv_sem, gather_send, gather_recv):
    plane, x, y, core = place()
    odd = plane // 2 % 2
    planes = (plane + 2 - 4 * odd, (plane + 6 + 4 * odd) % 8, (plane + 5 - 2 * (plane % 2)) % 8)
    others = [device(other, x, y, core) for other in planes]
    mates = plane_mates() + others
    greet(mates)
    eliminate(LEVELS - 1, inverse_ref, before_ref, had_ref, part_ref, h_ref)
    meet(mates)
    swaps = [send(part_ref, got_ref.at[i], (send_sem, recv_sem), i, others[i]) for i in (2, 0, 1)]
    for swap in swaps:
        swap.wait_recv()
    mine = part_ref[...] + got_ref[0]
    other = got_ref[1] + got_ref[2]
    lane = lax.broadcasted_iota(jnp.int32, (8, LANES), 1)
    tile, other_tile = mine[:, 2 * R:BOTH_B], other[:, 2 * R:BOTH_B]
    tile = jnp.where(lane == 1, other_tile[:, 2:3], jnp.where(lane == 3, tile + other_tile, tile))
    both_ref[:, 0:2 * R] = mine[:, 0:2 * R]
    both_ref[:, 2 * R:BOTH_B] = tile
    both_ref[:, BOTH_B:BOTH_B + 2 * R] = other[:, 0:2 * R]
    both_ref[:, BOTH_B + 2 * R:] = mine[:, BOTH_B:] + other[:, BOTH_B:]
    gather = Gather(both_ref, gathered_ref, (gather_send, gather_recv))
    gather.start()
    gather.turn()
    gather.finish()
    gather.close()
    for swap in swaps:
        swap.wait_send()


def node_call(inverse, gathered, own):
    return pl.pallas_call(
        node_kernel,
        out_shape=(
            jax.ShapeDtypeStruct((2,) + TILES + (BOTH,), F32),
            jax.ShapeDtypeStruct((R, 2 * R + LANES), F32),
        ),
        in_specs=vmem(3),
        out_specs=tuple(vmem(2)),
        scratch_shapes=[
            pltpu.VMEM((8, NODE), F32),
            pltpu.VMEM((3, 8, NODE), F32),
            pltpu.VMEM((8, BOTH), F32),
            pltpu.SemaphoreType.DMA((3,)),
            pltpu.SemaphoreType.DMA((3,)),
            pltpu.SemaphoreType.DMA((GATHER_COPIES,)),
            pltpu.SemaphoreType.DMA((GATHER_COPIES,)),
        ],
        compiler_params=pltpu.CompilerParams(
            vmem_limit_bytes=20 * 1024 * 1024, collective_id=2, has_side_effects=True
        ),
        name="node_gather",
    )(inverse, gathered, own)


def local(coords, latent, labels, site_order, level_bases):
    sites = jnp.concatenate(
        [coords, latent.reshape(1, M), labels.reshape(1, M).astype(F32), site_order.astype(F32)], axis=0
    )
    mh, ml, inverse, rows = leaf_call(sites)
    own, gathered = sum_call(mh, ml, rows, level_bases)
    gathered = gathered.reshape(R, HEAD)
    own, after, h1 = pair_call(inverse_call(gathered), gathered, own)
    gathered = after.reshape(R, 3 * R + LANES)
    both, h2 = node_call(inverse_call(gathered), gathered, own)
    return last_call(both.reshape(R, BOTH), h1, h2, inverse, rows, level_bases).reshape(M)


def solution(mesh):
    placed = (P(None, "leaf"), P("leaf"), P("leaf"), P("leaf", None), P(None, None, "leaf"))
    return jax.shard_map(local, mesh=mesh, in_specs=placed, out_specs=P("leaf"), check_vma=False)
```

```python
import functools
import math

import jax
import jax.numpy as jnp
from jax import lax
from jax.experimental import pallas as pl
from jax.experimental.pallas import tpu as pltpu
from jax.sharding import PartitionSpec as P

F32 = jnp.float32
BF16 = jnp.bfloat16
HIGHEST = lax.Precision.HIGHEST
LENGTH_SCALE = 0.25
VARIANCE = 16.0
ROOT_FIVE = math.sqrt(5.0)
M = 512
R = 256
LEVELS = 4
LANES = 128
PLANE = 32
NN = (((1,), (0,)), ((), ()))
NT = (((1,), (1,)), ((), ()))


def dot(a, b, dims=NN):
    return lax.dot_general(a, b, dims, preferred_element_type=F32)


def dot_f32(a, b, dims=NN):
    return lax.dot_general(a, b, dims, precision=HIGHEST, preferred_element_type=F32)


def split(x):
    hi = x.astype(BF16)
    return hi, (x - hi.astype(F32)).astype(BF16)


def split3(x):
    hi = x.astype(BF16)
    rest = x - hi.astype(F32)
    mid = rest.astype(BF16)
    return hi, mid, (rest - mid.astype(F32)).astype(BF16)


def dot3(a, b, dims=NN):
    return dot(a[0], b[0], dims) + (dot(a[0], b[1], dims) + dot(a[1], b[0], dims))


def packed_rows(v):
    row = lax.broadcasted_iota(jnp.int32, (16, v.shape[1]), 0)
    out = jnp.zeros((16, v.shape[1]), F32)
    for i, part in enumerate(split3(v)):
        out = jnp.where(row == i, part.astype(F32), out)
    return out.astype(BF16)


def row_dot(v, parts, dims=NN):
    rows = packed_rows(v)
    total = dot(rows, parts[0], dims)
    for part in parts[1:]:
        total = total + dot(rows, part, dims)
    return (total[0:1] + total[1:2]) + total[2:3]


def eye(n):
    return jnp.where(
        lax.broadcasted_iota(jnp.int32, (n, n), 0) == lax.broadcasted_iota(jnp.int32, (n, n), 1), 1.0, 0.0
    ).astype(F32)


def newton_polish(s, z):
    residual = eye(s.shape[0]) - dot_f32(s, z)
    return z + dot3(split(z), split(residual))


def newton_rough(matrices, refs):
    n = matrices[0].shape[0]
    sums = [jnp.sum(jnp.abs(s), axis=0, keepdims=True) for s in matrices]
    bound = jnp.max(functools.reduce(jnp.maximum, sums))
    alpha = 2.0 / (1.0 + bound)
    gap = (bound - 1.0) / (bound + 1.0)
    scale = 2.0 / (2.0 - gap * gap)
    for s, ref in zip(matrices, refs):
        first = eye(n) - alpha * s
        parts = split(first)
        ref[0:n] = (alpha * scale) * (eye(n) + first)
        ref[n:] = (1.0 - scale) * eye(n) + scale * dot3(parts, parts)

    def body(gap):
        scale = 2.0 / (2.0 - gap * gap)
        for ref in refs:
            hi, lo = split(ref[...])
            product = dot3((hi, lo), (hi[n:], lo[n:]))
            ref[0:n] = scale * (ref[0:n] + product[0:n])
            ref[n:] = (1.0 - scale) * eye(n) + scale * product[n:]
        return gap * gap / (2.0 - gap * gap)

    lax.while_loop(lambda gap: gap > 2e-3, body, gap * gap / (2.0 - gap * gap))

    def polish(step, carry):
        for s, ref in zip(matrices, refs):
            ref[0:n] = newton_polish(s, ref[0:n])
        return carry

    extra = jnp.where(bound < 256.0, 0, jnp.where(bound < 8192.0, 1, 2))
    lax.fori_loop(0, extra, polish, 0)


def newton_inverses(matrices, refs):
    newton_rough(matrices, refs)
    return [newton_polish(s, ref[0:s.shape[0]]) for s, ref in zip(matrices, refs)]


def newton_inverse(s, ref):
    return newton_inverses([s], [ref])[0]


def leaf_kernel(sites_ref, marks_ref, mh_ref, ml_ref, inverse_ref, rows_ref, a_ref, z_ref):
    picked = lax.broadcasted_iota(jnp.int32, (M, M), 0) == marks_ref[1:2]
    one_hot = jnp.where(picked, 1.0, 0.0).astype(BF16)
    hi, mid, lo = split3(sites_ref[3:4])
    row = lax.broadcasted_iota(jnp.int32, (16, M), 0)
    packed = jnp.where(row == 0, hi.astype(F32), 0.0)
    packed = jnp.where(row == 1, mid.astype(F32), packed)
    packed = jnp.where(row == 2, lo.astype(F32), packed)
    packed = jnp.where(row == 3, marks_ref[0:1].astype(F32), packed)
    got = dot(packed.astype(BF16), one_hot)
    tree_latent = (got[0:1] + got[1:2]) + got[2:3]
    tree_target = got[3:4]
    probability = 1.0 / (1.0 + jnp.exp(-tree_latent))
    weight = probability * (1.0 - probability)
    root_weight = jnp.sqrt(weight)
    right_side = root_weight * (weight * tree_latent + tree_target - probability)

    def column(value, i):
        return jnp.broadcast_to(value[:, i * LANES:(i + 1) * LANES], (LANES, LANES)).T

    axes = [sites_ref[k:k + 1, :] for k in range(3)]
    columns = []
    for i in range(4):
        cols = [column(axis, i) for axis in axes]
        weight_col = column(root_weight, i)
        columns.append(weight_col)
        for j in range(i, 4):
            span = slice(j * LANES, (j + 1) * LANES)
            total = None
            for axis, col in zip(axes, cols):
                difference = col - axis[:, span]
                total = difference * difference if total is None else total + difference * difference
            scaled = (ROOT_FIVE / LENGTH_SCALE) * jnp.sqrt(total)
            kernel = VARIANCE * (1.0 + scaled + scaled * scaled / 3.0) * jnp.exp(-scaled)
            block = weight_col * kernel * root_weight[:, span]
            if i == j:
                block = block + eye(LANES)
            a_ref[i * LANES:(i + 1) * LANES, span] = block
            if i != j:
                a_ref[span, i * LANES:(i + 1) * LANES] = block.T

    top, bottom = slice(0, R), slice(R, M)
    x = newton_inverse(a_ref[top, top], z_ref)
    u = dot_f32(x, a_ref[top, bottom])
    v = dot_f32(a_ref[bottom, top], x)
    schur = newton_inverse(a_ref[bottom, bottom] - dot_f32(v, a_ref[top, bottom]), z_ref)
    schur_parts, v_parts = split(schur), split(v)
    us = dot3(split(u), schur_parts)
    inverse_ref[bottom, bottom] = schur
    inverse_ref[top, bottom] = -us
    inverse_ref[bottom, top] = -dot3(schur_parts, v_parts)
    inverse_ref[top, top] = x + dot3(split(us), v_parts)

    for i in range(4):
        for j in range(4):
            rows, span = slice(i * LANES, (i + 1) * LANES), slice(j * LANES, (j + 1) * LANES)
            hi, lo = split(columns[i] * inverse_ref[rows, span] * root_weight[:, span])
            mh_ref[rows, span] = hi
            ml_ref[rows, span] = lo
    solved = row_dot(right_side, split3(inverse_ref[...]))
    row = lax.broadcasted_iota(jnp.int32, (8, M), 0)
    rows_ref[...] = jnp.where(row == 0, root_weight, jnp.where(row == 1, right_side, root_weight * solved))


def vmem(n):
    return [pl.BlockSpec(memory_space=pltpu.VMEM)] * n


FRONT = LEVELS * R + LANES + 6 * R
PARAMS = pltpu.CompilerParams(vmem_limit_bytes=20 * 1024 * 1024)


def leaf_call(sites, marks):
    return pl.pallas_call(
        leaf_kernel,
        out_shape=(
            jax.ShapeDtypeStruct((M, M), BF16),
            jax.ShapeDtypeStruct((M, M), BF16),
            jax.ShapeDtypeStruct((M, M), F32),
            jax.ShapeDtypeStruct((8, M), F32),
        ),
        in_specs=vmem(2),
        out_specs=tuple(vmem(4)),
        scratch_shapes=[pltpu.VMEM((M, M), F32), pltpu.VMEM((2 * R, R), F32)],
        compiler_params=PARAMS,
        cost_estimate=pl.CostEstimate(flops=8_000_000_000, bytes_accessed=3_000_000, transcendentals=1_000_000),
        name="leaf",
    )(sites, marks)


def inverse_kernel(gathered_ref, inverse_ref, z_ref):
    newton_rough([gathered_ref[...] + eye(R)], [z_ref])
    inverse_ref[...] = z_ref[0:R]


def inverse_call(gathered):
    return pl.pallas_call(
        inverse_kernel,
        grid=(1,),
        out_shape=jax.ShapeDtypeStruct((R, R), F32),
        in_specs=[pl.BlockSpec((R, R), lambda i: (0, 0))],
        out_specs=pl.BlockSpec((R, R), lambda i: (0, 0)),
        scratch_shapes=[pltpu.VMEM((2 * R, R), F32)],
        compiler_params=PARAMS,
        name="inverse",
    )(gathered)


def eliminate(left, inverse_ref, gathered_ref, own_ref, next_ref, h_ref):
    inverse = newton_polish(gathered_ref[:, 0:R] + eye(R), inverse_ref[...])
    h = dot3(split(inverse), split(gathered_ref[:, R:left * R + LANES]))
    h_ref[...] = h
    width = (left - 1) * R
    h_parts = split(h)
    mine = own_tile() * 8
    wanted = lax.broadcasted_iota(jnp.int32, (8, R), 1) == lax.broadcasted_iota(jnp.int32, (8, R), 0) + mine
    one_hot = jnp.where(wanted, 1.0, 0.0).astype(BF16)
    lane = lax.broadcasted_iota(jnp.int32, (8, LANES), 1)
    tile = own_ref[:, left * R:left * R + LANES]
    source, target = left * R + LANES, 0
    for k in range(1, left):
        block = split(gathered_ref[:, k * R:(k + 1) * R])
        rows = dot(one_hot, block[0], NT) + dot(one_hot, block[1], NT)
        drop = dot3(split(rows), h_parts)
        span = (left - k) * R
        next_ref[:, target:target + span] = own_ref[:, source:source + span] - drop[:, (k - 1) * R:width]
        source, target = source + span, target + span
        if k == 1:
            target += LANES
        at = LEVELS - left
        tile = tile - jnp.where(lane == at + k, drop[:, width + at:width + at + 1], 0.0)
    next_ref[:, width:width + LANES] = tile


def own_width(left):
    return LANES + R * (left * (left + 1) // 2)


NODE = own_width(2)
BOTH_B = 2 * R + LANES
BOTH = 5 * R + LANES


def last_kernel(gathered_ref, h1_ref, h2_ref, inverse_ref, basis_ref, rows_ref, out_ref, za_ref, zb_ref):
    starts = (0, BOTH_B)
    inverses = newton_inverses([gathered_ref[:, at:at + R] + eye(R) for at in starts], [za_ref, zb_ref])
    tile = gathered_ref[:, 2 * R:BOTH_B]
    tile_parts = split(tile)
    core = eye(R) + gathered_ref[:, BOTH_B + 2 * R:]
    right = tile.T[3:4, :]
    kept = []
    for at, inverse, lane in zip(starts, inverses, (2, 1)):
        coupling = gathered_ref[:, at + R:at + 2 * R]
        inverse_parts, turned = split(inverse), split(coupling.T)
        h = dot3(inverse_parts, split(coupling))
        tile_h = dot3(inverse_parts, tile_parts)
        core = core - dot3(turned, split(h))
        right = right - dot3(turned, split(tile_h)).T[lane:lane + 1, :]
        kept.append((h, tile_h))
    z = row_dot(right, split(newton_inverse(core, za_ref)))
    h_all = (h1_ref[...], h2_ref[...], kept[0][0])
    tiles = (h1_ref[:, 3 * R:], h2_ref[:, 2 * R:], kept[0][1])
    rows = [part.T[i:i + 1, :] for i, part in enumerate(tiles)] + [z]
    total = jnp.zeros((16, M), F32)
    for level in reversed(range(LEVELS)):
        z = packed_rows(rows[level])
        total = total + dot(z, basis_ref[level])
        for i in range(level):
            at = (level - i - 1) * R
            parts = split(h_all[i][:, at:at + R])
            drop = dot(z, parts[0], NT) + dot(z, parts[1], NT)
            rows[i] = rows[i] - ((drop[0:1] + drop[1:2]) + drop[2:3])
    spread = (total[0:1] + total[1:2]) + total[2:3]
    out_ref[...] = row_dot(rows_ref[1:2] - rows_ref[0:1] * spread, split(inverse_ref[...]))


def last_call(gathered, h1, h2, inverse, rows, bases):
    return pl.pallas_call(
        last_kernel,
        out_shape=jax.ShapeDtypeStruct((1, M), F32),
        in_specs=vmem(6),
        out_specs=vmem(1)[0],
        scratch_shapes=[pltpu.VMEM((2 * R, R), F32)] * 2,
        compiler_params=PARAMS,
        name="last",
    )(gathered, h1, h2, inverse, bases, rows)


def place():
    at = lax.axis_index("leaf")
    return at // PLANE, at // 8 % 4, at // 2 % 4, at % 2


def device(plane, x, y, core):
    return ((plane * 4 + x) * 4 + y) * 2 + core


def own_tile():
    plane, x, y, core = place()
    return core * 16 + x * 4 + y


def along(axis, k):
    plane, x, y, core = place()
    if axis == 0:
        to = (x + k) % 4
        return device(plane, to, y, core), to
    to = (y + k) % 4
    return device(plane, x, to, core), to


def partner():
    plane, x, y, core = place()
    return device(plane, x, y, 1 - core)


def greet(others):
    barrier = pltpu.get_barrier_semaphore()
    for other in others:
        pl.semaphore_signal(barrier, inc=1, device_id=(other,), device_id_type=pl.DeviceIdType.MESH)


def meet(others):
    pl.semaphore_wait(pltpu.get_barrier_semaphore(), len(others))


def plane_mates():
    return [partner()] + [along(axis, k)[0] for axis in (0, 1) for k in (1, 2, 3)]


def send(source, target, sems, index, to):
    copy = pltpu.make_async_remote_copy(
        src_ref=source,
        dst_ref=target,
        send_sem=sems[0].at[index],
        recv_sem=sems[1].at[index],
        device_id=(to,),
        device_id_type=pl.DeviceIdType.MESH,
    )
    copy.start()
    return copy


class Gather:
    def __init__(self, own_ref, gathered_ref, sems):
        width = gathered_ref.shape[-1]
        half = width // 2 // LANES * LANES
        self.own, self.out, self.sems = own_ref, gathered_ref, sems
        self.halves = ((0, slice(0, half)), (1, slice(half, width)))
        self.width, self.index, self.fence = width, 0, []
        self.first, self.second = [], ({}, {})

    def send(self, source, target, to):
        self.index += 1
        return send(source, target, self.sems, self.index - 1, to)

    def share(self, block):
        self.fence.append(self.send(block, block, partner()))

    def tile(self, axis, back):
        plane, x, y, core = place()
        at = along(axis, 4 - back)[1]
        return (core, at, y) if axis == 0 else (core, x, at)

    def start(self):
        plane, x, y, core = place()
        for half, (axis, cols) in enumerate(self.halves):
            block = self.own.at[:, cols]
            target = self.out.at[core, x, y, :, cols]
            self.first.append({k: self.send(block, target, along(axis, k)[0]) for k in (2, 1, 3)})
            self.second[half][0] = {k: self.send(block, target, along(1 - axis, k)[0]) for k in (2, 1, 3)}
        whole = slice(0, self.width)
        self.fence.append(self.send(self.own.at[:, whole], self.out.at[core, x, y], partner()))
        self.out[core, x, y] = self.own[:, whole]

    def turn(self):
        for back in (1, 3, 2):
            for half, (axis, cols) in enumerate(self.halves):
                self.first[half][back].wait_recv()
                core, at_x, at_y = self.tile(axis, back)
                block = self.out.at[core, at_x, at_y, :, cols]
                self.second[half][back] = {k: self.send(block, block, along(1 - axis, k)[0]) for k in (2, 1, 3)}
                self.share(block)

    def finish(self):
        plane, x, y, core = place()
        for k in (1, 3, 2):
            for half, (axis, cols) in enumerate(self.halves):
                for back in (0, 1, 3, 2):
                    self.second[half][back][k].wait_recv()
                if axis == 0:
                    self.share(self.out.at[core, :, along(1, 4 - k)[1], :, cols])
                else:
                    self.share(self.out.at[core, along(0, 4 - k)[1], :, :, cols])

    def close(self):
        for half in range(2):
            for copies in [self.first[half], *self.second[half].values()]:
                for copy in copies.values():
                    copy.wait_send()
        for copy in self.fence:
            copy.wait()


class Scatter:
    def __init__(self, mine, got, a, b, got_a, got_b, a2, b2, got_a2, got_b2, sems):
        self.mine, self.got, self.a, self.b, self.got_a, self.got_b = mine, got, a, b, got_a, got_b
        self.a2, self.b2, self.got_a2, self.got_b2, self.sems = a2, b2, got_a2, got_b2, sems
        split_at = a.shape[-1]
        self.cols = (slice(0, split_at), slice(split_at, mine.shape[-1]))
        self.all = []

    def spread(self, source, target, axis, index):
        copies = []
        for k in (2, 1, 3):
            to, at = along(axis, k)
            copies.append(send(source.at[at], target.at[k - 1], self.sems, index + k - 1, to))
        self.all += copies
        return copies

    def swap(self, theirs):
        self.swaps = [
            send(theirs.at[:, :, :, c], self.got.at[:, :, :, c], self.sems, i, partner()) for i, c in enumerate(self.cols)
        ]
        self.all += self.swaps

    def first(self):
        self.swaps[0].wait_recv()
        self.a[...] = self.mine[:, :, :, self.cols[0]] + self.got[:, :, :, self.cols[0]]
        self.first_a = self.spread(self.a, self.got_a, 0, 2)
        self.swaps[1].wait_recv()
        for i in range(4):
            self.b[:, i] = self.mine[i, :, :, self.cols[1]] + self.got[i, :, :, self.cols[1]]
        self.first_b = self.spread(self.b, self.got_b, 1, 5)

    def second(self):
        plane, x, y, core = place()
        for copy in self.first_a:
            copy.wait_recv()
        self.a2[...] = (self.a[x] + self.got_a[0]) + (self.got_a[1] + self.got_a[2])
        self.second_a = self.spread(self.a2, self.got_a2, 1, 8)
        for copy in self.first_b:
            copy.wait_recv()
        self.b2[...] = (self.b[y] + self.got_b[0]) + (self.got_b[1] + self.got_b[2])
        self.second_b = self.spread(self.b2, self.got_b2, 0, 11)

    def finish(self, own_ref, offset):
        plane, x, y, core = place()
        cut, end = offset + self.cols[0].stop, offset + self.cols[1].stop
        for copy in self.second_a:
            copy.wait_recv()
        own_ref[:, offset:cut] = (self.a2[y] + self.got_a2[0]) + (self.got_a2[1] + self.got_a2[2])
        for copy in self.second_b:
            copy.wait_recv()
        own_ref[:, cut:end] = (self.b2[x] + self.got_b2[0]) + (self.got_b2[1] + self.got_b2[2])

    def close(self):
        for copy in self.all:
            copy.wait_send()


GATHER_COPIES = 43
HEAD = LEVELS * R + LANES
TAIL = FRONT - HEAD
HEAD_CUT = 5 * LANES
TAIL_CUT = 6 * LANES
TILES = (4, 4, 8)


def scatter_scratch(width, cut):
    rest = width - cut
    shapes = [
        TILES + (width,), TILES + (width,), TILES + (width,), TILES + (cut,), TILES + (rest,), (3, 4, 8, cut),
        (3, 4, 8, rest), (4, 8, cut), (4, 8, rest), (3, 8, cut), (3, 8, rest),
    ]
    return [pltpu.VMEM(shape, F32) for shape in shapes] + [pltpu.SemaphoreType.DMA((14,))] * 2


def sum_kernel(mh_ref, ml_ref, rows_ref, basis_ref, own_ref, gathered_ref, tile_ref, *scratch):
    plane, x, y, core = place()
    mates = plane_mates()
    greet(mates)

    def grams(half, level, target, offset):
        basis = basis_ref[level, pl.ds(pl.multiple_of(half * LANES, LANES), LANES), :]
        part = split(dot(basis, mh_ref[...]) + dot(basis, ml_ref[...]))
        for other in range(level, LEVELS):
            block = dot(part[0], basis_ref[other], NT) + dot(part[1], basis_ref[other], NT)
            target[:, :, :, offset:offset + R] = block.reshape(TILES + (R,))
            offset += R
        if level == 0:
            tile = tile_ref[pl.ds(pl.multiple_of(half * LANES, LANES), LANES), :]
            target[:, :, :, offset:offset + LANES] = tile.reshape(TILES + (LANES,))

    def tail(half, target):
        grams(half, 1, target, 0)
        grams(half, 2, target, 3 * R)
        grams(half, 3, target, 5 * R)

    theirs0, mine0, theirs1, mine1 = scratch[0], scratch[1], scratch[13], scratch[14]
    head_sum = Scatter(*scratch[1:11], scratch[11:13])
    tail_sum = Scatter(*scratch[14:24], scratch[24:26])
    gather = Gather(own_ref, gathered_ref, scratch[26:28])
    weighted = [jnp.broadcast_to(part.astype(F32), (LANES, M)).astype(BF16) for part in split3(rows_ref[2:3])]
    bases = basis_ref[...].reshape(LEVELS * R, M)
    projections = dot(bases, weighted[0], NT) + (dot(bases, weighted[1], NT) + dot(bases, weighted[2], NT))
    lane = lax.broadcasted_iota(jnp.int32, (R, LANES), 1)
    tile = jnp.zeros((R, LANES), F32)
    for level in range(LEVELS):
        tile = jnp.where(lane == level, projections[level * R:(level + 1) * R], tile)
    tile_ref[...] = tile
    grams(1 - core, 0, theirs0, 0)
    meet(mates)
    head_sum.swap(theirs0)
    grams(core, 0, mine0, 0)
    head_sum.first()
    tail(1 - core, theirs1)
    tail_sum.swap(theirs1)
    tail(core, mine1)
    head_sum.second()
    tail_sum.first()
    head_sum.finish(own_ref, 0)
    gather.start()
    gather.turn()
    tail_sum.second()
    gather.finish()
    tail_sum.finish(own_ref, HEAD)
    gather.close()
    head_sum.close()
    tail_sum.close()


def sum_call(mh, ml, rows, bases):
    return pl.pallas_call(
        sum_kernel,
        out_shape=(
            jax.ShapeDtypeStruct((8, FRONT), F32),
            jax.ShapeDtypeStruct((2,) + TILES + (HEAD,), F32),
        ),
        in_specs=vmem(4),
        out_specs=tuple(vmem(2)),
        scratch_shapes=[pltpu.VMEM((R, LANES), F32)]
        + scatter_scratch(HEAD, HEAD_CUT)
        + scatter_scratch(TAIL, TAIL_CUT)
        + [pltpu.SemaphoreType.DMA((GATHER_COPIES,))] * 2,
        compiler_params=pltpu.CompilerParams(
            vmem_limit_bytes=20 * 1024 * 1024, collective_id=0, has_side_effects=True
        ),
        name="sum_gather",
    )(mh, ml, rows, bases)


def pair_kernel(inverse_ref, before_ref, had_ref, own_ref, gathered_ref, h_ref, part_ref, got_ref,
                send_sem, recv_sem, gather_send, gather_recv):
    plane, x, y, core = place()
    mates = plane_mates() + [device(plane + 1 - 2 * (plane % 2), x, y, core)]
    greet(mates)
    eliminate(LEVELS, inverse_ref, before_ref, had_ref, part_ref, h_ref)
    meet(mates)
    cut = gathered_ref.shape[-1]
    pieces = (slice(0, cut), slice(cut, part_ref.shape[-1]))
    swaps = [
        send(part_ref.at[:, cols], got_ref.at[:, cols], (send_sem, recv_sem), i, mates[-1]) for i, cols in enumerate(pieces)
    ]
    swaps[0].wait_recv()
    own_ref[:, 0:cut] = part_ref[:, 0:cut] + got_ref[:, 0:cut]
    gather = Gather(own_ref, gathered_ref, (gather_send, gather_recv))
    gather.start()
    gather.turn()
    swaps[1].wait_recv()
    own_ref[:, cut:] = part_ref[:, cut:] + got_ref[:, cut:]
    gather.finish()
    gather.close()
    for swap in swaps:
        swap.wait_send()


def pair_call(inverse, gathered, own):
    left = LEVELS - 1
    width = left * R + LANES
    slab = (8, own_width(left))
    return pl.pallas_call(
        pair_kernel,
        out_shape=(
            jax.ShapeDtypeStruct(slab, F32),
            jax.ShapeDtypeStruct((2,) + TILES + (width,), F32),
            jax.ShapeDtypeStruct((R, width), F32),
        ),
        in_specs=vmem(3),
        out_specs=tuple(vmem(3)),
        scratch_shapes=[
            pltpu.VMEM(slab, F32),
            pltpu.VMEM(slab, F32),
            pltpu.SemaphoreType.DMA((2,)),
            pltpu.SemaphoreType.DMA((2,)),
            pltpu.SemaphoreType.DMA((GATHER_COPIES,)),
            pltpu.SemaphoreType.DMA((GATHER_COPIES,)),
        ],
        compiler_params=pltpu.CompilerParams(
            vmem_limit_bytes=20 * 1024 * 1024, collective_id=1, has_side_effects=True
        ),
        name="pair_gather",
    )(inverse, gathered, own)


def node_kernel(inverse_ref, before_ref, had_ref, gathered_ref, h_ref, part_ref, got_ref, both_ref,
                send_sem, recv_sem, gather_send, gather_recv):
    plane, x, y, core = place()
    odd = plane // 2 % 2
    planes = (plane + 2 - 4 * odd, (plane + 6 + 4 * odd) % 8, (plane + 5 - 2 * (plane % 2)) % 8)
    others = [device(other, x, y, core) for other in planes]
    mates = plane_mates() + others
    greet(mates)
    eliminate(LEVELS - 1, inverse_ref, before_ref, had_ref, part_ref, h_ref)
    meet(mates)
    swaps = [send(part_ref, got_ref.at[i], (send_sem, recv_sem), i, others[i]) for i in (2, 0, 1)]
    for swap in swaps:
        swap.wait_recv()
    mine = part_ref[...] + got_ref[0]
    other = got_ref[1] + got_ref[2]
    lane = lax.broadcasted_iota(jnp.int32, (8, LANES), 1)
    tile, other_tile = mine[:, 2 * R:BOTH_B], other[:, 2 * R:BOTH_B]
    tile = jnp.where(lane == 1, other_tile[:, 2:3], jnp.where(lane == 3, tile + other_tile, tile))
    both_ref[:, 0:2 * R] = mine[:, 0:2 * R]
    both_ref[:, 2 * R:BOTH_B] = tile
    both_ref[:, BOTH_B:BOTH_B + 2 * R] = other[:, 0:2 * R]
    both_ref[:, BOTH_B + 2 * R:] = mine[:, BOTH_B:] + other[:, BOTH_B:]
    gather = Gather(both_ref, gathered_ref, (gather_send, gather_recv))
    gather.start()
    gather.turn()
    gather.finish()
    gather.close()
    for swap in swaps:
        swap.wait_send()


def node_call(inverse, gathered, own):
    return pl.pallas_call(
        node_kernel,
        out_shape=(
            jax.ShapeDtypeStruct((2,) + TILES + (BOTH,), F32),
            jax.ShapeDtypeStruct((R, 2 * R + LANES), F32),
        ),
        in_specs=vmem(3),
        out_specs=tuple(vmem(2)),
        scratch_shapes=[
            pltpu.VMEM((8, NODE), F32),
            pltpu.VMEM((3, 8, NODE), F32),
            pltpu.VMEM((8, BOTH), F32),
            pltpu.SemaphoreType.DMA((3,)),
            pltpu.SemaphoreType.DMA((3,)),
            pltpu.SemaphoreType.DMA((GATHER_COPIES,)),
            pltpu.SemaphoreType.DMA((GATHER_COPIES,)),
        ],
        compiler_params=pltpu.CompilerParams(
            vmem_limit_bytes=20 * 1024 * 1024, collective_id=2, has_side_effects=True
        ),
        name="node_gather",
    )(inverse, gathered, own)


def local(coords, latent, labels, site_order, level_bases):
    sites = jnp.concatenate([coords, latent.reshape(1, M)], axis=0)
    marks = jnp.concatenate([labels.reshape(1, M), site_order], axis=0)
    mh, ml, inverse, rows = leaf_call(sites, marks)
    own, gathered = sum_call(mh, ml, rows, level_bases)
    gathered = gathered.reshape(R, HEAD)
    own, after, h1 = pair_call(inverse_call(gathered), gathered, own)
    gathered = after.reshape(R, 3 * R + LANES)
    both, h2 = node_call(inverse_call(gathered), gathered, own)
    return last_call(both.reshape(R, BOTH), h1, h2, inverse, rows, level_bases).reshape(M)


def solution(mesh):
    placed = (P(None, "leaf"), P("leaf"), P("leaf"), P("leaf", None), P(None, None, "leaf"))
    return jax.shard_map(local, mesh=mesh, in_specs=placed, out_specs=P("leaf"), check_vma=False)
```

```python
import functools
import math

import jax
import jax.numpy as jnp
from jax import lax
from jax.experimental import pallas as pl
from jax.experimental.pallas import tpu as pltpu
from jax.sharding import PartitionSpec as P

F32 = jnp.float32
BF16 = jnp.bfloat16
HIGHEST = lax.Precision.HIGHEST
LENGTH_SCALE = 0.25
VARIANCE = 16.0
ROOT_FIVE = math.sqrt(5.0)
M = 512
R = 256
LEVELS = 4
LANES = 128
PLANE = 32
NN = (((1,), (0,)), ((), ()))
NT = (((1,), (1,)), ((), ()))


def dot(a, b, dims=NN):
    return lax.dot_general(a, b, dims, preferred_element_type=F32)


def dot_f32(a, b, dims=NN):
    return lax.dot_general(a, b, dims, precision=HIGHEST, preferred_element_type=F32)


def split(x):
    hi = x.astype(BF16)
    return hi, (x - hi.astype(F32)).astype(BF16)


def split3(x):
    hi = x.astype(BF16)
    rest = x - hi.astype(F32)
    mid = rest.astype(BF16)
    return hi, mid, (rest - mid.astype(F32)).astype(BF16)


def dot3(a, b, dims=NN):
    return dot(a[0], b[0], dims) + (dot(a[0], b[1], dims) + dot(a[1], b[0], dims))


def packed_rows(v):
    row = lax.broadcasted_iota(jnp.int32, (16, v.shape[1]), 0)
    out = jnp.zeros((16, v.shape[1]), F32)
    for i, part in enumerate(split3(v)):
        out = jnp.where(row == i, part.astype(F32), out)
    return out.astype(BF16)


def row_dot(v, parts, dims=NN):
    rows = packed_rows(v)
    total = dot(rows, parts[0], dims)
    for part in parts[1:]:
        total = total + dot(rows, part, dims)
    return (total[0:1] + total[1:2]) + total[2:3]


def eye(n):
    return jnp.where(
        lax.broadcasted_iota(jnp.int32, (n, n), 0) == lax.broadcasted_iota(jnp.int32, (n, n), 1), 1.0, 0.0
    ).astype(F32)


def newton_polish(s, z):
    residual = eye(s.shape[0]) - dot_f32(s, z)
    return z + dot3(split(z), split(residual))


def newton_rough(matrices, refs):
    n = matrices[0].shape[0]
    sums = [jnp.sum(jnp.abs(s), axis=0, keepdims=True) for s in matrices]
    bound = jnp.max(functools.reduce(jnp.maximum, sums))
    alpha = 2.0 / (1.0 + bound)
    gap = (bound - 1.0) / (bound + 1.0)
    scale = 2.0 / (2.0 - gap * gap)
    for s, ref in zip(matrices, refs):
        first = eye(n) - alpha * s
        parts = split(first)
        ref[0:n] = (alpha * scale) * (eye(n) + first)
        ref[n:] = (1.0 - scale) * eye(n) + scale * dot3(parts, parts)

    def body(gap):
        scale = 2.0 / (2.0 - gap * gap)
        for ref in refs:
            hi, lo = split(ref[...])
            product = dot3((hi, lo), (hi[n:], lo[n:]))
            ref[0:n] = scale * (ref[0:n] + product[0:n])
            ref[n:] = (1.0 - scale) * eye(n) + scale * product[n:]
        return gap * gap / (2.0 - gap * gap)

    lax.while_loop(lambda gap: gap > 2e-3, body, gap * gap / (2.0 - gap * gap))

    def polish(step, carry):
        for s, ref in zip(matrices, refs):
            ref[0:n] = newton_polish(s, ref[0:n])
        return carry

    extra = jnp.where(bound < 256.0, 0, jnp.where(bound < 8192.0, 1, 2))
    lax.fori_loop(0, extra, polish, 0)


def newton_inverses(matrices, refs):
    newton_rough(matrices, refs)
    return [newton_polish(s, ref[0:s.shape[0]]) for s, ref in zip(matrices, refs)]


def newton_inverse(s, ref):
    return newton_inverses([s], [ref])[0]


def leaf_kernel(sites_ref, marks_ref, mh_ref, ml_ref, inverse_ref, rows_ref, a_ref, z_ref):
    picked = lax.broadcasted_iota(jnp.int32, (M, M), 0) == marks_ref[1:2]
    one_hot = jnp.where(picked, 1.0, 0.0).astype(BF16)
    hi, mid, lo = split3(sites_ref[3:4])
    row = lax.broadcasted_iota(jnp.int32, (16, M), 0)
    packed = jnp.where(row == 0, hi.astype(F32), 0.0)
    packed = jnp.where(row == 1, mid.astype(F32), packed)
    packed = jnp.where(row == 2, lo.astype(F32), packed)
    packed = jnp.where(row == 3, marks_ref[0:1].astype(F32), packed)
    got = dot(packed.astype(BF16), one_hot)
    tree_latent = (got[0:1] + got[1:2]) + got[2:3]
    tree_target = got[3:4]
    probability = 1.0 / (1.0 + jnp.exp(-tree_latent))
    weight = probability * (1.0 - probability)
    root_weight = jnp.sqrt(weight)
    right_side = root_weight * (weight * tree_latent + tree_target - probability)

    def column(value, i):
        return jnp.broadcast_to(value[:, i * LANES:(i + 1) * LANES], (LANES, LANES)).T

    axes = [sites_ref[k:k + 1, :] for k in range(3)]
    columns = []
    for i in range(4):
        cols = [column(axis, i) for axis in axes]
        weight_col = column(root_weight, i)
        columns.append(weight_col)
        for j in range(i, 4):
            span = slice(j * LANES, (j + 1) * LANES)
            total = None
            for axis, col in zip(axes, cols):
                difference = col - axis[:, span]
                total = difference * difference if total is None else total + difference * difference
            scaled = (ROOT_FIVE / LENGTH_SCALE) * jnp.sqrt(total)
            kernel = VARIANCE * (1.0 + scaled + scaled * scaled / 3.0) * jnp.exp(-scaled)
            block = weight_col * kernel * root_weight[:, span]
            if i == j:
                block = block + eye(LANES)
            a_ref[i * LANES:(i + 1) * LANES, span] = block
            if i != j:
                a_ref[span, i * LANES:(i + 1) * LANES] = block.T

    top, bottom = slice(0, R), slice(R, M)
    x = newton_inverse(a_ref[top, top], z_ref)
    u = dot_f32(x, a_ref[top, bottom])
    v = dot_f32(a_ref[bottom, top], x)
    schur = newton_inverse(a_ref[bottom, bottom] - dot_f32(v, a_ref[top, bottom]), z_ref)
    schur_parts, v_parts = split(schur), split(v)
    us = dot3(split(u), schur_parts)
    inverse_ref[bottom, bottom] = schur
    inverse_ref[top, bottom] = -us
    inverse_ref[bottom, top] = -dot3(schur_parts, v_parts)
    inverse_ref[top, top] = x + dot3(split(us), v_parts)

    for i in range(4):
        for j in range(4):
            rows, span = slice(i * LANES, (i + 1) * LANES), slice(j * LANES, (j + 1) * LANES)
            hi, lo = split(columns[i] * inverse_ref[rows, span] * root_weight[:, span])
            mh_ref[rows, span] = hi
            ml_ref[rows, span] = lo
    solved = row_dot(right_side, split3(inverse_ref[...]))
    row = lax.broadcasted_iota(jnp.int32, (8, M), 0)
    rows_ref[...] = jnp.where(row == 0, root_weight, jnp.where(row == 1, right_side, root_weight * solved))


def vmem(n):
    return [pl.BlockSpec(memory_space=pltpu.VMEM)] * n


FRONT = LEVELS * R + LANES + 6 * R
PARAMS = pltpu.CompilerParams(vmem_limit_bytes=20 * 1024 * 1024)


def leaf_call(sites, marks):
    return pl.pallas_call(
        leaf_kernel,
        out_shape=(
            jax.ShapeDtypeStruct((M, M), BF16),
            jax.ShapeDtypeStruct((M, M), BF16),
            jax.ShapeDtypeStruct((M, M), F32),
            jax.ShapeDtypeStruct((8, M), F32),
        ),
        in_specs=vmem(2),
        out_specs=tuple(vmem(4)),
        scratch_shapes=[pltpu.VMEM((M, M), F32), pltpu.VMEM((2 * R, R), F32)],
        compiler_params=PARAMS,
        cost_estimate=pl.CostEstimate(flops=8_000_000_000, bytes_accessed=3_000_000, transcendentals=1_000_000),
        name="leaf",
    )(sites, marks)


def inverse_kernel(gathered_ref, inverse_ref, z_ref):
    newton_rough([gathered_ref[...] + eye(R)], [z_ref])
    inverse_ref[...] = z_ref[0:R]


def inverse_call(gathered):
    return pl.pallas_call(
        inverse_kernel,
        grid=(1,),
        out_shape=jax.ShapeDtypeStruct((R, R), F32),
        in_specs=[pl.BlockSpec((R, R), lambda i: (0, 0))],
        out_specs=pl.BlockSpec((R, R), lambda i: (0, 0)),
        scratch_shapes=[pltpu.VMEM((2 * R, R), F32)],
        compiler_params=PARAMS,
        name="inverse",
    )(gathered)


def eliminate(left, inverse_ref, gathered_ref, own_ref, next_ref, h_ref):
    inverse = newton_polish(gathered_ref[:, 0:R] + eye(R), inverse_ref[...])
    h = dot3(split(inverse), split(gathered_ref[:, R:left * R + LANES]))
    h_ref[...] = h
    width = (left - 1) * R
    h_parts = split(h)
    mine = own_tile() * 8
    wanted = lax.broadcasted_iota(jnp.int32, (8, R), 1) == lax.broadcasted_iota(jnp.int32, (8, R), 0) + mine
    one_hot = jnp.where(wanted, 1.0, 0.0).astype(BF16)
    lane = lax.broadcasted_iota(jnp.int32, (8, LANES), 1)
    tile = own_ref[:, left * R:left * R + LANES]
    source, target = left * R + LANES, 0
    for k in range(1, left):
        block = split(gathered_ref[:, k * R:(k + 1) * R])
        rows = dot(one_hot, block[0], NT) + dot(one_hot, block[1], NT)
        drop = dot3(split(rows), h_parts)
        span = (left - k) * R
        next_ref[:, target:target + span] = own_ref[:, source:source + span] - drop[:, (k - 1) * R:width]
        source, target = source + span, target + span
        if k == 1:
            target += LANES
        at = LEVELS - left
        tile = tile - jnp.where(lane == at + k, drop[:, width + at:width + at + 1], 0.0)
    next_ref[:, width:width + LANES] = tile


def own_width(left):
    return LANES + R * (left * (left + 1) // 2)


NODE = own_width(2)
BOTH_B = 2 * R + LANES
BOTH = 5 * R + LANES


def last_kernel(gathered_ref, h1_ref, h2_ref, inverse_ref, basis_ref, rows_ref, out_ref, za_ref, zb_ref):
    starts = (0, BOTH_B)
    inverses = newton_inverses([gathered_ref[:, at:at + R] + eye(R) for at in starts], [za_ref, zb_ref])
    tile = gathered_ref[:, 2 * R:BOTH_B]
    tile_parts = split(tile)
    core = eye(R) + gathered_ref[:, BOTH_B + 2 * R:]
    right = tile.T[3:4, :]
    kept = []
    for at, inverse, lane in zip(starts, inverses, (2, 1)):
        coupling = gathered_ref[:, at + R:at + 2 * R]
        inverse_parts, turned = split(inverse), split(coupling.T)
        h = dot3(inverse_parts, split(coupling))
        tile_h = dot3(inverse_parts, tile_parts)
        core = core - dot3(turned, split(h))
        right = right - dot3(turned, split(tile_h)).T[lane:lane + 1, :]
        kept.append((h, tile_h))
    z = row_dot(right, split(newton_inverse(core, za_ref)))
    h_all = (h1_ref[...], h2_ref[...], kept[0][0])
    tiles = (h1_ref[:, 3 * R:], h2_ref[:, 2 * R:], kept[0][1])
    rows = [part.T[i:i + 1, :] for i, part in enumerate(tiles)] + [z]
    total = jnp.zeros((16, M), F32)
    for level in reversed(range(LEVELS)):
        z = packed_rows(rows[level])
        total = total + dot(z, basis_ref[level])
        for i in range(level):
            at = (level - i - 1) * R
            parts = split(h_all[i][:, at:at + R])
            drop = dot(z, parts[0], NT) + dot(z, parts[1], NT)
            rows[i] = rows[i] - ((drop[0:1] + drop[1:2]) + drop[2:3])
    spread = (total[0:1] + total[1:2]) + total[2:3]
    out_ref[...] = row_dot(rows_ref[1:2] - rows_ref[0:1] * spread, split(inverse_ref[...]))


def last_call(gathered, h1, h2, inverse, rows, bases):
    return pl.pallas_call(
        last_kernel,
        out_shape=jax.ShapeDtypeStruct((1, M), F32),
        in_specs=vmem(6),
        out_specs=vmem(1)[0],
        scratch_shapes=[pltpu.VMEM((2 * R, R), F32)] * 2,
        compiler_params=PARAMS,
        name="last",
    )(gathered, h1, h2, inverse, bases, rows)


def place():
    at = lax.axis_index("leaf")
    return at // PLANE, at // 8 % 4, at // 2 % 4, at % 2


def device(plane, x, y, core):
    return ((plane * 4 + x) * 4 + y) * 2 + core


def own_tile():
    plane, x, y, core = place()
    return core * 16 + x * 4 + y


def along(axis, k):
    plane, x, y, core = place()
    if axis == 0:
        to = (x + k) % 4
        return device(plane, to, y, core), to
    to = (y + k) % 4
    return device(plane, x, to, core), to


def partner():
    plane, x, y, core = place()
    return device(plane, x, y, 1 - core)


def greet(others):
    barrier = pltpu.get_barrier_semaphore()
    for other in others:
        pl.semaphore_signal(barrier, inc=1, device_id=(other,), device_id_type=pl.DeviceIdType.MESH)


def meet(others):
    pl.semaphore_wait(pltpu.get_barrier_semaphore(), len(others))


def plane_mates():
    return [partner()] + [along(axis, k)[0] for axis in (0, 1) for k in (1, 2, 3)]


def send(source, target, sems, index, to):
    copy = pltpu.make_async_remote_copy(
        src_ref=source,
        dst_ref=target,
        send_sem=sems[0].at[index],
        recv_sem=sems[1].at[index],
        device_id=(to,),
        device_id_type=pl.DeviceIdType.MESH,
    )
    copy.start()
    return copy


class Gather:
    def __init__(self, own_ref, gathered_ref, sems):
        width = gathered_ref.shape[-1]
        half = width // 2 // LANES * LANES
        self.own, self.out, self.sems = own_ref, gathered_ref, sems
        self.halves = ((0, slice(0, half)), (1, slice(half, width)))
        self.width, self.index, self.fence = width, 0, []
        self.first, self.second = [], ({}, {})

    def send(self, source, target, to):
        self.index += 1
        return send(source, target, self.sems, self.index - 1, to)

    def share(self, block):
        self.fence.append(self.send(block, block, partner()))

    def tile(self, axis, back):
        plane, x, y, core = place()
        at = along(axis, 4 - back)[1]
        return (core, at, y) if axis == 0 else (core, x, at)

    def start(self):
        plane, x, y, core = place()
        for half, (axis, cols) in enumerate(self.halves):
            block = self.own.at[:, cols]
            target = self.out.at[core, x, y, :, cols]
            self.first.append({k: self.send(block, target, along(axis, k)[0]) for k in (2, 1, 3)})
            self.second[half][0] = {k: self.send(block, target, along(1 - axis, k)[0]) for k in (2, 1, 3)}
        whole = slice(0, self.width)
        self.fence.append(self.send(self.own.at[:, whole], self.out.at[core, x, y], partner()))
        self.out[core, x, y] = self.own[:, whole]

    def turn(self):
        for back in (1, 3, 2):
            for half, (axis, cols) in enumerate(self.halves):
                self.first[half][back].wait_recv()
                core, at_x, at_y = self.tile(axis, back)
                block = self.out.at[core, at_x, at_y, :, cols]
                self.second[half][back] = {k: self.send(block, block, along(1 - axis, k)[0]) for k in (2, 1, 3)}
                self.share(block)

    def finish(self):
        plane, x, y, core = place()
        for k in (1, 3, 2):
            for half, (axis, cols) in enumerate(self.halves):
                for back in (0, 1, 3, 2):
                    self.second[half][back][k].wait_recv()
                if axis == 0:
                    self.share(self.out.at[core, :, along(1, 4 - k)[1], :, cols])
                else:
                    self.share(self.out.at[core, along(0, 4 - k)[1], :, :, cols])

    def close(self):
        for half in range(2):
            for copies in [self.first[half], *self.second[half].values()]:
                for copy in copies.values():
                    copy.wait_send()
        for copy in self.fence:
            copy.wait()


class Scatter:
    def __init__(self, mine, got, a, b, got_a, got_b, a2, b2, got_a2, got_b2, sems):
        self.mine, self.got, self.a, self.b, self.got_a, self.got_b = mine, got, a, b, got_a, got_b
        self.a2, self.b2, self.got_a2, self.got_b2, self.sems = a2, b2, got_a2, got_b2, sems
        split_at = a.shape[-1]
        self.cols = (slice(0, split_at), slice(split_at, mine.shape[-1]))
        self.all = []

    def spread(self, source, target, axis, index):
        copies = []
        for k in (2, 1, 3):
            to, at = along(axis, k)
            copies.append(send(source.at[at], target.at[k - 1], self.sems, index + k - 1, to))
        self.all += copies
        return copies

    def swap(self, theirs):
        self.swaps = [
            send(theirs.at[:, :, :, c], self.got.at[:, :, :, c], self.sems, i, partner()) for i, c in enumerate(self.cols)
        ]
        self.all += self.swaps

    def first(self):
        self.swaps[0].wait_recv()
        self.a[...] = self.mine[:, :, :, self.cols[0]] + self.got[:, :, :, self.cols[0]]
        self.first_a = self.spread(self.a, self.got_a, 0, 2)
        self.swaps[1].wait_recv()
        for i in range(4):
            self.b[:, i] = self.mine[i, :, :, self.cols[1]] + self.got[i, :, :, self.cols[1]]
        self.first_b = self.spread(self.b, self.got_b, 1, 5)

    def second(self):
        plane, x, y, core = place()
        for copy in self.first_a:
            copy.wait_recv()
        self.a2[...] = (self.a[x] + self.got_a[0]) + (self.got_a[1] + self.got_a[2])
        self.second_a = self.spread(self.a2, self.got_a2, 1, 8)
        for copy in self.first_b:
            copy.wait_recv()
        self.b2[...] = (self.b[y] + self.got_b[0]) + (self.got_b[1] + self.got_b[2])
        self.second_b = self.spread(self.b2, self.got_b2, 0, 11)

    def finish(self, own_ref, offset):
        plane, x, y, core = place()
        cut, end = offset + self.cols[0].stop, offset + self.cols[1].stop
        for copy in self.second_a:
            copy.wait_recv()
        own_ref[:, offset:cut] = (self.a2[y] + self.got_a2[0]) + (self.got_a2[1] + self.got_a2[2])
        for copy in self.second_b:
            copy.wait_recv()
        own_ref[:, cut:end] = (self.b2[x] + self.got_b2[0]) + (self.got_b2[1] + self.got_b2[2])

    def close(self):
        for copy in self.all:
            copy.wait_send()


GATHER_COPIES = 43
HEAD = LEVELS * R + LANES
TAIL = FRONT - HEAD
HEAD_CUT = 5 * LANES
TAIL_CUT = 6 * LANES
TILES = (4, 4, 8)


def scatter_scratch(width, cut):
    rest = width - cut
    shapes = [
        TILES + (width,), TILES + (width,), TILES + (width,), TILES + (cut,), TILES + (rest,), (3, 4, 8, cut),
        (3, 4, 8, rest), (4, 8, cut), (4, 8, rest), (3, 8, cut), (3, 8, rest),
    ]
    return [pltpu.VMEM(shape, F32) for shape in shapes] + [pltpu.SemaphoreType.DMA((14,))] * 2


def sum_kernel(mh_ref, ml_ref, rows_ref, basis_ref, own_ref, gathered_ref, tile_ref, *scratch):
    plane, x, y, core = place()
    mates = plane_mates()
    greet(mates)

    def grams(half, level, target, offset):
        basis = basis_ref[level, pl.ds(pl.multiple_of(half * LANES, LANES), LANES), :]
        part = split(dot(basis, mh_ref[...]) + dot(basis, ml_ref[...]))
        for other in range(level, LEVELS):
            block = dot(part[0], basis_ref[other], NT) + dot(part[1], basis_ref[other], NT)
            target[:, :, :, offset:offset + R] = block.reshape(TILES + (R,))
            offset += R
        if level == 0:
            tile = tile_ref[pl.ds(pl.multiple_of(half * LANES, LANES), LANES), :]
            target[:, :, :, offset:offset + LANES] = tile.reshape(TILES + (LANES,))

    def tail(half, target):
        grams(half, 1, target, 0)
        grams(half, 2, target, 3 * R)
        grams(half, 3, target, 5 * R)

    theirs0, mine0, theirs1, mine1 = scratch[0], scratch[1], scratch[13], scratch[14]
    head_sum = Scatter(*scratch[1:11], scratch[11:13])
    tail_sum = Scatter(*scratch[14:24], scratch[24:26])
    gather = Gather(own_ref, gathered_ref, scratch[26:28])
    weighted = [jnp.broadcast_to(part.astype(F32), (LANES, M)).astype(BF16) for part in split3(rows_ref[2:3])]
    bases = basis_ref[...].reshape(LEVELS * R, M)
    projections = dot(bases, weighted[0], NT) + (dot(bases, weighted[1], NT) + dot(bases, weighted[2], NT))
    lane = lax.broadcasted_iota(jnp.int32, (R, LANES), 1)
    tile = jnp.zeros((R, LANES), F32)
    for level in range(LEVELS):
        tile = jnp.where(lane == level, projections[level * R:(level + 1) * R], tile)
    tile_ref[...] = tile
    grams(1 - core, 0, theirs0, 0)
    meet(mates)
    head_sum.swap(theirs0)
    grams(core, 0, mine0, 0)
    head_sum.first()
    tail(1 - core, theirs1)
    tail_sum.swap(theirs1)
    tail(core, mine1)
    head_sum.second()
    tail_sum.first()
    head_sum.finish(own_ref, 0)
    gather.start()
    tail_sum.second()
    gather.turn()
    gather.finish()
    tail_sum.finish(own_ref, HEAD)
    gather.close()
    head_sum.close()
    tail_sum.close()


def sum_call(mh, ml, rows, bases):
    return pl.pallas_call(
        sum_kernel,
        out_shape=(
            jax.ShapeDtypeStruct((8, FRONT), F32),
            jax.ShapeDtypeStruct((2,) + TILES + (HEAD,), F32),
        ),
        in_specs=vmem(4),
        out_specs=tuple(vmem(2)),
        scratch_shapes=[pltpu.VMEM((R, LANES), F32)]
        + scatter_scratch(HEAD, HEAD_CUT)
        + scatter_scratch(TAIL, TAIL_CUT)
        + [pltpu.SemaphoreType.DMA((GATHER_COPIES,))] * 2,
        compiler_params=pltpu.CompilerParams(
            vmem_limit_bytes=20 * 1024 * 1024, collective_id=0, has_side_effects=True
        ),
        name="sum_gather",
    )(mh, ml, rows, bases)


def pair_kernel(inverse_ref, before_ref, had_ref, own_ref, gathered_ref, h_ref, part_ref, got_ref,
                send_sem, recv_sem, gather_send, gather_recv):
    plane, x, y, core = place()
    mates = plane_mates() + [device(plane + 1 - 2 * (plane % 2), x, y, core)]
    greet(mates)
    eliminate(LEVELS, inverse_ref, before_ref, had_ref, part_ref, h_ref)
    meet(mates)
    cut = gathered_ref.shape[-1]
    pieces = (slice(0, cut), slice(cut, part_ref.shape[-1]))
    swaps = [
        send(part_ref.at[:, cols], got_ref.at[:, cols], (send_sem, recv_sem), i, mates[-1]) for i, cols in enumerate(pieces)
    ]
    swaps[0].wait_recv()
    own_ref[:, 0:cut] = part_ref[:, 0:cut] + got_ref[:, 0:cut]
    gather = Gather(own_ref, gathered_ref, (gather_send, gather_recv))
    gather.start()
    gather.turn()
    swaps[1].wait_recv()
    own_ref[:, cut:] = part_ref[:, cut:] + got_ref[:, cut:]
    gather.finish()
    gather.close()
    for swap in swaps:
        swap.wait_send()


def pair_call(inverse, gathered, own):
    left = LEVELS - 1
    width = left * R + LANES
    slab = (8, own_width(left))
    return pl.pallas_call(
        pair_kernel,
        out_shape=(
            jax.ShapeDtypeStruct(slab, F32),
            jax.ShapeDtypeStruct((2,) + TILES + (width,), F32),
            jax.ShapeDtypeStruct((R, width), F32),
        ),
        in_specs=vmem(3),
        out_specs=tuple(vmem(3)),
        scratch_shapes=[
            pltpu.VMEM(slab, F32),
            pltpu.VMEM(slab, F32),
            pltpu.SemaphoreType.DMA((2,)),
            pltpu.SemaphoreType.DMA((2,)),
            pltpu.SemaphoreType.DMA((GATHER_COPIES,)),
            pltpu.SemaphoreType.DMA((GATHER_COPIES,)),
        ],
        compiler_params=pltpu.CompilerParams(
            vmem_limit_bytes=20 * 1024 * 1024, collective_id=1, has_side_effects=True
        ),
        name="pair_gather",
    )(inverse, gathered, own)


def node_kernel(inverse_ref, before_ref, had_ref, gathered_ref, h_ref, part_ref, got_ref, both_ref,
                send_sem, recv_sem, gather_send, gather_recv):
    plane, x, y, core = place()
    odd = plane // 2 % 2
    planes = (plane + 2 - 4 * odd, (plane + 6 + 4 * odd) % 8, (plane + 5 - 2 * (plane % 2)) % 8)
    others = [device(other, x, y, core) for other in planes]
    mates = plane_mates() + others
    greet(mates)
    eliminate(LEVELS - 1, inverse_ref, before_ref, had_ref, part_ref, h_ref)
    meet(mates)
    swaps = [send(part_ref, got_ref.at[i], (send_sem, recv_sem), i, others[i]) for i in (2, 0, 1)]
    for swap in swaps:
        swap.wait_recv()
    mine = part_ref[...] + got_ref[0]
    other = got_ref[1] + got_ref[2]
    lane = lax.broadcasted_iota(jnp.int32, (8, LANES), 1)
    tile, other_tile = mine[:, 2 * R:BOTH_B], other[:, 2 * R:BOTH_B]
    tile = jnp.where(lane == 1, other_tile[:, 2:3], jnp.where(lane == 3, tile + other_tile, tile))
    both_ref[:, 0:2 * R] = mine[:, 0:2 * R]
    both_ref[:, 2 * R:BOTH_B] = tile
    both_ref[:, BOTH_B:BOTH_B + 2 * R] = other[:, 0:2 * R]
    both_ref[:, BOTH_B + 2 * R:] = mine[:, BOTH_B:] + other[:, BOTH_B:]
    gather = Gather(both_ref, gathered_ref, (gather_send, gather_recv))
    gather.start()
    gather.turn()
    gather.finish()
    gather.close()
    for swap in swaps:
        swap.wait_send()


def node_call(inverse, gathered, own):
    return pl.pallas_call(
        node_kernel,
        out_shape=(
            jax.ShapeDtypeStruct((2,) + TILES + (BOTH,), F32),
            jax.ShapeDtypeStruct((R, 2 * R + LANES), F32),
        ),
        in_specs=vmem(3),
        out_specs=tuple(vmem(2)),
        scratch_shapes=[
            pltpu.VMEM((8, NODE), F32),
            pltpu.VMEM((3, 8, NODE), F32),
            pltpu.VMEM((8, BOTH), F32),
            pltpu.SemaphoreType.DMA((3,)),
            pltpu.SemaphoreType.DMA((3,)),
            pltpu.SemaphoreType.DMA((GATHER_COPIES,)),
            pltpu.SemaphoreType.DMA((GATHER_COPIES,)),
        ],
        compiler_params=pltpu.CompilerParams(
            vmem_limit_bytes=20 * 1024 * 1024, collective_id=2, has_side_effects=True
        ),
        name="node_gather",
    )(inverse, gathered, own)


def local(coords, latent, labels, site_order, level_bases):
    sites = jnp.concatenate([coords, latent.reshape(1, M)], axis=0)
    marks = jnp.concatenate([labels.reshape(1, M), site_order], axis=0)
    mh, ml, inverse, rows = leaf_call(sites, marks)
    own, gathered = sum_call(mh, ml, rows, level_bases)
    gathered = gathered.reshape(R, HEAD)
    own, after, h1 = pair_call(inverse_call(gathered), gathered, own)
    gathered = after.reshape(R, 3 * R + LANES)
    both, h2 = node_call(inverse_call(gathered), gathered, own)
    return last_call(both.reshape(R, BOTH), h1, h2, inverse, rows, level_bases).reshape(M)


def solution(mesh):
    placed = (P(None, "leaf"), P("leaf"), P("leaf"), P("leaf", None), P(None, None, "leaf"))
    return jax.shard_map(local, mesh=mesh, in_specs=placed, out_specs=P("leaf"), check_vma=False)
```
